32 devices in a mesh: ctx: 8 (over z, y), head: 4 (over x, core).
Axes of the slice: x: 2, y: 2, z: 4, core: 2. Of those that a mesh axis runs over, the one named last changes fastest.
Arguments:
- tokens: bfloat16 [4096, 1024], P('ctx'), may hold values from -24 to 24
- w_query: bfloat16 [1024, 1024], P(None, 'head'), may hold values from -0.1875 to 0.1875
- w_key: bfloat16 [1024, 1024], P(None, 'head'), may hold values from -0.1875 to 0.1875
- w_value: bfloat16 [1024, 1024], P(None, 'head'), may hold values from -0.1875 to 0.1875
- w_out: bfloat16 [1024, 1024], P('head'), may hold values from -0.1875 to 0.1875
- block_mask: int32 [32, 32], replicated, may hold values from 0 to 1, as said below
- block_order: int32 [32], replicated, may hold values from 0 to 31, each once
Outputs:
- mixed: bfloat16 [4096, 1024], P('ctx', 'head')
The draws below stay inside these ranges and needn't reach their ends.
Inputs may be any that keep to these rules, and one draw needn't show every extreme that they name: `block_mask`: entries are 0 or 1 and every diagonal entry is 1. `block_order`: each initial block index appears once.
All inputs are finite; a program needn't handle non-finite values.
Results may differ from the reference program's by a relative error of at most 0.013.
Values may be sent and summed in bfloat16 or wider, within the bound.
No kernel may reach another device: no remote copies, remote signals or barrier semaphores. Data moves between devices by JAX's collectives and lax.ppermute only.
A program may use at most 256 MiB of HBM per device.

```python
import jax
import jax.numpy as jnp
from jax import lax

D = 1024
HEADS = 16
HEAD_DIM = 64
BLOCK = 128
TOKENS = 4096
NB = 32


def draw_tokens(key, part):
    key_base = jax.random.fold_in(key, 11)
    result = jnp.clip(jax.random.normal(key_base, (TOKENS, D), jnp.float32), -5.0, 5.0)
    return result.astype(jnp.bfloat16)


def draw_block_mask(key, part):
    key_width = jax.random.fold_in(key, 21)
    key_rates = jax.random.fold_in(key, 22)
    key_entry = jax.random.fold_in(key, 23)
    rows = jnp.arange(NB, dtype=jnp.int32)[:, None]
    cols = jnp.arange(NB, dtype=jnp.int32)[None, :]
    band_width = jax.random.randint(key_width, (NB, 1), 1, 5)
    band = jnp.abs(rows - cols) <= band_width
    row_rates = jnp.left_shift(1, jax.random.randint(key_rates, (NB, 1), 0, 5))
    entry_draw = jax.random.randint(key_entry, (NB, NB), 0, 256)
    cross = entry_draw < row_rates
    return jnp.where(band | cross, 1, 0).astype(jnp.int32)


def levels(rng, shape, shards, smallest, top_value):
    gain = 1.0
    for position, parts in shards:
        steps = jax.random.uniform(jax.random.fold_in(jax.random.fold_in(rng, 6), position), (parts,), jnp.float32, smallest / len(shards), top_value / len(shards))
        gain = gain * jnp.repeat(jnp.exp(steps), shape[position] // parts).reshape((-1,) + (1,) * (len(shape) - 1 - position))
    return gain


def normal_values(own_key, dims, scale, limit, cuts=(), kind=jnp.bfloat16):
    gain = levels(own_key, dims, cuts, -0.22, 0.18) if cuts else 1.0
    drawn = jax.random.normal(own_key, dims, jnp.float32) * scale * gain
    return jnp.minimum(jnp.maximum(drawn, -limit), limit).astype(kind)


def setup_inputs(seed: int = 0) -> dict:
    arg_keys = jax.random.split(jax.random.key(seed), 8)
    tokens = draw_tokens(jax.random.fold_in(arg_keys[7], 71), 0)
    w_query = normal_values(arg_keys[1], (D, D), D ** -0.5, 0.1875, ((1, 4),))
    w_key = normal_values(arg_keys[2], (D, D), D ** -0.5, 0.1875, ((1, 4),))
    w_value = normal_values(arg_keys[3], (D, D), D ** -0.5, 0.1875, ((1, 4),))
    w_out = normal_values(arg_keys[4], (D, D), D ** -0.5, 0.1875, ((0, 4),))
    block_mask = draw_block_mask(jax.random.fold_in(arg_keys[7], 71), 0)
    block_order = jax.random.permutation(arg_keys[6], NB).astype(jnp.int32)
    return {"tokens": tokens, "w_query": w_query, "w_key": w_key, "w_value": w_value, "w_out": w_out, "block_mask": block_mask, "block_order": block_order}


def reference(tokens, w_query, w_key, w_value, w_out, block_mask, block_order):
    query_proj = jnp.dot(tokens, w_query, preferred_element_type=jnp.float32).astype(jnp.bfloat16)
    key_proj = jnp.dot(tokens, w_key, preferred_element_type=jnp.float32).astype(jnp.bfloat16)
    value_proj = jnp.dot(tokens, w_value, preferred_element_type=jnp.float32).astype(jnp.bfloat16)
    query_heads = query_proj.reshape(TOKENS, HEADS, HEAD_DIM)
    key_heads = key_proj.reshape(TOKENS, HEADS, HEAD_DIM).astype(jnp.float32)
    value_heads = value_proj.reshape(TOKENS, HEADS, HEAD_DIM).astype(jnp.float32)
    ordered = jnp.take(jnp.take(block_mask, block_order, axis=0), block_order, axis=1)
    scale = HEAD_DIM ** -0.5

    def one_block(block_index):
        query_rows = lax.dynamic_slice_in_dim(query_heads, (block_index * BLOCK).astype(jnp.int32), BLOCK, 0).astype(jnp.float32)
        mask_row = lax.dynamic_index_in_dim(ordered, block_index.astype(jnp.int32), 0, keepdims=False)
        allowed = (jnp.repeat(mask_row, BLOCK) > 0)[None, None, :]
        scores = jnp.einsum("qhd,khd->hqk", query_rows, key_heads) * scale
        row_max = jnp.max(jnp.where(allowed, scores, -1e30), axis=2)
        probs = jnp.where(allowed, jnp.exp(scores - row_max[:, :, None]), 0.0)
        row_sum = jnp.sum(probs, axis=2)
        weighted = jnp.einsum("hqk,khd->qhd", probs.astype(jnp.bfloat16).astype(jnp.float32), value_heads)
        return (weighted / jnp.transpose(row_sum)[:, :, None]).astype(jnp.bfloat16)

    attended = lax.map(one_block, jnp.arange(NB, dtype=jnp.int32)).reshape(TOKENS, D)
    return jnp.dot(attended, w_out, preferred_element_type=jnp.float32).astype(jnp.bfloat16)
```

```python
import functools

import jax
import jax.numpy as jnp
from jax import lax
from jax.experimental import pallas as pl
from jax.experimental.pallas import tpu as pltpu
from jax.sharding import PartitionSpec as P

HEAD_DIM = 64
BLOCK = 128
LANES = 128
SLOTS = 4
NEG = -1e30


ANY = pl.BlockSpec(memory_space=pl.ANY)
VMEM = pl.BlockSpec(memory_space=pltpu.VMEM)
SMEM = pl.BlockSpec(memory_space=pltpu.SMEM)
BIG = 60 * 1024 * 1024


def low_half(shape):
    return lax.broadcasted_iota(jnp.int32, shape, len(shape) - 1) < HEAD_DIM


def swap_halves(x):
    return pltpu.roll(x, HEAD_DIM, 1)


def send_out(src, a, outs, sems):
    copies = [
        pltpu.make_async_copy(src.at[a ^ j], out, sems.at[j]) for j, out in enumerate(outs)
    ]
    for copy in copies:
        copy.start()
    for copy in copies:
        copy.wait()


def kv_kernel(inner, heads, tok, wk, wv, *rest):
    outs, (kv, sems) = rest[:heads], rest[heads:]
    a = lax.axis_index("ctx") // inner
    t = tok[...]
    k = jnp.dot(t, wk[...], preferred_element_type=jnp.float32)
    v = jnp.dot(t, wv[...], preferred_element_type=jnp.float32)
    low = low_half((k.shape[0], LANES))
    for h in range(heads):
        cols = slice(LANES * (h // 2), LANES * (h // 2) + LANES)
        kk, vv = k[:, cols], v[:, cols]
        if h % 2 == 0:
            vv = swap_halves(vv)
        else:
            kk = swap_halves(kk)
        kv[h] = jnp.where(low, kk, vv).astype(jnp.bfloat16)
    send_out(kv, a, outs, sems)


def q_kernel(inner, heads, tok, wq, *rest):
    outs, (qs, sems) = rest[:heads], rest[heads:]
    a = lax.axis_index("ctx") // inner
    q = jnp.dot(tok[...], wq[...], preferred_element_type=jnp.float32) * HEAD_DIM ** (-0.5)
    half = q.shape[0] // 2
    low = low_half((half, LANES))
    for h in range(heads):
        cols = slice(LANES * (h // 2), LANES * (h // 2) + LANES)
        top, bottom = q[:half, cols], q[half:, cols]
        if h % 2 == 0:
            bottom = swap_halves(bottom)
        else:
            top = swap_halves(top)
        qs[h] = jnp.where(low, top, bottom).astype(jnp.bfloat16)
    send_out(qs, a, outs, sems)


def list_kernel(inner, outer, per, mask, order, lists, counts, names):
    c = lax.axis_index("ctx")
    a, b = c // inner, c % inner
    blocks = inner * outer * per

    def name(slot, _):
        dev = slot // per
        kb = (((dev // inner) ^ a) * inner + ((dev % inner) ^ b)) * per + slot % per
        names[slot] = order[kb]
        return 0

    lax.fori_loop(0, blocks, name, 0)

    def row(qi, _):
        qb = (((qi // per) ^ a) * inner + b) * per + qi % per
        own = order[qb]

        def col(slot, count):
            lists[qi, count] = slot
            return count + mask[own, names[slot]]

        count = lax.fori_loop(0, blocks, col, 0, unroll=4)
        counts[qi] = count
        for extra in range(SLOTS):
            lists[qi, count + extra] = 0
        return 0

    lax.fori_loop(0, outer * per, row, 0)


def attend_kernel(inner, outer, per, lists, counts, *rest):
    n_kv = inner * outer
    kv_in, rest = rest[:n_kv], rest[n_kv:]
    q_in, rest = rest[:outer], rest[outer:]
    outs, rest = rest[:outer], rest[outer:]
    kv, qs, os, m_s, l_s, acc_s, sems = rest
    copies = [
        pltpu.make_async_copy(src, kv.at[pl.ds(n * per, per)], sems.at[n])
        for n, src in enumerate(kv_in)
    ] + [
        pltpu.make_async_copy(src, qs.at[n], sems.at[n_kv + n]) for n, src in enumerate(q_in)
    ]
    for copy in copies:
        copy.start()
    for copy in copies:
        copy.wait()
    half = per // 2
    low = low_half((BLOCK, LANES))

    def piece(k, _):
        qps = []
        for i in range(per):
            r = i % half
            q = qs[k, r * BLOCK : (r + 1) * BLOCK, :].astype(jnp.float32)
            if i >= half:
                q = swap_halves(q)
            qps.append(jnp.where(low, q, 0.0).astype(jnp.bfloat16))
        m_s[...] = jnp.full(m_s.shape, NEG, jnp.float32)
        l_s[...] = jnp.zeros(l_s.shape, jnp.float32)
        acc_s[...] = jnp.zeros(acc_s.shape, jnp.float32)
        most = counts[k * per]
        for i in range(1, per):
            most = jnp.maximum(most, counts[k * per + i])

        def step(t, _):
            for i in range(per):
                qi = k * per + i
                tiles, keys = [], []
                for s in range(0, SLOTS, 2):
                    pair = jnp.concatenate(
                        [kv[lists[qi, jnp.minimum(t * SLOTS + s + e, counts[qi])]] for e in (0, 1)],
                        axis=0,
                    )
                    keys.append(pair)
                    sc = lax.dot_general(
                        qps[i], pair, (((1,), (1,)), ((), ())), preferred_element_type=jnp.float32
                    )
                    for e in (0, 1):
                        bias = jnp.where(t * SLOTS + s + e < counts[qi], 0.0, NEG)
                        tiles.append(sc[:, e * BLOCK : (e + 1) * BLOCK] + bias)
                top = functools.reduce(jnp.maximum, tiles)
                m_old = m_s[i]
                m_new = jnp.maximum(m_old, jnp.max(top, axis=1, keepdims=True))
                alpha = jnp.exp(m_old - m_new)
                probs = [jnp.exp(tile - m_new) for tile in tiles]
                l_s[i] = l_s[i] * alpha + functools.reduce(jnp.add, probs)
                acc = acc_s[i] * alpha
                for n, pair in enumerate(keys):
                    pp = jnp.concatenate(
                        [probs[2 * n].astype(jnp.bfloat16), probs[2 * n + 1].astype(jnp.bfloat16)],
                        axis=1,
                    )
                    acc = acc + jnp.dot(pp, pair, preferred_element_type=jnp.float32)
                acc_s[i] = acc
                m_s[i] = m_new
            return 0

        lax.fori_loop(0, (most + SLOTS - 1) // SLOTS, step, 0)
        done = [acc_s[i] * (1.0 / jnp.sum(l_s[i], axis=1, keepdims=True)) for i in range(per)]
        for r in range(half):
            os[k, r * BLOCK : (r + 1) * BLOCK, :] = jnp.where(
                low, swap_halves(done[r]), done[r + half]
            ).astype(jnp.bfloat16)
        return 0

    lax.fori_loop(0, outer, piece, 0)
    backs = [pltpu.make_async_copy(os.at[n], out, sems.at[n]) for n, out in enumerate(outs)]
    for copy in backs:
        copy.start()
    for copy in backs:
        copy.wait()


def out_kernel(inner, heads, groups, *refs):
    pieces = [refs[g * heads : (g + 1) * heads] for g in range(groups)]
    ws = refs[groups * heads : groups * heads + groups]
    out = refs[-1]
    a = lax.axis_index("ctx") // inner
    half = pieces[0][0].shape[0]
    low = low_half((half, LANES))
    tops, bottoms, rows = [], [], []
    for g in range(groups):
        for k in range(0, heads, 2):
            p0 = pieces[g][k][...].astype(jnp.float32)
            p1 = pieces[g][k + 1][...].astype(jnp.float32)
            tops.append(jnp.where(low, p0, swap_halves(p1)).astype(jnp.bfloat16))
            bottoms.append(jnp.where(low, swap_halves(p0), p1).astype(jnp.bfloat16))
            for e in (0, 1):
                start = pl.multiple_of(HEAD_DIM * (a ^ (k + e)), HEAD_DIM)
                rows.append(ws[g][pl.ds(start, HEAD_DIM), :])
    w = jnp.concatenate(rows, axis=0)
    for n, parts in enumerate((tops, bottoms)):
        x = jnp.concatenate(parts, axis=1)
        out[n * half : (n + 1) * half, :] = jnp.dot(
            x, w, preferred_element_type=jnp.float32
        ).astype(out.dtype)


def solution(mesh):
    ctx, groups = mesh.shape["ctx"], mesh.shape["head"]

    def body(tokens, w_query, w_key, w_value, w_out, block_mask, block_order):
        rows = tokens.shape[0]
        heads = w_query.shape[1] // HEAD_DIM
        inner = ctx // heads
        per = rows // BLOCK
        nb = block_mask.shape[0]
        cols = w_out.shape[1] // groups
        bf = jnp.bfloat16
        params = pltpu.CompilerParams(vmem_limit_bytes=BIG)

        def outer_swap(x, j):
            return lax.ppermute(x, "ctx", [(c, ((c // inner) ^ j) * inner + c % inner) for c in range(ctx)]) if j else x

        def inner_swap(x, j):
            return lax.ppermute(x, "ctx", [(c, c ^ j) for c in range(ctx)]) if j else x

        def head_swap(x, j):
            return lax.ppermute(x, "head", [(h, h ^ j) for h in range(groups)]) if j else x

        kv = pl.pallas_call(
            functools.partial(kv_kernel, inner, heads),
            out_shape=[jax.ShapeDtypeStruct((rows, LANES), bf)] * heads,
            in_specs=[VMEM] * 3,
            out_specs=[ANY] * heads,
            scratch_shapes=[
                pltpu.VMEM((heads, rows, LANES), bf),
                pltpu.SemaphoreType.DMA((heads,)),
            ],
            compiler_params=params,
            name="kv_proj",
        )(tokens, w_key, w_value)
        kv_got = [outer_swap(kv[j], j) for j in range(heads)]
        qp = pl.pallas_call(
            functools.partial(q_kernel, inner, heads),
            out_shape=[jax.ShapeDtypeStruct((rows // 2, LANES), bf)] * heads,
            in_specs=[VMEM] * 2,
            out_specs=[ANY] * heads,
            scratch_shapes=[
                pltpu.VMEM((heads, rows // 2, LANES), bf),
                pltpu.SemaphoreType.DMA((heads,)),
            ],
            compiler_params=params,
            name="q_proj",
        )(tokens, w_query)
        q_got = [outer_swap(qp[j], j) for j in range(heads)]
        kv_all = [inner_swap(kv_got[j], i) for j in range(heads) for i in range(inner)]
        lists, counts = pl.pallas_call(
            functools.partial(list_kernel, inner, heads, per),
            out_shape=[
                jax.ShapeDtypeStruct((heads * per, nb + SLOTS), jnp.int32),
                jax.ShapeDtypeStruct((heads * per,), jnp.int32),
            ],
            in_specs=[SMEM] * 2,
            out_specs=[SMEM] * 2,
            scratch_shapes=[pltpu.SMEM((nb,), jnp.int32)],
            name="block_lists",
        )(block_mask, block_order)
        h = lax.axis_index("head")
        w_cols = [
            head_swap(lax.dynamic_slice_in_dim(w_out, (h ^ j) * cols, cols, axis=1), j)
            for j in range(groups)
        ]
        kv_all = [x.reshape(per, BLOCK, LANES) for x in kv_all]
        o = pl.pallas_call(
            functools.partial(attend_kernel, inner, heads, per),
            out_shape=[jax.ShapeDtypeStruct((rows // 2, LANES), bf)] * heads,
            in_specs=[SMEM] * 2 + [ANY] * (heads * inner + heads),
            out_specs=[ANY] * heads,
            scratch_shapes=[
                pltpu.VMEM((nb, BLOCK, LANES), bf),
                pltpu.VMEM((heads, rows // 2, LANES), bf),
                pltpu.VMEM((heads, rows // 2, LANES), bf),
                pltpu.VMEM((per, BLOCK, 1), jnp.float32),
                pltpu.VMEM((per, BLOCK, LANES), jnp.float32),
                pltpu.VMEM((per, BLOCK, LANES), jnp.float32),
                pltpu.SemaphoreType.DMA((heads * inner + heads,)),
            ],
            compiler_params=params,
            name="attend",
        )(lists, counts, *kv_all, *q_got)
        mine = [outer_swap(o[j], j) for j in range(heads)]
        parts = [mine]
        for j in range(1, groups):
            if j % 2:
                parts.append([head_swap(x, 1) for x in parts[j - 1]])
            else:
                parts.append([head_swap(x, j) for x in mine])
        return pl.pallas_call(
            functools.partial(out_kernel, inner, heads, groups),
            out_shape=jax.ShapeDtypeStruct((rows, cols), bf),
            in_specs=[VMEM] * (groups * heads + groups),
            out_specs=VMEM,
            compiler_params=params,
            name="out_proj",
        )(*[x for part in parts for x in part], *w_cols)

    placed = (
        P("ctx", None),
        P(None, "head"),
        P(None, "head"),
        P(None, "head"),
        P("head", None),
        P(),
        P(),
    )
    return jax.shard_map(
        body, mesh=mesh, in_specs=placed, out_specs=P("ctx", "head"), check_vma=False
    )
```

```python
import functools

import jax
import jax.numpy as jnp
from jax import lax
from jax.experimental import pallas as pl
from jax.experimental.pallas import tpu as pltpu
from jax.sharding import PartitionSpec as P

HEAD_DIM = 64
BLOCK = 128
LANES = 128
SLOTS = 4
STREAMS = 4
NEG = -1e30


ANY = pl.BlockSpec(memory_space=pl.ANY)
VMEM = pl.BlockSpec(memory_space=pltpu.VMEM)
SMEM = pl.BlockSpec(memory_space=pltpu.SMEM)
BIG = 60 * 1024 * 1024


def low_half(shape):
    return lax.broadcasted_iota(jnp.int32, shape, len(shape) - 1) < HEAD_DIM


def swap_halves(x):
    return pltpu.roll(x, HEAD_DIM, 1)


def proj_kernel(inner, heads, tok, wq, wk, wv, *rest):
    outs, (msg, sems) = rest[:heads], rest[heads:]
    a = lax.axis_index("ctx") // inner
    t = tok[...]
    rows = t.shape[0]
    half = rows // 2
    k = jnp.dot(t, wk[...], preferred_element_type=jnp.float32)
    v = jnp.dot(t, wv[...], preferred_element_type=jnp.float32)
    q = jnp.dot(t, wq[...], preferred_element_type=jnp.float32) * HEAD_DIM ** (-0.5)
    low = low_half((rows, LANES))
    for h in range(heads):
        cols = slice(LANES * (h // 2), LANES * (h // 2) + LANES)
        kk, vv, top, bottom = k[:, cols], v[:, cols], q[:half, cols], q[half:, cols]
        if h % 2 == 0:
            vv, bottom = swap_halves(vv), swap_halves(bottom)
        else:
            kk, top = swap_halves(kk), swap_halves(top)
        msg[h, :rows] = jnp.where(low, kk, vv).astype(jnp.bfloat16)
        msg[h, rows:] = jnp.where(low[:half], top, bottom).astype(jnp.bfloat16)
    copies = [
        pltpu.make_async_copy(msg.at[a ^ j], out, sems.at[j]) for j, out in enumerate(outs)
    ]
    for copy in copies:
        copy.start()
    for copy in copies:
        copy.wait()


def list_kernel(inner, outer, per, cap, mask, order, who, which, valid, first, steps, names, load):
    c = lax.axis_index("ctx")
    a = c // inner
    b = (c % inner) // 2 * 2 + lax.axis_index("head") % 2
    blocks = inner * outer * per

    def name(slot, _):
        dev = slot // per
        kb = (((dev // inner) ^ a) * inner + ((dev % inner) ^ b)) * per + slot % per
        names[slot] = order[kb]
        return 0

    lax.fori_loop(0, blocks, name, 0)
    for s in range(STREAMS):
        load[s] = 0

    def row(qi, _):
        qb = (((qi // per) ^ a) * inner + b) * per + qi % per
        own = order[qb]
        s, least = 0, load[0]
        for other in range(1, STREAMS):
            better = load[other] < least
            s = jnp.where(better, other, s)
            least = jnp.minimum(load[other], least)
        base = least * SLOTS

        def col(slot, count):
            which[s, base + count] = slot
            return count + mask[own, names[slot]]

        count = lax.fori_loop(0, blocks, col, 0, unroll=4)
        keep = which[s, base]
        for extra in range(SLOTS):
            which[s, base + count + extra] = keep
        items = (count + SLOTS - 1) // SLOTS

        def item(t, _):
            who[s, least + t] = qi
            valid[s, least + t] = count - t * SLOTS
            first[s, least + t] = jnp.where(t == 0, 1, 0)
            return 0

        lax.fori_loop(0, items, item, 0)
        load[s] = least + items
        return 0

    lax.fori_loop(0, outer * per, row, 0)
    most = load[0]
    for s in range(1, STREAMS):
        most = jnp.maximum(most, load[s])
    steps[0] = most
    for s in range(STREAMS):
        last = jnp.maximum(load[s] - 1, 0)
        idle = load[s] == 0
        qi = jnp.where(idle, outer * per, who[s, last])
        key = jnp.where(idle, 0, which[s, last * SLOTS])

        def fill(t, _):
            who[s, t] = qi
            valid[s, t] = 0
            first[s, t] = 0
            for e in range(SLOTS):
                which[s, t * SLOTS + e] = key
            return 0

        lax.fori_loop(load[s], most + 1, fill, 0)


def attend_kernel(inner, outer, per, who, which, valid, first, steps, *rest):
    n_in = inner * outer
    ins, rest = rest[:n_in], rest[n_in:]
    outs, rest = rest[:outer], rest[outer:]
    msgs, vt, qt, sc, m_s, al_s, l_s, acc_s, os, sems = rest
    copies = [pltpu.make_async_copy(src, msgs.at[n], sems.at[n]) for n, src in enumerate(ins)]
    for copy in copies:
        copy.start()
    half = per // 2
    nq = outer * per
    zero = jnp.zeros((HEAD_DIM, BLOCK), jnp.bfloat16)
    for n, copy in enumerate(copies):
        copy.wait()
        for i in range(per):
            block = msgs[n, i * BLOCK : (i + 1) * BLOCK, :]
            vt[n * per + i] = jnp.transpose(block)[HEAD_DIM:, :]
        if n % inner == 0:
            k = n // inner
            for r in range(half):
                start = (per + r) * BLOCK
                both = jnp.transpose(msgs[n, start : start + BLOCK, :])
                qt[k * per + r] = jnp.concatenate([both[:HEAD_DIM], zero], axis=0)
                qt[k * per + r + half] = jnp.concatenate([both[HEAD_DIM:], zero], axis=0)
    qt[nq] = jnp.zeros((LANES, BLOCK), jnp.bfloat16)
    m_s[...] = jnp.full(m_s.shape, NEG, jnp.float32)
    l_s[...] = jnp.zeros(l_s.shape, jnp.float32)
    acc_s[...] = jnp.zeros(acc_s.shape, jnp.float32)

    def keys(s, t):
        return [which[s, t * SLOTS + e] for e in range(SLOTS)]

    def score(t):
        for s in range(STREAMS):
            qi = who[s, t]
            q = qt[qi]
            tiles = []
            for e, slot in enumerate(keys(s, t)):
                row = pl.multiple_of((slot % per) * BLOCK, BLOCK)
                tile = jnp.dot(
                    msgs[slot // per, pl.ds(row, BLOCK), :], q, preferred_element_type=jnp.float32
                )
                sc[s, e] = tile
                tiles.append(tile.reshape(BLOCK // 8, 8, BLOCK))
            top = jnp.max(functools.reduce(jnp.maximum, tiles), axis=0)
            top = jnp.max(top, axis=0, keepdims=True)
            m_old = jnp.where(first[s, t] == 1, NEG, m_s[s])
            m_new = jnp.maximum(m_old, top)
            al_s[s] = jnp.exp(m_old - m_new)
            m_s[s] = m_new

    def weigh(t):
        for s in range(STREAMS):
            qi = who[s, t]
            n_valid = valid[s, t]
            m, alpha = m_s[s], al_s[s]
            acc = acc_s[qi] * alpha
            total = l_s[qi] * alpha
            ids = keys(s, t)
            for e in range(0, SLOTS, 2):
                probs = []
                for f in (e, e + 1):
                    shut = m + jnp.where(f < n_valid, 0.0, -NEG)
                    p = jnp.exp(sc[s, f] - shut)
                    total = total + jnp.sum(p.reshape(BLOCK // 8, 8, BLOCK), axis=0)
                    probs.append(p.astype(jnp.bfloat16))
                acc = acc + jnp.dot(
                    jnp.concatenate([vt[ids[e]], vt[ids[e + 1]]], axis=1),
                    jnp.concatenate(probs, axis=0),
                    preferred_element_type=jnp.float32,
                )
            acc_s[qi] = acc
            l_s[qi] = total

    score(0)

    def step(t, _):
        weigh(t)
        score(t + 1)
        return 0

    lax.fori_loop(0, steps[0], step, 0)
    for k in range(outer):
        for r in range(half):
            done = []
            for i in (k * per + r, k * per + r + half):
                done.append(acc_s[i] * (1.0 / jnp.sum(l_s[i], axis=0, keepdims=True)))
            os[k, r * BLOCK : (r + 1) * BLOCK, :] = jnp.transpose(
                jnp.concatenate(done, axis=0)
            ).astype(jnp.bfloat16)
    backs = [pltpu.make_async_copy(os.at[n], out, sems.at[n]) for n, out in enumerate(outs)]
    for copy in backs:
        copy.start()
    for copy in backs:
        copy.wait()


def out_kernel(inner, heads, groups, *refs):
    pieces = [refs[g * heads : (g + 1) * heads] for g in range(groups)]
    ws = refs[groups * heads : groups * heads + groups]
    out = refs[-1]
    a = lax.axis_index("ctx") // inner
    half = pieces[0][0].shape[0]
    low = low_half((half, LANES))
    tops, bottoms, rows = [], [], []
    for g in range(groups):
        for k in range(0, heads, 2):
            p0 = pieces[g][k][...].astype(jnp.float32)
            p1 = pieces[g][k + 1][...].astype(jnp.float32)
            tops.append(jnp.where(low, p0, swap_halves(p1)).astype(jnp.bfloat16))
            bottoms.append(jnp.where(low, swap_halves(p0), p1).astype(jnp.bfloat16))
            for e in (0, 1):
                start = pl.multiple_of(HEAD_DIM * (a ^ (k + e)), HEAD_DIM)
                rows.append(ws[g][pl.ds(start, HEAD_DIM), :])
    w = jnp.concatenate(rows, axis=0)
    for n, parts in enumerate((tops, bottoms)):
        x = jnp.concatenate(parts, axis=1)
        out[n * half : (n + 1) * half, :] = jnp.dot(
            x, w, preferred_element_type=jnp.float32
        ).astype(out.dtype)


def solution(mesh):
    ctx, groups = mesh.shape["ctx"], mesh.shape["head"]

    def body(tokens, w_query, w_key, w_value, w_out, block_mask, block_order):
        rows = tokens.shape[0]
        heads = w_query.shape[1] // HEAD_DIM
        inner = ctx // heads
        per = rows // BLOCK
        nb = block_mask.shape[0]
        nq = heads * per
        cols = w_out.shape[1] // groups
        bf = jnp.bfloat16
        params = pltpu.CompilerParams(vmem_limit_bytes=BIG)
        both = ("ctx", "head")
        places = [(c // inner, c % inner, h) for c in range(ctx) for h in range(groups)]

        def index(a, b, h):
            return (a * inner + b) * groups + h

        def turn(x, j):
            pairs = [
                (index(a, b, h), index(a ^ j, (b & ~1) | (h & 1), (h & ~1) | (b & 1)))
                for a, b, h in places
            ]
            return lax.ppermute(x, both, pairs)

        def spread(x, e):
            pairs = [
                (index(a, b, h), index(a, b ^ (e & ~1), h ^ (e & 1))) for a, b, h in places
            ]
            return lax.ppermute(x, both, pairs) if e else x

        def head_swap(x, j):
            return lax.ppermute(x, "head", [(h, h ^ j) for h in range(groups)]) if j else x

        size = rows + rows // 2
        msgs = pl.pallas_call(
            functools.partial(proj_kernel, inner, heads),
            out_shape=[jax.ShapeDtypeStruct((size, LANES), bf)] * heads,
            in_specs=[VMEM] * 4,
            out_specs=[ANY] * heads,
            scratch_shapes=[
                pltpu.VMEM((heads, size, LANES), bf),
                pltpu.SemaphoreType.DMA((heads,)),
            ],
            compiler_params=params,
            name="proj",
        )(tokens, w_query, w_key, w_value)
        got = [turn(msgs[j], j) for j in range(heads)]
        every = [spread(got[j], e) for j in range(heads) for e in range(inner)]
        longest = -(-nb // SLOTS)
        cap = -(-nq * longest // STREAMS) + longest + 2
        tables = pl.pallas_call(
            functools.partial(list_kernel, inner, heads, per, cap),
            out_shape=[
                jax.ShapeDtypeStruct((STREAMS, cap), jnp.int32),
                jax.ShapeDtypeStruct((STREAMS, cap * SLOTS), jnp.int32),
                jax.ShapeDtypeStruct((STREAMS, cap), jnp.int32),
                jax.ShapeDtypeStruct((STREAMS, cap), jnp.int32),
                jax.ShapeDtypeStruct((1,), jnp.int32),
            ],
            in_specs=[SMEM] * 2,
            out_specs=[SMEM] * 5,
            scratch_shapes=[pltpu.SMEM((nb,), jnp.int32), pltpu.SMEM((STREAMS,), jnp.int32)],
            name="block_lists",
        )(block_mask, block_order)
        h = lax.axis_index("head")
        w_cols = [
            head_swap(lax.dynamic_slice_in_dim(w_out, (h ^ j) * cols, cols, axis=1), j)
            for j in range(groups)
        ]
        o = pl.pallas_call(
            functools.partial(attend_kernel, inner, heads, per),
            out_shape=[jax.ShapeDtypeStruct((rows // 2, LANES), bf)] * heads,
            in_specs=[SMEM] * 5 + [ANY] * (heads * inner),
            out_specs=[ANY] * heads,
            scratch_shapes=[
                pltpu.VMEM((heads * inner, size, LANES), bf),
                pltpu.VMEM((nb, HEAD_DIM, BLOCK), bf),
                pltpu.VMEM((nq + 1, LANES, BLOCK), bf),
                pltpu.VMEM((STREAMS, SLOTS, BLOCK, BLOCK), jnp.float32),
                pltpu.VMEM((STREAMS, 1, BLOCK), jnp.float32),
                pltpu.VMEM((STREAMS, 1, BLOCK), jnp.float32),
                pltpu.VMEM((nq + 1, 8, BLOCK), jnp.float32),
                pltpu.VMEM((nq + 1, HEAD_DIM, BLOCK), jnp.float32),
                pltpu.VMEM((heads, rows // 2, LANES), bf),
                pltpu.SemaphoreType.DMA((heads * inner,)),
            ],
            compiler_params=params,
            name="attend",
        )(*tables, *every)
        mine = [turn(o[j], j) for j in range(heads)]
        parts = [mine]
        for j in range(1, groups):
            if j % 2:
                parts.append([head_swap(x, 1) for x in parts[j - 1]])
            else:
                parts.append([head_swap(x, j) for x in mine])
        return pl.pallas_call(
            functools.partial(out_kernel, inner, heads, groups),
            out_shape=jax.ShapeDtypeStruct((rows, cols), bf),
            in_specs=[VMEM] * (groups * heads + groups),
            out_specs=VMEM,
            compiler_params=params,
            name="out_proj",
        )(*[x for part in parts for x in part], *w_cols)

    placed = (
        P("ctx", None),
        P(None, "head"),
        P(None, "head"),
        P(None, "head"),
        P("head", None),
        P(),
        P(),
    )
    return jax.shard_map(
        body, mesh=mesh, in_specs=placed, out_specs=P("ctx", "head"), check_vma=False
    )
```

```python
import functools

import jax
import jax.numpy as jnp
from jax import lax
from jax.experimental import pallas as pl
from jax.experimental.pallas import tpu as pltpu
from jax.sharding import PartitionSpec as P

HEAD_DIM = 64
BLOCK = 128
LANES = 128
SLOTS = 4
STREAMS = 4
NEG = -1e30


ANY = pl.BlockSpec(memory_space=pl.ANY)
VMEM = pl.BlockSpec(memory_space=pltpu.VMEM)
SMEM = pl.BlockSpec(memory_space=pltpu.SMEM)
GRANT = 16 * 1024 * 1024


def low_half(shape):
    return lax.broadcasted_iota(jnp.int32, shape, len(shape) - 1) < HEAD_DIM


def swap_halves(x):
    return pltpu.roll(x, HEAD_DIM, 1)


def proj_kernel(inner, heads, tok, wq, wk, wv, *rest):
    outs, (msg, sems) = rest[:heads], rest[heads:]
    a = lax.axis_index("ctx") // inner
    t = tok[...]
    rows = t.shape[0]
    half = rows // 2
    k = jnp.dot(t, wk[...], preferred_element_type=jnp.float32)
    v = jnp.dot(t, wv[...], preferred_element_type=jnp.float32)
    q = jnp.dot(t, wq[...], preferred_element_type=jnp.float32) * HEAD_DIM ** (-0.5)
    low = low_half((rows, LANES))
    for h in range(heads):
        cols = slice(LANES * (h // 2), LANES * (h // 2) + LANES)
        kk, vv, top, bottom = k[:, cols], v[:, cols], q[:half, cols], q[half:, cols]
        if h % 2 == 0:
            vv, bottom = swap_halves(vv), swap_halves(bottom)
        else:
            kk, top = swap_halves(kk), swap_halves(top)
        msg[h, :rows] = jnp.where(low, kk, vv).astype(jnp.bfloat16)
        msg[h, rows:] = jnp.where(low[:half], top, bottom).astype(jnp.bfloat16)
    copies = [
        pltpu.make_async_copy(msg.at[a ^ j], out, sems.at[j]) for j, out in enumerate(outs)
    ]
    for copy in copies:
        copy.start()
    for copy in copies:
        copy.wait()


def list_kernel(inner, outer, per, cap, mask, order, who, which, valid, first, steps, names, load):
    c = lax.axis_index("ctx")
    a = c // inner
    b = (c % inner) // 2 * 2 + lax.axis_index("head") % 2
    blocks = inner * outer * per

    def name(slot, _):
        dev = slot // per
        kb = (((dev // inner) ^ a) * inner + ((dev % inner) ^ b)) * per + slot % per
        names[slot] = order[kb]
        return 0

    lax.fori_loop(0, blocks, name, 0)
    for s in range(STREAMS):
        load[s] = 0

    def row(qi, _):
        qb = (((qi // per) ^ a) * inner + b) * per + qi % per
        own = order[qb]
        s, least = 0, load[0]
        for other in range(1, STREAMS):
            better = load[other] < least
            s = jnp.where(better, other, s)
            least = jnp.minimum(load[other], least)
        base = least * SLOTS

        def col(slot, count):
            which[s, base + count] = slot
            return count + mask[own, names[slot]]

        count = lax.fori_loop(0, blocks, col, 0, unroll=4)
        keep = which[s, base]
        for extra in range(SLOTS):
            which[s, base + count + extra] = keep
        items = (count + SLOTS - 1) // SLOTS

        def item(t, _):
            who[s, least + t] = qi
            valid[s, least + t] = count - t * SLOTS
            first[s, least + t] = jnp.where(t == 0, 1, 0)
            return 0

        lax.fori_loop(0, items, item, 0)
        load[s] = least + items
        return 0

    lax.fori_loop(0, outer * per, row, 0)
    most = load[0]
    for s in range(1, STREAMS):
        most = jnp.maximum(most, load[s])
    steps[0] = most
    for s in range(STREAMS):
        last = jnp.maximum(load[s] - 1, 0)
        idle = load[s] == 0
        qi = jnp.where(idle, outer * per, who[s, last])
        key = jnp.where(idle, 0, which[s, last * SLOTS])

        def fill(t, _):
            who[s, t] = qi
            valid[s, t] = 0
            first[s, t] = 0
            for e in range(SLOTS):
                which[s, t * SLOTS + e] = key
            return 0

        lax.fori_loop(load[s], most + 1, fill, 0)


def attend_kernel(inner, outer, per, who, which, valid, first, steps, *rest):
    n_in = inner * outer
    ins, rest = rest[:n_in], rest[n_in:]
    outs, rest = rest[:outer], rest[outer:]
    msgs, vt, qt, sc, m_s, al_s, l_s, acc_s, os, sems = rest
    copies = [pltpu.make_async_copy(src, msgs.at[n], sems.at[n]) for n, src in enumerate(ins)]
    for copy in copies:
        copy.start()
    half = per // 2
    nq = outer * per
    zero = jnp.zeros((HEAD_DIM, BLOCK), jnp.bfloat16)
    for n, copy in enumerate(copies):
        copy.wait()
        for i in range(per):
            block = msgs[n, i * BLOCK : (i + 1) * BLOCK, :]
            vt[n * per + i] = jnp.transpose(block)[HEAD_DIM:, :]
        if n % inner == 0:
            k = n // inner
            for r in range(half):
                start = (per + r) * BLOCK
                both = jnp.transpose(msgs[n, start : start + BLOCK, :])
                qt[k * per + r] = jnp.concatenate([both[:HEAD_DIM], zero], axis=0)
                qt[k * per + r + half] = jnp.concatenate([both[HEAD_DIM:], zero], axis=0)
    qt[nq] = jnp.zeros((LANES, BLOCK), jnp.bfloat16)
    m_s[...] = jnp.full(m_s.shape, NEG, jnp.float32)
    l_s[...] = jnp.zeros(l_s.shape, jnp.float32)
    acc_s[...] = jnp.zeros(acc_s.shape, jnp.float32)

    def keys(s, t):
        return [which[s, t * SLOTS + e] for e in range(SLOTS)]

    def score(t):
        for s in range(STREAMS):
            qi = who[s, t]
            q = qt[qi]
            tiles = []
            for e, slot in enumerate(keys(s, t)):
                row = pl.multiple_of((slot % per) * BLOCK, BLOCK)
                tile = jnp.dot(
                    msgs[slot // per, pl.ds(row, BLOCK), :], q, preferred_element_type=jnp.float32
                )
                sc[s, e] = tile
                tiles.append(tile.reshape(BLOCK // 8, 8, BLOCK))
            top = jnp.max(functools.reduce(jnp.maximum, tiles), axis=0)
            top = jnp.max(top, axis=0, keepdims=True)
            m_old = jnp.where(first[s, t] == 1, NEG, m_s[s])
            m_new = jnp.maximum(m_old, top)
            al_s[s] = jnp.exp(m_old - m_new)
            m_s[s] = m_new

    def weigh(t):
        for s in range(STREAMS):
            qi = who[s, t]
            n_valid = valid[s, t]
            m, alpha = m_s[s], al_s[s]
            acc = acc_s[qi] * alpha
            total = l_s[qi] * alpha
            ids = keys(s, t)
            for e in range(0, SLOTS, 2):
                probs = []
                for f in (e, e + 1):
                    shut = m + jnp.where(f < n_valid, 0.0, -NEG)
                    p = jnp.exp(sc[s, f] - shut)
                    total = total + jnp.sum(p.reshape(BLOCK // 8, 8, BLOCK), axis=0)
                    probs.append(p.astype(jnp.bfloat16))
                acc = acc + jnp.dot(
                    jnp.concatenate([vt[ids[e]], vt[ids[e + 1]]], axis=1),
                    jnp.concatenate(probs, axis=0),
                    preferred_element_type=jnp.float32,
                )
            acc_s[qi] = acc
            l_s[qi] = total

    score(0)

    def step(t, _):
        weigh(t)
        score(t + 1)
        return 0

    lax.fori_loop(0, steps[0], step, 0)
    for k in range(outer):
        for r in range(half):
            done = []
            for i in (k * per + r, k * per + r + half):
                done.append(acc_s[i] * (1.0 / jnp.sum(l_s[i], axis=0, keepdims=True)))
            os[k, r * BLOCK : (r + 1) * BLOCK, :] = jnp.transpose(
                jnp.concatenate(done, axis=0)
            ).astype(jnp.bfloat16)
    backs = [pltpu.make_async_copy(os.at[n], out, sems.at[n]) for n, out in enumerate(outs)]
    for copy in backs:
        copy.start()
    for copy in backs:
        copy.wait()


def out_kernel(inner, heads, groups, *refs):
    pieces = [refs[g * heads : (g + 1) * heads] for g in range(groups)]
    ws = refs[groups * heads : groups * heads + groups]
    out = refs[-1]
    a = lax.axis_index("ctx") // inner
    half = pieces[0][0].shape[0]
    low = low_half((half, LANES))
    tops, bottoms, rows = [], [], []
    for g in range(groups):
        for k in range(0, heads, 2):
            p0 = pieces[g][k][...].astype(jnp.float32)
            p1 = pieces[g][k + 1][...].astype(jnp.float32)
            tops.append(jnp.where(low, p0, swap_halves(p1)).astype(jnp.bfloat16))
            bottoms.append(jnp.where(low, swap_halves(p0), p1).astype(jnp.bfloat16))
            for e in (0, 1):
                start = pl.multiple_of(HEAD_DIM * (a ^ (k + e)), HEAD_DIM)
                rows.append(ws[g][pl.ds(start, HEAD_DIM), :])
    w = jnp.concatenate(rows, axis=0)
    for n, parts in enumerate((tops, bottoms)):
        x = jnp.concatenate(parts, axis=1)
        out[n * half : (n + 1) * half, :] = jnp.dot(
            x, w, preferred_element_type=jnp.float32
        ).astype(out.dtype)


def solution(mesh):
    ctx, groups = mesh.shape["ctx"], mesh.shape["head"]

    def body(tokens, w_query, w_key, w_value, w_out, block_mask, block_order):
        rows = tokens.shape[0]
        heads = w_query.shape[1] // HEAD_DIM
        inner = ctx // heads
        per = rows // BLOCK
        nb = block_mask.shape[0]
        nq = heads * per
        cols = w_out.shape[1] // groups
        bf = jnp.bfloat16
        params = pltpu.CompilerParams(vmem_limit_bytes=GRANT)
        both = ("ctx", "head")
        places = [(c // inner, c % inner, h) for c in range(ctx) for h in range(groups)]

        def index(a, b, h):
            return (a * inner + b) * groups + h

        def turn(x, j):
            pairs = [
                (index(a, b, h), index(a ^ j, (b & ~1) | (h & 1), (h & ~1) | (b & 1)))
                for a, b, h in places
            ]
            return lax.ppermute(x, both, pairs)

        def spread(x, e):
            pairs = [
                (index(a, b, h), index(a, b ^ (e & ~1), h ^ (e & 1))) for a, b, h in places
            ]
            return lax.ppermute(x, both, pairs) if e else x

        def head_swap(x, j):
            return lax.ppermute(x, "head", [(h, h ^ j) for h in range(groups)]) if j else x

        size = rows + rows // 2
        msgs = pl.pallas_call(
            functools.partial(proj_kernel, inner, heads),
            out_shape=[jax.ShapeDtypeStruct((size, LANES), bf)] * heads,
            in_specs=[VMEM] * 4,
            out_specs=[ANY] * heads,
            scratch_shapes=[
                pltpu.VMEM((heads, size, LANES), bf),
                pltpu.SemaphoreType.DMA((heads,)),
            ],
            compiler_params=params,
            name="proj",
        )(tokens, w_query, w_key, w_value)
        got = [turn(msgs[j], j) for j in range(heads)]
        longest = -(-nb // SLOTS)
        cap = -(-nq * longest // STREAMS) + longest + 2
        tables = pl.pallas_call(
            functools.partial(list_kernel, inner, heads, per, cap),
            out_shape=[
                jax.ShapeDtypeStruct((STREAMS, cap), jnp.int32),
                jax.ShapeDtypeStruct((STREAMS, cap * SLOTS), jnp.int32),
                jax.ShapeDtypeStruct((STREAMS, cap), jnp.int32),
                jax.ShapeDtypeStruct((STREAMS, cap), jnp.int32),
                jax.ShapeDtypeStruct((1,), jnp.int32),
            ],
            in_specs=[SMEM] * 2,
            out_specs=[SMEM] * 5,
            scratch_shapes=[pltpu.SMEM((nb,), jnp.int32), pltpu.SMEM((STREAMS,), jnp.int32)],
            name="block_lists",
        )(block_mask, block_order)
        h = lax.axis_index("head")
        w_out, msgs = lax.optimization_barrier((w_out, msgs))
        w_cols = [
            head_swap(lax.dynamic_slice_in_dim(w_out, (h ^ j) * cols, cols, axis=1), j)
            for j in range(groups)
        ]
        got[0], tables, w_cols = lax.optimization_barrier((got[0], tables, w_cols))
        every = [spread(got[j], e) for j in range(heads) for e in range(inner)]
        o = pl.pallas_call(
            functools.partial(attend_kernel, inner, heads, per),
            out_shape=[jax.ShapeDtypeStruct((rows // 2, LANES), bf)] * heads,
            in_specs=[SMEM] * 5 + [ANY] * (heads * inner),
            out_specs=[ANY] * heads,
            scratch_shapes=[
                pltpu.VMEM((heads * inner, size, LANES), bf),
                pltpu.VMEM((nb, HEAD_DIM, BLOCK), bf),
                pltpu.VMEM((nq + 1, LANES, BLOCK), bf),
                pltpu.VMEM((STREAMS, SLOTS, BLOCK, BLOCK), jnp.float32),
                pltpu.VMEM((STREAMS, 1, BLOCK), jnp.float32),
                pltpu.VMEM((STREAMS, 1, BLOCK), jnp.float32),
                pltpu.VMEM((nq + 1, 8, BLOCK), jnp.float32),
                pltpu.VMEM((nq + 1, HEAD_DIM, BLOCK), jnp.float32),
                pltpu.VMEM((heads, rows // 2, LANES), bf),
                pltpu.SemaphoreType.DMA((heads * inner,)),
            ],
            compiler_params=params,
            name="attend",
        )(*tables, *every)
        mine = [turn(o[j], j) for j in range(heads)]
        parts = [mine]
        for j in range(1, groups):
            if j % 2:
                parts.append([head_swap(x, 1) for x in parts[j - 1]])
            else:
                parts.append([head_swap(x, j) for x in mine])
        return pl.pallas_call(
            functools.partial(out_kernel, inner, heads, groups),
            out_shape=jax.ShapeDtypeStruct((rows, cols), bf),
            in_specs=[VMEM] * (groups * heads + groups),
            out_specs=VMEM,
            compiler_params=params,
            name="out_proj",
        )(*[x for part in parts for x in part], *w_cols)

    placed = (
        P("ctx", None),
        P(None, "head"),
        P(None, "head"),
        P(None, "head"),
        P("head", None),
        P(),
        P(),
    )
    return jax.shard_map(
        body, mesh=mesh, in_specs=placed, out_specs=P("ctx", "head"), check_vma=False
    )
```

```python
import functools

import jax
import jax.numpy as jnp
from jax import lax
from jax.experimental import pallas as pl
from jax.experimental.pallas import tpu as pltpu
from jax.sharding import PartitionSpec as P


HEAD_DIM = 64
BLOCK = 128
LANES = 128
SLOTS = 4
STREAMS = 4
NEG = -1e30


HBM = pl.BlockSpec(memory_space=pltpu.HBM)
VMEM = pl.BlockSpec(memory_space=pltpu.VMEM)
SMEM = pl.BlockSpec(memory_space=pltpu.SMEM)
GRANT = 16 * 1024 * 1024
WHOLE = 60 * 1024 * 1024


def low_half(shape):
    return lax.broadcasted_iota(jnp.int32, shape, len(shape) - 1) < HEAD_DIM


def swap_halves(x):
    return pltpu.roll(x, HEAD_DIM, 1)


def proj_kernel(inner, heads, tok_in, wk_in, wv_in, wq_in, *rest):
    outs, (tok, wk, wv, wq, msg, sems) = rest[:heads], rest[heads:]
    loads = [
        pltpu.make_async_copy(src, dst, sems.at[n])
        for n, (src, dst) in enumerate(((tok_in, tok), (wv_in, wv), (wk_in, wk), (wq_in, wq)))
    ]
    for load in loads:
        load.start()
    a = lax.axis_index("ctx") // inner
    rows = tok.shape[0]
    low = low_half((rows, LANES))
    loads[0].wait()
    loads[1].wait()
    v = jnp.dot(tok[...], wv[...], preferred_element_type=jnp.float32)
    loads[2].wait()
    loads[3].wait()
    k = jnp.dot(tok[...], wk[...], preferred_element_type=jnp.float32)
    q = jnp.dot(tok[...], wq[...], preferred_element_type=jnp.float32) * HEAD_DIM ** (-0.5)
    for g in range(heads // 2):
        for i in range(rows // BLOCK):
            block = v[i * BLOCK : (i + 1) * BLOCK, g * LANES : (g + 1) * LANES]
            turned = jnp.transpose(block).astype(jnp.bfloat16)
            start = rows + i * HEAD_DIM
            msg[2 * g, start : start + HEAD_DIM] = turned[:HEAD_DIM]
            msg[2 * g + 1, start : start + HEAD_DIM] = turned[HEAD_DIM:]
    for h in range(heads):
        cols = slice(LANES * (h // 2), LANES * (h // 2) + LANES)
        kk, qq = k[:, cols], q[:, cols]
        if h % 2 == 0:
            qq = swap_halves(qq)
        else:
            kk = swap_halves(kk)
        msg[h, :rows] = jnp.where(low, kk, qq).astype(jnp.bfloat16)
    for j, out in enumerate(outs):
        out[...] = msg[a ^ j]


def list_kernel(inner, outer, per, mask, order, who, which, valid, first, steps, names, load):
    c = lax.axis_index("ctx")
    a = c // inner
    b = (c % inner) // 2 * 2 + lax.axis_index("head") % 2
    blocks = inner * outer * per

    def name(slot, _):
        dev = slot // per
        kb = (((dev // inner) ^ a) * inner + ((dev % inner) ^ b)) * per + slot % per
        names[slot] = order[kb]
        return 0

    lax.fori_loop(0, blocks, name, 0)
    for s in range(STREAMS):
        load[s] = 0

    def row(qi, _):
        qb = (((qi // per) ^ a) * inner + b) * per + qi % per
        own = order[qb]
        s, least = 0, load[0]
        for other in range(1, STREAMS):
            better = load[other] < least
            s = jnp.where(better, other, s)
            least = jnp.minimum(load[other], least)
        base = least * SLOTS

        def col(slot, count):
            which[s, base + count] = slot
            return count + mask[own, names[slot]]

        count = lax.fori_loop(0, blocks, col, 0, unroll=4)
        keep = which[s, base]
        for extra in range(SLOTS):
            which[s, base + count + extra] = keep
        items = (count + SLOTS - 1) // SLOTS

        def item(t, _):
            who[s, least + t] = qi
            valid[s, least + t] = count - t * SLOTS
            first[s, least + t] = jnp.where(t == 0, 1, 0)
            return 0

        lax.fori_loop(0, items, item, 0)
        load[s] = least + items
        return 0

    lax.fori_loop(0, outer * per, row, 0)
    most = load[0]
    for s in range(1, STREAMS):
        most = jnp.maximum(most, load[s])
    steps[0] = most
    for s in range(STREAMS):
        last = jnp.maximum(load[s] - 1, 0)
        idle = load[s] == 0
        qi = jnp.where(idle, outer * per, who[s, last])
        key = jnp.where(idle, 0, which[s, last * SLOTS])

        def fill(t, _):
            who[s, t] = qi
            valid[s, t] = 0
            first[s, t] = 0
            for e in range(SLOTS):
                which[s, t * SLOTS + e] = key
            return 0

        lax.fori_loop(load[s], most + 2, fill, 0)


def attend_kernel(inner, outer, per, who, which, valid, first, steps, *rest):
    n_in = inner * outer
    ins, rest = rest[:n_in], rest[n_in:]
    outs, rest = rest[:outer], rest[outer:]
    kq, vt, qt, sc, m_s, al_s, l_s, acc_s, l_all, acc_all = rest
    half = per // 2
    nq = outer * per
    rows = per * BLOCK
    zero = jnp.zeros((HEAD_DIM, BLOCK), jnp.bfloat16)
    for n, msg in enumerate(ins):
        for i in range(per):
            block = msg[i * BLOCK : (i + 1) * BLOCK, :]
            kq[n * per + i] = block
            start = rows + i * HEAD_DIM
            vt[n * per + i] = msg[start : start + HEAD_DIM, :]
            if n % inner == 0:
                turned = jnp.transpose(block)[HEAD_DIM:]
                qt[n // inner * per + i] = jnp.concatenate([turned, zero], axis=0)
    qt[nq] = jnp.zeros((LANES, BLOCK), jnp.bfloat16)
    m_s[...] = jnp.full(m_s.shape, NEG, jnp.float32)
    l_s[...] = jnp.zeros(l_s.shape, jnp.float32)
    acc_s[...] = jnp.zeros(acc_s.shape, jnp.float32)

    def keys(s, t):
        return [which[s, t * SLOTS + e] for e in range(SLOTS)]

    def score(t, buf):
        for s in range(STREAMS):
            q = qt[who[s, t]]
            tiles = []
            for e, slot in enumerate(keys(s, t)):
                tile = jnp.dot(kq[slot], q, preferred_element_type=jnp.float32)
                sc[buf, s, e] = tile
                tiles.append(tile.reshape(BLOCK // 8, 8, BLOCK))
            top = jnp.max(functools.reduce(jnp.maximum, tiles), axis=0)
            top = jnp.max(top, axis=0, keepdims=True)
            m_old = jnp.where(first[s, t] == 1, NEG, m_s[1 - buf, s])
            m_new = jnp.maximum(m_old, top)
            al_s[buf, s] = jnp.exp(m_old - m_new)
            m_s[buf, s] = m_new

    def weigh(t, buf):
        for s in range(STREAMS):
            qi = who[s, t]
            n_valid = valid[s, t]
            m, alpha = m_s[buf, s], al_s[buf, s]
            acc = acc_s[s] * alpha
            total = l_s[s] * alpha
            ids = keys(s, t)
            for e in range(0, SLOTS, 2):
                probs = []
                for f in (e, e + 1):
                    shut = m + jnp.where(f < n_valid, 0.0, -NEG)
                    p = jnp.exp(sc[buf, s, f] - shut)
                    total = total + jnp.sum(p.reshape(BLOCK // 8, 8, BLOCK), axis=0)
                    probs.append(p.astype(jnp.bfloat16))
                acc = acc + jnp.dot(
                    jnp.concatenate([vt[ids[e]], vt[ids[e + 1]]], axis=1),
                    jnp.concatenate(probs, axis=0),
                    preferred_element_type=jnp.float32,
                )
            acc_s[s] = acc
            l_s[s] = total
            acc_all[qi] = acc
            l_all[qi] = total

    score(0, 0)

    def step(u, _):
        t = 2 * u
        score(t + 1, 1)
        weigh(t, 0)
        score(t + 2, 0)
        weigh(t + 1, 1)
        return 0

    lax.fori_loop(0, (steps[0] + 1) // 2, step, 0)
    for k in range(outer):
        for r in range(half):
            done = []
            for i in (k * per + r, k * per + r + half):
                done.append(acc_all[i] * (1.0 / jnp.sum(l_all[i], axis=0, keepdims=True)))
            outs[k][r * BLOCK : (r + 1) * BLOCK, :] = jnp.transpose(
                jnp.concatenate(done, axis=0)
            ).astype(jnp.bfloat16)


def out_kernel(inner, heads, groups, *refs):
    pieces = [refs[g * heads : (g + 1) * heads] for g in range(groups)]
    ws = refs[groups * heads : groups * heads + groups]
    out = refs[-1]
    a = lax.axis_index("ctx") // inner
    half = pieces[0][0].shape[0]
    low = low_half((half, LANES))
    tops, bottoms, rows = [], [], []
    for g in range(groups):
        for k in range(0, heads, 2):
            p0 = pieces[g][k][...].astype(jnp.float32)
            p1 = pieces[g][k + 1][...].astype(jnp.float32)
            tops.append(jnp.where(low, p0, swap_halves(p1)).astype(jnp.bfloat16))
            bottoms.append(jnp.where(low, swap_halves(p0), p1).astype(jnp.bfloat16))
            for e in (0, 1):
                start = pl.multiple_of(HEAD_DIM * (a ^ (k + e)), HEAD_DIM)
                rows.append(ws[g][pl.ds(start, HEAD_DIM), :])
    w = jnp.concatenate(rows, axis=0)
    for n, parts in enumerate((tops, bottoms)):
        x = jnp.concatenate(parts, axis=1)
        out[n * half : (n + 1) * half, :] = jnp.dot(
            x, w, preferred_element_type=jnp.float32
        ).astype(out.dtype)


def solution(mesh):
    ctx, groups = mesh.shape["ctx"], mesh.shape["head"]

    def body(tokens, w_query, w_key, w_value, w_out, block_mask, block_order):
        rows = tokens.shape[0]
        heads = w_query.shape[1] // HEAD_DIM
        inner = ctx // heads
        per = rows // BLOCK
        nb = block_mask.shape[0]
        nq = heads * per
        cols = w_out.shape[1] // groups
        bf = jnp.bfloat16
        params = pltpu.CompilerParams(vmem_limit_bytes=GRANT)
        both = ("ctx", "head")
        places = [(c // inner, c % inner, h) for c in range(ctx) for h in range(groups)]

        def index(a, b, h):
            return (a * inner + b) * groups + h

        def turn(x, j):
            pairs = [
                (index(a, b, h), index(a ^ j, (b & ~1) | (h & 1), (h & ~1) | (b & 1)))
                for a, b, h in places
            ]
            return lax.ppermute(x, both, pairs)

        def spread(x, e):
            pairs = [
                (index(a, b, h), index(a, b ^ (e & ~1), h ^ (e & 1))) for a, b, h in places
            ]
            return lax.ppermute(x, both, pairs) if e else x

        def head_swap(x, j):
            return lax.ppermute(x, "head", [(h, h ^ j) for h in range(groups)]) if j else x

        size = rows + rows // 2
        msgs = pl.pallas_call(
            functools.partial(proj_kernel, inner, heads),
            out_shape=[jax.ShapeDtypeStruct((size, LANES), bf)] * heads,
            in_specs=[HBM] * 4,
            out_specs=[VMEM] * heads,
            scratch_shapes=[pltpu.VMEM(x.shape, bf) for x in (tokens, w_value, w_key, w_query)]
            + [
                pltpu.VMEM((heads, size, LANES), bf),
                pltpu.SemaphoreType.DMA((4,)),
            ],
            compiler_params=pltpu.CompilerParams(vmem_limit_bytes=WHOLE),
            name="proj",
        )(tokens, w_key, w_value, w_query)
        got = [None] * heads
        for j in reversed(range(heads)):
            got[j] = turn(msgs[j], j)
        longest = -(-nb // SLOTS)
        cap = -(-nq * longest // STREAMS) + longest + 3
        tables = pl.pallas_call(
            functools.partial(list_kernel, inner, heads, per),
            out_shape=[
                jax.ShapeDtypeStruct((STREAMS, cap), jnp.int32),
                jax.ShapeDtypeStruct((STREAMS, cap * SLOTS), jnp.int32),
                jax.ShapeDtypeStruct((STREAMS, cap), jnp.int32),
                jax.ShapeDtypeStruct((STREAMS, cap), jnp.int32),
                jax.ShapeDtypeStruct((1,), jnp.int32),
            ],
            in_specs=[SMEM] * 2,
            out_specs=[SMEM] * 5,
            scratch_shapes=[pltpu.SMEM((nb,), jnp.int32), pltpu.SMEM((STREAMS,), jnp.int32)],
            name="block_lists",
        )(block_mask, block_order)
        h = lax.axis_index("head")
        w_out, msgs = lax.optimization_barrier((w_out, msgs))
        w_cols = [
            head_swap(lax.dynamic_slice_in_dim(w_out, (h ^ j) * cols, cols, axis=1), j)
            for j in range(groups)
        ]
        got[0], tables, w_cols = lax.optimization_barrier((got[0], tables, w_cols))
        every = [spread(got[j], e) for j in range(heads) for e in range(inner)]
        o = pl.pallas_call(
            functools.partial(attend_kernel, inner, heads, per),
            out_shape=[jax.ShapeDtypeStruct((rows // 2, LANES), bf)] * heads,
            in_specs=[SMEM] * 5 + [VMEM] * (heads * inner),
            out_specs=[VMEM] * heads,
            scratch_shapes=[
                pltpu.VMEM((nb, BLOCK, LANES), bf),
                pltpu.VMEM((nb, HEAD_DIM, BLOCK), bf),
                pltpu.VMEM((nq + 1, LANES, BLOCK), bf),
                pltpu.VMEM((2, STREAMS, SLOTS, BLOCK, BLOCK), jnp.float32),
                pltpu.VMEM((2, STREAMS, 1, BLOCK), jnp.float32),
                pltpu.VMEM((2, STREAMS, 1, BLOCK), jnp.float32),
                pltpu.VMEM((STREAMS, 8, BLOCK), jnp.float32),
                pltpu.VMEM((STREAMS, HEAD_DIM, BLOCK), jnp.float32),
                pltpu.VMEM((nq + 1, 8, BLOCK), jnp.float32),
                pltpu.VMEM((nq + 1, HEAD_DIM, BLOCK), jnp.float32),
            ],
            compiler_params=params,
            name="attend",
        )(*tables, *every)
        mine = [turn(o[j], j) for j in reversed(range(heads))][::-1]
        parts = [mine]
        for j in range(1, groups):
            if j % 2:
                parts.append([head_swap(x, 1) for x in parts[j - 1]])
            else:
                parts.append([head_swap(x, j) for x in mine])
        return pl.pallas_call(
            functools.partial(out_kernel, inner, heads, groups),
            out_shape=jax.ShapeDtypeStruct((rows, cols), bf),
            in_specs=[VMEM] * (groups * heads + groups),
            out_specs=VMEM,
            compiler_params=params,
            name="out_proj",
        )(*[x for part in parts for x in part], *w_cols)

    placed = (
        P("ctx", None),
        P(None, "head"),
        P(None, "head"),
        P(None, "head"),
        P("head", None),
        P(),
        P(),
    )
    return jax.shard_map(
        body, mesh=mesh, in_specs=placed, out_specs=P("ctx", "head"), check_vma=False
    )
```

```python
import functools

import jax
import jax.numpy as jnp
from jax import lax
from jax.experimental import pallas as pl
from jax.experimental.pallas import tpu as pltpu
from jax.sharding import PartitionSpec as P


HEAD_DIM = 64
BLOCK = 128
LANES = 128
SLOTS = 4
STREAMS = 4
NEG = -1e30


HBM = pl.BlockSpec(memory_space=pltpu.HBM)
VMEM = pl.BlockSpec(memory_space=pltpu.VMEM)
SMEM = pl.BlockSpec(memory_space=pltpu.SMEM)
GRANT = 16 * 1024 * 1024
WHOLE = 60 * 1024 * 1024


def low_half(shape):
    return lax.broadcasted_iota(jnp.int32, shape, len(shape) - 1) < HEAD_DIM


def swap_halves(x):
    return pltpu.roll(x, HEAD_DIM, 1)


def proj_kernel(inner, heads, near, tok_in, wk_in, wv_in, wq_in, *rest):
    n_out = 2 * heads - near
    outs, (tok, wk, wv, wq, msg, sems) = rest[:n_out], rest[n_out:]
    loads = [
        pltpu.make_async_copy(src, dst, sems.at[n])
        for n, (src, dst) in enumerate(((tok_in, tok), (wv_in, wv), (wk_in, wk), (wq_in, wq)))
    ]
    for load in loads:
        load.start()
    a = lax.axis_index("ctx") // inner
    rows = tok.shape[0]
    half = rows // 2
    low = low_half((half, LANES))
    loads[0].wait()
    loads[1].wait()
    v = jnp.dot(tok[...], wv[...], preferred_element_type=jnp.float32)
    loads[2].wait()
    loads[3].wait()
    q = jnp.dot(tok[...], wq[...], preferred_element_type=jnp.float32) * HEAD_DIM ** (-0.5)
    k = jnp.dot(tok[...], wk[...], preferred_element_type=jnp.float32)
    for base, x in ((half, v), (rows, q)):
        for g in range(heads // 2):
            for i in range(rows // BLOCK):
                block = x[i * BLOCK : (i + 1) * BLOCK, g * LANES : (g + 1) * LANES]
                turned = jnp.transpose(block).astype(jnp.bfloat16)
                start = base + i * HEAD_DIM
                msg[2 * g, start : start + HEAD_DIM] = turned[:HEAD_DIM]
                msg[2 * g + 1, start : start + HEAD_DIM] = turned[HEAD_DIM:]
    for h in range(heads):
        cols = slice(LANES * (h // 2), LANES * (h // 2) + LANES)
        top, bottom = k[:half, cols], k[half:, cols]
        if h % 2 == 0:
            bottom = swap_halves(bottom)
        else:
            top = swap_halves(top)
        msg[h, :half] = jnp.where(low, top, bottom).astype(jnp.bfloat16)
    for j in range(heads):
        if j < near:
            outs[j][...] = msg[a ^ j]
        else:
            outs[j][...] = msg[a ^ j, :rows]
            outs[heads + j - near][...] = msg[a ^ j, rows:]


def list_kernel(inner, outer, per, cap, parts, mask, order, who, which, valid, first, steps, names, load):
    c = lax.axis_index("ctx")
    a = c // inner
    b = (c % inner) // 2 * 2 + lax.axis_index("head") % 2
    blocks = inner * outer * per
    half = per // 2
    size = outer * per // parts

    def name(dev, _):
        kb = ((lax.div(dev, inner) ^ a) * inner + (lax.rem(dev, inner) ^ b)) * per
        for i in range(per):
            names[dev * per + i] = order[kb + i // 2 + i % 2 * half]
        return 0

    lax.fori_loop(0, inner * outer, name, 0)
    for part in range(parts):
        for s in range(STREAMS):
            load[s] = 0

        def row(qi, _):
            qb = ((lax.div(qi, per) ^ a) * inner + b) * per + lax.rem(qi, per)
            own = order[qb]
            s, least = jnp.int32(0), load[0]
            for other in range(1, STREAMS):
                here = load[other]
                s = jnp.where(here < least, other, s)
                least = jnp.minimum(here, least)
            item = (part * STREAMS + s) * cap + least
            base = item * SLOTS

            def col(n, to):
                for e in range(8):
                    slot = n * 8 + e
                    which[to] = slot
                    to = to + mask[own, names[slot]]
                return to

            end = lax.fori_loop(0, blocks // 8, col, base)
            count = end - base
            keep = which[base]
            for extra in range(SLOTS):
                which[end + extra] = keep
            items = lax.div(count + (SLOTS - 1), SLOTS)

            def mark(t, left):
                who[item + t] = qi - part * size
                valid[item + t] = left
                first[item + t] = 0
                return left - SLOTS

            lax.fori_loop(0, items, mark, count)
            first[item] = 1
            load[s] = least + items
            return 0

        lax.fori_loop(part * size, (part + 1) * size, row, 0)
        most = load[0]
        for s in range(1, STREAMS):
            most = jnp.maximum(most, load[s])
        steps[part] = most
        for s in range(STREAMS):
            start = (part * STREAMS + s) * cap
            last = start + jnp.maximum(load[s] - 1, 0)
            idle = load[s] == 0
            qi = jnp.where(idle, size, who[last])
            key = jnp.where(idle, 0, which[last * SLOTS])

            def fill(t, _):
                at = start + t
                who[at] = qi
                valid[at] = 0
                first[at] = 0
                for e in range(SLOTS):
                    which[at * SLOTS + e] = key
                return 0

            lax.fori_loop(load[s], most + 2, fill, 0)


def attend_kernel(part, per, cap, n_kv, spans, who, which, valid, first, steps, *rest):
    ins, rest = rest[:n_kv], rest[n_kv:]
    q_in, rest = rest[: len(spans)], rest[len(spans) :]
    outs, rest = rest[: len(spans)], rest[len(spans) :]
    if part == 0:
        (kq, vt), rest = rest[:2], rest[2:]
    else:
        kq, vt = ins
    qt, sc, m_s, al_s, l_s, acc_s, l_all, acc_all = rest
    half = per // 2
    nq = len(spans) * per
    zero = jnp.zeros((HEAD_DIM, BLOCK), jnp.bfloat16)
    for k, start in enumerate(spans):
        for i in range(per):
            turned = q_in[k][start + i * HEAD_DIM : start + (i + 1) * HEAD_DIM, :]
            qt[0, k * per + i] = jnp.concatenate([turned, zero], axis=0)
            qt[1, k * per + i] = jnp.concatenate([zero, turned], axis=0)
    qt[:, nq] = jnp.zeros((2, LANES, BLOCK), jnp.bfloat16)
    if part == 0:
        for n, msg in enumerate(ins):
            for r in range(half):
                kq[n * half + r] = msg[r * BLOCK : (r + 1) * BLOCK, :]
            for i in range(per):
                start = half * BLOCK + (i // 2 + i % 2 * half) * HEAD_DIM
                vt[n * per + i] = msg[start : start + HEAD_DIM, :]
    m_s[...] = jnp.full(m_s.shape, NEG, jnp.float32)
    l_s[...] = jnp.zeros(l_s.shape, jnp.float32)
    acc_s[...] = jnp.zeros(acc_s.shape, jnp.float32)

    def keys(s, t):
        return [which[((part * STREAMS + s) * cap + t) * SLOTS + e] for e in range(SLOTS)]

    def score(t, buf):
        for s in range(STREAMS):
            qi = who[(part * STREAMS + s) * cap + t]
            tiles = []
            for e, slot in enumerate(keys(s, t)):
                tile = jnp.dot(
                    kq[slot >> 1], qt[slot & 1, qi], preferred_element_type=jnp.float32
                )
                sc[buf, s, e] = tile
                tiles.append(tile.reshape(BLOCK // 8, 8, BLOCK))
            top = jnp.max(functools.reduce(jnp.maximum, tiles), axis=0)
            top = jnp.max(top, axis=0, keepdims=True)
            m_old = jnp.where(first[(part * STREAMS + s) * cap + t] == 1, NEG, m_s[1 - buf, s])
            m_new = jnp.maximum(m_old, top)
            al_s[buf, s] = jnp.exp(m_old - m_new)
            m_s[buf, s] = m_new

    def weigh(t, buf):
        for s in range(STREAMS):
            qi = who[(part * STREAMS + s) * cap + t]
            n_valid = valid[(part * STREAMS + s) * cap + t]
            m, alpha = m_s[buf, s], al_s[buf, s]
            acc = acc_s[s] * alpha
            total = l_s[s] * alpha
            ids = keys(s, t)
            for e in range(0, SLOTS, 2):
                probs = []
                for f in (e, e + 1):
                    shut = m + jnp.where(f < n_valid, 0.0, -NEG)
                    p = jnp.exp(sc[buf, s, f] - shut)
                    total = total + jnp.sum(p.reshape(BLOCK // 8, 8, BLOCK), axis=0)
                    probs.append(p.astype(jnp.bfloat16))
                acc = acc + jnp.dot(
                    jnp.concatenate([vt[ids[e]], vt[ids[e + 1]]], axis=1),
                    jnp.concatenate(probs, axis=0),
                    preferred_element_type=jnp.float32,
                )
            acc_s[s] = acc
            l_s[s] = total
            acc_all[qi] = acc
            l_all[qi] = total

    score(0, 0)

    def step(u, _):
        t = 2 * u
        score(t + 1, 1)
        weigh(t, 0)
        score(t + 2, 0)
        weigh(t + 1, 1)
        return 0

    lax.fori_loop(0, lax.div(steps[part] + 1, 2), step, 0)
    for k in range(len(spans)):
        for r in range(half):
            done = []
            for i in (k * per + r, k * per + r + half):
                done.append(acc_all[i] * (1.0 / jnp.sum(l_all[i], axis=0, keepdims=True)))
            outs[k][r * BLOCK : (r + 1) * BLOCK, :] = jnp.transpose(
                jnp.concatenate(done, axis=0)
            ).astype(jnp.bfloat16)


def out_kernel(inner, heads, groups, *refs):
    pieces = [refs[g * heads : (g + 1) * heads] for g in range(groups)]
    ws = refs[groups * heads : groups * heads + groups]
    out = refs[-1]
    a = lax.axis_index("ctx") // inner
    half = pieces[0][0].shape[0]
    low = low_half((half, LANES))
    tops, bottoms, rows = [], [], []
    for g in range(groups):
        for k in range(0, heads, 2):
            p0 = pieces[g][k][...].astype(jnp.float32)
            p1 = pieces[g][k + 1][...].astype(jnp.float32)
            tops.append(jnp.where(low, p0, swap_halves(p1)).astype(jnp.bfloat16))
            bottoms.append(jnp.where(low, swap_halves(p0), p1).astype(jnp.bfloat16))
            for e in (0, 1):
                start = pl.multiple_of(HEAD_DIM * (a ^ (k + e)), HEAD_DIM)
                rows.append(ws[g][pl.ds(start, HEAD_DIM), :])
    w = jnp.concatenate(rows, axis=0)
    for n, parts in enumerate((tops, bottoms)):
        x = jnp.concatenate(parts, axis=1)
        out[n * half : (n + 1) * half, :] = jnp.dot(
            x, w, preferred_element_type=jnp.float32
        ).astype(out.dtype)


def solution(mesh):
    ctx, groups = mesh.shape["ctx"], mesh.shape["head"]

    def body(tokens, w_query, w_key, w_value, w_out, block_mask, block_order):
        rows = tokens.shape[0]
        heads = w_query.shape[1] // HEAD_DIM
        inner = ctx // heads
        per = rows // BLOCK
        nb = block_mask.shape[0]
        nq = heads * per
        cols = w_out.shape[1] // groups
        bf = jnp.bfloat16
        params = pltpu.CompilerParams(vmem_limit_bytes=GRANT)
        both = ("ctx", "head")
        places = [(c // inner, c % inner, h) for c in range(ctx) for h in range(groups)]

        def index(a, b, h):
            return (a * inner + b) * groups + h

        def turn(x, j):
            pairs = [
                (index(a, b, h), index(a ^ j, (b & ~1) | (h & 1), (h & ~1) | (b & 1)))
                for a, b, h in places
            ]
            return lax.ppermute(x, both, pairs)

        def spread(x, e):
            pairs = [
                (index(a, b, h), index(a, b ^ (e & ~1), h ^ (e & 1))) for a, b, h in places
            ]
            return lax.ppermute(x, both, pairs) if e else x

        def head_swap(x, j):
            return lax.ppermute(x, "head", [(h, h ^ j) for h in range(groups)]) if j else x

        half, size = rows // 2, rows + rows // 2
        near = heads // 2
        sizes = [size] * near + [rows] * (heads - near) + [half] * (heads - near)
        msgs = pl.pallas_call(
            functools.partial(proj_kernel, inner, heads, near),
            out_shape=[jax.ShapeDtypeStruct((n, LANES), bf) for n in sizes],
            in_specs=[HBM] * 4,
            out_specs=[VMEM] * len(sizes),
            scratch_shapes=[pltpu.VMEM(x.shape, bf) for x in (tokens, w_value, w_key, w_query)]
            + [
                pltpu.VMEM((heads, size, LANES), bf),
                pltpu.SemaphoreType.DMA((4,)),
            ],
            compiler_params=pltpu.CompilerParams(vmem_limit_bytes=WHOLE),
            name="proj",
        )(tokens, w_key, w_value, w_query)
        got, late = [None] * heads, [None] * heads
        for j in reversed(range(heads)):
            got[j] = turn(msgs[j], j)
        for j in range(near, heads):
            late[j] = turn(msgs[heads + j - near], j)
        parts = heads // near
        longest = -(-nb // SLOTS)
        cap = -(-nq // parts * longest // STREAMS) + longest + 3
        tables = pl.pallas_call(
            functools.partial(list_kernel, inner, heads, per, cap, parts),
            out_shape=[
                jax.ShapeDtypeStruct((parts * STREAMS * cap,), jnp.int32),
                jax.ShapeDtypeStruct((parts * STREAMS * cap * SLOTS,), jnp.int32),
                jax.ShapeDtypeStruct((parts * STREAMS * cap,), jnp.int32),
                jax.ShapeDtypeStruct((parts * STREAMS * cap,), jnp.int32),
                jax.ShapeDtypeStruct((parts,), jnp.int32),
            ],
            in_specs=[SMEM] * 2,
            out_specs=[SMEM] * 5,
            scratch_shapes=[pltpu.SMEM((nb,), jnp.int32), pltpu.SMEM((STREAMS,), jnp.int32)],
            name="block_lists",
        )(block_mask, block_order)
        h = lax.axis_index("head")
        w_out, msgs = lax.optimization_barrier((w_out, msgs))
        w_cols = []
        for j in range(groups):
            part = lax.dynamic_slice_in_dim(w_out, (h ^ j) * cols, cols, axis=1)
            w_cols.append(head_swap(part, j))
        got[0], tables, w_cols = lax.optimization_barrier((got[0], tables, w_cols))
        kv = [spread(got[j], e) for j in range(heads) for e in range(inner)]
        o = []
        for part in range(parts):
            if part == 0:
                queries, spans = got[:near], (rows,) * near
                extra = [
                    jax.ShapeDtypeStruct((nb // 2, BLOCK, LANES), bf),
                    jax.ShapeDtypeStruct((nb, HEAD_DIM, BLOCK), bf),
                ]
            else:
                queries, spans, extra = late[part * near : (part + 1) * near], (0,) * near, []
            mini = near * per + 1
            made = pl.pallas_call(
                functools.partial(attend_kernel, part, per, cap, len(kv), spans),
                out_shape=[jax.ShapeDtypeStruct((half, LANES), bf)] * near + extra,
                in_specs=[SMEM] * 5 + [VMEM] * (len(kv) + near),
                out_specs=[VMEM] * (near + len(extra)),
                scratch_shapes=[
                    pltpu.VMEM((2, mini, LANES, BLOCK), bf),
                    pltpu.VMEM((2, STREAMS, SLOTS, BLOCK, BLOCK), jnp.float32),
                    pltpu.VMEM((2, STREAMS, 1, BLOCK), jnp.float32),
                    pltpu.VMEM((2, STREAMS, 1, BLOCK), jnp.float32),
                    pltpu.VMEM((STREAMS, 8, BLOCK), jnp.float32),
                    pltpu.VMEM((STREAMS, HEAD_DIM, BLOCK), jnp.float32),
                    pltpu.VMEM((mini, 8, BLOCK), jnp.float32),
                    pltpu.VMEM((mini, HEAD_DIM, BLOCK), jnp.float32),
                ],
                compiler_params=params,
            )(*tables, *kv, *queries)
            o += made[:near]
            if part == 0:
                kv = made[near:]
        mine = [None] * heads
        for j in reversed(range(heads)):
            mine[j] = turn(o[j], j)
        parts = [mine]
        for g in range(1, groups):
            part = []
            for j in range(heads):
                if g % 2:
                    part.append(head_swap(parts[g - 1][j], 1))
                else:
                    part.append(head_swap(mine[j], g))
            parts.append(part)
        return pl.pallas_call(
            functools.partial(out_kernel, inner, heads, groups),
            out_shape=jax.ShapeDtypeStruct((rows, cols), bf),
            in_specs=[VMEM] * (groups * heads + groups),
            out_specs=VMEM,
            compiler_params=params,
            name="out_proj",
        )(*[x for part in parts for x in part], *w_cols)

    placed = (
        P("ctx", None),
        P(None, "head"),
        P(None, "head"),
        P(None, "head"),
        P("head", None),
        P(),
        P(),
    )
    return jax.shard_map(
        body, mesh=mesh, in_specs=placed, out_specs=P("ctx", "head"), check_vma=False
    )
```

```python
import functools

import jax
import jax.numpy as jnp
from jax import lax
from jax.experimental import pallas as pl
from jax.experimental.pallas import tpu as pltpu
from jax.sharding import PartitionSpec as P


HEAD_DIM = 64
BLOCK = 128
LANES = 128
SLOTS = 4
STREAMS = 4
NEG = -1e30


HBM = pl.BlockSpec(memory_space=pltpu.HBM)
VMEM = pl.BlockSpec(memory_space=pltpu.VMEM)
SMEM = pl.BlockSpec(memory_space=pltpu.SMEM)
GRANT = 16 * 1024 * 1024
WHOLE = 60 * 1024 * 1024


def low_half(shape):
    return lax.broadcasted_iota(jnp.int32, shape, len(shape) - 1) < HEAD_DIM


def swap_halves(x):
    return pltpu.roll(x, HEAD_DIM, 1)


def proj_kernel(inner, heads, near, tok_in, wk_in, wv_in, wq_in, *rest):
    n_out = 2 * heads - near
    outs, (tok, wk, wv, wq, msg, sems) = rest[:n_out], rest[n_out:]
    loads = [
        pltpu.make_async_copy(src, dst, sems.at[n])
        for n, (src, dst) in enumerate(((tok_in, tok), (wv_in, wv), (wk_in, wk), (wq_in, wq)))
    ]
    for load in loads:
        load.start()
    a = lax.axis_index("ctx") // inner
    rows = tok.shape[0]
    half = rows // 2
    low = low_half((half, LANES))
    loads[0].wait()
    loads[1].wait()
    v = jnp.dot(tok[...], wv[...], preferred_element_type=jnp.float32)
    loads[2].wait()
    loads[3].wait()
    q = jnp.dot(tok[...], wq[...], preferred_element_type=jnp.float32) * HEAD_DIM ** (-0.5)
    k = jnp.dot(tok[...], wk[...], preferred_element_type=jnp.float32)
    for base, x in ((half, v), (rows, q)):
        for g in range(heads // 2):
            for i in range(rows // BLOCK):
                block = x[i * BLOCK : (i + 1) * BLOCK, g * LANES : (g + 1) * LANES]
                turned = jnp.transpose(block).astype(jnp.bfloat16)
                start = base + i * HEAD_DIM
                msg[2 * g, start : start + HEAD_DIM] = turned[:HEAD_DIM]
                msg[2 * g + 1, start : start + HEAD_DIM] = turned[HEAD_DIM:]
    for h in range(heads):
        cols = slice(LANES * (h // 2), LANES * (h // 2) + LANES)
        top, bottom = k[:half, cols], k[half:, cols]
        if h % 2 == 0:
            bottom = swap_halves(bottom)
        else:
            top = swap_halves(top)
        msg[h, :half] = jnp.where(low, top, bottom).astype(jnp.bfloat16)
    for j in range(heads):
        if j < near:
            outs[j][...] = msg[a ^ j]
        else:
            outs[j][...] = msg[a ^ j, :rows]
            outs[heads + j - near][...] = msg[a ^ j, rows:]


def list_kernel(inner, outer, per, cap, parts, mask, order, who, where, which, valid, first, steps, names, ends, load):
    c = lax.axis_index("ctx")
    a = c // inner
    b = (c % inner) // 2 * 2 + lax.axis_index("head") % 2
    blocks = inner * outer * per
    half = per // 2
    size = outer * per // parts
    span = blocks + SLOTS

    def name(dev, _):
        kb = ((lax.div(dev, inner) ^ a) * inner + (lax.rem(dev, inner) ^ b)) * per
        for i in range(per):
            names[dev * per + i] = order[kb + i // 2 + i % 2 * half]
        return 0

    lax.fori_loop(0, inner * outer, name, 0)

    def piece(k, _):
        qb = ((k ^ a) * inner + b) * per
        own = [order[qb + i] for i in range(per)]

        def col(n, to):
            to = list(to)
            for e in range(8):
                slot = n * 8 + e
                key = names[slot]
                for i in range(per):
                    which[to[i]] = slot
                    to[i] = to[i] + mask[own[i], key]
            return tuple(to)

        begin = [(k * per + i) * span for i in range(per)]
        end = lax.fori_loop(0, blocks // 8, col, tuple(begin))
        for i in range(per):
            keep = which[begin[i]]
            for extra in range(SLOTS):
                which[end[i] + extra] = keep
            ends[k * per + i] = end[i]
        return 0

    lax.fori_loop(0, outer, piece, 0)
    for part in range(parts):
        for s in range(STREAMS):
            load[s] = 0

        def row(qi, _):
            s, least = jnp.int32(0), load[0]
            for other in range(1, STREAMS):
                here = load[other]
                s = jnp.where(here < least, other, s)
                least = jnp.minimum(here, least)
            item = (part * STREAMS + s) * cap + least
            start = qi * span
            count = ends[qi] - start
            items = lax.div(count + (SLOTS - 1), SLOTS)

            def mark(t, left):
                who[item + t] = qi - part * size
                where[item + t] = start + t * SLOTS
                valid[item + t] = left
                first[item + t] = 0
                return left - SLOTS

            lax.fori_loop(0, items, mark, count)
            first[item] = 1
            load[s] = least + items
            return 0

        lax.fori_loop(part * size, (part + 1) * size, row, 0)
        most = load[0]
        for s in range(1, STREAMS):
            most = jnp.maximum(most, load[s])
        steps[part] = most
        for s in range(STREAMS):
            start = (part * STREAMS + s) * cap
            last = start + jnp.maximum(load[s] - 1, 0)
            idle = load[s] == 0
            qi = jnp.where(idle, size, who[last])
            key = jnp.where(idle, 0, where[last])

            def fill(t, _):
                who[start + t] = qi
                where[start + t] = key
                valid[start + t] = 0
                first[start + t] = 0
                return 0

            lax.fori_loop(load[s], most + 2, fill, 0)


def attend_kernel(part, per, cap, n_kv, spans, who, where, which, valid, first, steps, *rest):
    ins, rest = rest[:n_kv], rest[n_kv:]
    q_in, rest = rest[: len(spans)], rest[len(spans) :]
    outs, rest = rest[: len(spans)], rest[len(spans) :]
    if part == 0:
        (kq, vt), rest = rest[:2], rest[2:]
    else:
        kq, vt = ins
    qt, sc, m_s, al_s, l_s, acc_s, l_all, acc_all = rest
    half = per // 2
    nq = len(spans) * per
    zero = jnp.zeros((HEAD_DIM, BLOCK), jnp.bfloat16)
    for k, start in enumerate(spans):
        for i in range(per):
            turned = q_in[k][start + i * HEAD_DIM : start + (i + 1) * HEAD_DIM, :]
            qt[0, k * per + i] = jnp.concatenate([turned, zero], axis=0)
            qt[1, k * per + i] = jnp.concatenate([zero, turned], axis=0)
    qt[:, nq] = jnp.zeros((2, LANES, BLOCK), jnp.bfloat16)
    if part == 0:
        for n, msg in enumerate(ins):
            for r in range(half):
                kq[n * half + r] = msg[r * BLOCK : (r + 1) * BLOCK, :]
            for i in range(per):
                start = half * BLOCK + (i // 2 + i % 2 * half) * HEAD_DIM
                vt[n * per + i] = msg[start : start + HEAD_DIM, :]
    m_s[...] = jnp.full(m_s.shape, NEG, jnp.float32)
    l_s[...] = jnp.zeros(l_s.shape, jnp.float32)
    acc_s[...] = jnp.zeros(acc_s.shape, jnp.float32)

    def keys(s, t):
        start = where[(part * STREAMS + s) * cap + t]
        return [which[start + e] for e in range(SLOTS)]

    def score(t, buf):
        for s in range(STREAMS):
            qi = who[(part * STREAMS + s) * cap + t]
            tiles = []
            for e, slot in enumerate(keys(s, t)):
                tile = jnp.dot(
                    kq[slot >> 1], qt[slot & 1, qi], preferred_element_type=jnp.float32
                )
                sc[buf, s, e] = tile
                tiles.append(tile.reshape(BLOCK // 8, 8, BLOCK))
            top = jnp.max(functools.reduce(jnp.maximum, tiles), axis=0)
            top = jnp.max(top, axis=0, keepdims=True)
            m_old = jnp.where(first[(part * STREAMS + s) * cap + t] == 1, NEG, m_s[1 - buf, s])
            m_new = jnp.maximum(m_old, top)
            al_s[buf, s] = jnp.exp(m_old - m_new)
            m_s[buf, s] = m_new

    def weigh(t, buf):
        for s in range(STREAMS):
            qi = who[(part * STREAMS + s) * cap + t]
            n_valid = valid[(part * STREAMS + s) * cap + t]
            m, alpha = m_s[buf, s], al_s[buf, s]
            acc = acc_s[s] * alpha
            total = l_s[s] * alpha
            ids = keys(s, t)
            for e in range(0, SLOTS, 2):
                probs = []
                for f in (e, e + 1):
                    shut = m + jnp.where(f < n_valid, 0.0, -NEG)
                    p = jnp.exp(sc[buf, s, f] - shut)
                    total = total + jnp.sum(p.reshape(BLOCK // 8, 8, BLOCK), axis=0)
                    probs.append(p.astype(jnp.bfloat16))
                acc = acc + jnp.dot(
                    jnp.concatenate([vt[ids[e]], vt[ids[e + 1]]], axis=1),
                    jnp.concatenate(probs, axis=0),
                    preferred_element_type=jnp.float32,
                )
            acc_s[s] = acc
            l_s[s] = total
            acc_all[qi] = acc
            l_all[qi] = total

    score(0, 0)

    def step(u, _):
        t = 2 * u
        score(t + 1, 1)
        weigh(t, 0)
        score(t + 2, 0)
        weigh(t + 1, 1)
        return 0

    lax.fori_loop(0, lax.div(steps[part] + 1, 2), step, 0)
    for k in range(len(spans)):
        for r in range(half):
            done = []
            for i in (k * per + r, k * per + r + half):
                done.append(acc_all[i] * (1.0 / jnp.sum(l_all[i], axis=0, keepdims=True)))
            outs[k][r * BLOCK : (r + 1) * BLOCK, :] = jnp.transpose(
                jnp.concatenate(done, axis=0)
            ).astype(jnp.bfloat16)


def out_kernel(inner, heads, groups, other, *refs):
    pieces = [refs[g * heads : (g + 1) * heads] for g in range(groups)]
    ws = refs[groups * heads : groups * heads + groups]
    out = refs[-1]
    a = lax.axis_index("ctx") // inner
    side = (lax.axis_index("head") % 2) ^ other
    cols = pl.ds(pl.multiple_of(side * out.shape[1], LANES), out.shape[1])
    half = pieces[0][0].shape[0]
    low = low_half((half, LANES))
    tops, bottoms, rows = [], [], []
    for g in range(groups):
        for k in range(0, heads, 2):
            p0 = pieces[g][k][...].astype(jnp.float32)
            p1 = pieces[g][k + 1][...].astype(jnp.float32)
            tops.append(jnp.where(low, p0, swap_halves(p1)).astype(jnp.bfloat16))
            bottoms.append(jnp.where(low, swap_halves(p0), p1).astype(jnp.bfloat16))
            for e in (0, 1):
                start = pl.multiple_of(HEAD_DIM * (a ^ (k + e)), HEAD_DIM)
                rows.append(ws[g][pl.ds(start, HEAD_DIM), cols])
    w = jnp.concatenate(rows, axis=0)
    for n, parts in enumerate((tops, bottoms)):
        x = jnp.concatenate(parts, axis=1)
        out[n * half : (n + 1) * half, :] = jnp.dot(
            x, w, preferred_element_type=jnp.float32
        ).astype(out.dtype)


def solution(mesh):
    ctx, groups = mesh.shape["ctx"], mesh.shape["head"]

    def body(tokens, w_query, w_key, w_value, w_out, block_mask, block_order):
        rows = tokens.shape[0]
        heads = w_query.shape[1] // HEAD_DIM
        inner = ctx // heads
        per = rows // BLOCK
        nb = block_mask.shape[0]
        nq = heads * per
        cols = w_out.shape[1] // groups
        bf = jnp.bfloat16
        params = pltpu.CompilerParams(vmem_limit_bytes=GRANT)
        both = ("ctx", "head")
        places = [(c // inner, c % inner, h) for c in range(ctx) for h in range(groups)]

        def index(a, b, h):
            return (a * inner + b) * groups + h

        def turn(x, j):
            pairs = [
                (index(a, b, h), index(a ^ j, (b & ~1) | (h & 1), (h & ~1) | (b & 1)))
                for a, b, h in places
            ]
            return lax.ppermute(x, both, pairs)

        def spread(x, e):
            pairs = [
                (index(a, b, h), index(a, b ^ (e & ~1), h ^ (e & 1))) for a, b, h in places
            ]
            return lax.ppermute(x, both, pairs) if e else x

        def head_swap(x, j):
            return lax.ppermute(x, "head", [(h, h ^ j) for h in range(groups)]) if j else x

        half, size = rows // 2, rows + rows // 2
        near = heads // 2
        sizes = [size] * near + [rows] * (heads - near) + [half] * (heads - near)
        msgs = pl.pallas_call(
            functools.partial(proj_kernel, inner, heads, near),
            out_shape=[jax.ShapeDtypeStruct((n, LANES), bf) for n in sizes],
            in_specs=[HBM] * 4,
            out_specs=[VMEM] * len(sizes),
            scratch_shapes=[pltpu.VMEM(x.shape, bf) for x in (tokens, w_value, w_key, w_query)]
            + [
                pltpu.VMEM((heads, size, LANES), bf),
                pltpu.SemaphoreType.DMA((4,)),
            ],
            compiler_params=pltpu.CompilerParams(vmem_limit_bytes=WHOLE),
            name="proj",
        )(tokens, w_key, w_value, w_query)
        got, late = [None] * heads, [None] * heads
        for j in reversed(range(heads)):
            got[j] = turn(msgs[j], j)
        for j in range(near, heads):
            late[j] = turn(msgs[heads + j - near], j)
        parts = heads // near
        longest = -(-nb // SLOTS)
        cap = -(-nq // parts * longest // STREAMS) + longest + 3
        tables = pl.pallas_call(
            functools.partial(list_kernel, inner, heads, per, cap, parts),
            out_shape=[
                jax.ShapeDtypeStruct((parts * STREAMS * cap,), jnp.int32),
                jax.ShapeDtypeStruct((parts * STREAMS * cap,), jnp.int32),
                jax.ShapeDtypeStruct((nq * (nb + SLOTS),), jnp.int32),
                jax.ShapeDtypeStruct((parts * STREAMS * cap,), jnp.int32),
                jax.ShapeDtypeStruct((parts * STREAMS * cap,), jnp.int32),
                jax.ShapeDtypeStruct((parts,), jnp.int32),
            ],
            in_specs=[SMEM] * 2,
            out_specs=[SMEM] * 6,
            scratch_shapes=[
                pltpu.SMEM((nb,), jnp.int32),
                pltpu.SMEM((nq,), jnp.int32),
                pltpu.SMEM((STREAMS,), jnp.int32),
            ],
            name="block_lists",
        )(block_mask, block_order)
        h = lax.axis_index("head")
        w_out, msgs = lax.optimization_barrier((w_out, msgs))
        w_cols = []
        for g in range(0, groups, 2):
            part = lax.dynamic_slice_in_dim(w_out, (h // 2 ^ g // 2) * 2 * cols, 2 * cols, axis=1)
            w_cols.append(head_swap(part, g))
        got[0], tables, w_cols = lax.optimization_barrier((got[0], tables, w_cols))
        kv = [spread(got[j], e) for j in range(heads) for e in range(inner)]
        o = []
        for part in range(parts):
            if part == 0:
                queries, spans = got[:near], (rows,) * near
                extra = [
                    jax.ShapeDtypeStruct((nb // 2, BLOCK, LANES), bf),
                    jax.ShapeDtypeStruct((nb, HEAD_DIM, BLOCK), bf),
                ]
            else:
                queries, spans, extra = late[part * near : (part + 1) * near], (0,) * near, []
            mini = near * per + 1
            made = pl.pallas_call(
                functools.partial(attend_kernel, part, per, cap, len(kv), spans),
                out_shape=[jax.ShapeDtypeStruct((half, LANES), bf)] * near + extra,
                in_specs=[SMEM] * 6 + [VMEM] * (len(kv) + near),
                out_specs=[VMEM] * (near + len(extra)),
                scratch_shapes=[
                    pltpu.VMEM((2, mini, LANES, BLOCK), bf),
                    pltpu.VMEM((2, STREAMS, SLOTS, BLOCK, BLOCK), jnp.float32),
                    pltpu.VMEM((2, STREAMS, 1, BLOCK), jnp.float32),
                    pltpu.VMEM((2, STREAMS, 1, BLOCK), jnp.float32),
                    pltpu.VMEM((STREAMS, 8, BLOCK), jnp.float32),
                    pltpu.VMEM((STREAMS, HEAD_DIM, BLOCK), jnp.float32),
                    pltpu.VMEM((mini, 8, BLOCK), jnp.float32),
                    pltpu.VMEM((mini, HEAD_DIM, BLOCK), jnp.float32),
                ],
                compiler_params=params,
            )(*tables, *kv, *queries)
            o += made[:near]
            if part == 0:
                kv = made[near:]
        mine = [None] * heads
        for j in reversed(range(heads)):
            mine[j] = turn(o[j], j)
        pieces = []
        for g in range(0, groups, 2):
            for j in range(heads):
                pieces.append(head_swap(mine[j], g))

        def out(other, dtype):
            return pl.pallas_call(
                functools.partial(out_kernel, inner, heads, groups // 2, other),
                out_shape=jax.ShapeDtypeStruct((rows, cols), dtype),
                in_specs=[VMEM] * (len(pieces) + len(w_cols)),
                out_specs=VMEM,
                compiler_params=params,
                cost_estimate=pl.CostEstimate(
                    flops=rows * cols * w_out.shape[0] * 4, bytes_accessed=0, transcendentals=0
                ),
            )(*pieces, *w_cols)

        theirs = head_swap(out(1, bf), 1)
        return (out(0, jnp.float32) + theirs.astype(jnp.float32)).astype(bf)

    placed = (
        P("ctx", None),
        P(None, "head"),
        P(None, "head"),
        P(None, "head"),
        P("head", None),
        P(),
        P(),
    )
    return jax.shard_map(
        body, mesh=mesh, in_specs=placed, out_specs=P("ctx", "head"), check_vma=False
    )
```

```python
import functools

import jax
import jax.numpy as jnp
from jax import lax
from jax.experimental import pallas as pl
from jax.experimental.pallas import tpu as pltpu
from jax.sharding import PartitionSpec as P


HEAD_DIM = 64
BLOCK = 128
LANES = 128
SLOTS = 4
STREAMS = 4
NEG = -1e30


HBM = pl.BlockSpec(memory_space=pltpu.HBM)
VMEM = pl.BlockSpec(memory_space=pltpu.VMEM)
SMEM = pl.BlockSpec(memory_space=pltpu.SMEM)
GRANT = 16 * 1024 * 1024
WHOLE = 60 * 1024 * 1024


def low_half(shape):
    return lax.broadcasted_iota(jnp.int32, shape, len(shape) - 1) < HEAD_DIM


def swap_halves(x):
    return pltpu.roll(x, HEAD_DIM, 1)


def proj_kernel(inner, heads, near, tok_in, wk_in, wv_in, wq_in, *rest):
    n_out = 2 * heads - near
    outs, (tok, wk, wv, wq, msg, sems) = rest[:n_out], rest[n_out:]
    loads = [
        pltpu.make_async_copy(src, dst, sems.at[n])
        for n, (src, dst) in enumerate(((tok_in, tok), (wv_in, wv), (wk_in, wk), (wq_in, wq)))
    ]
    for load in loads:
        load.start()
    a = lax.axis_index("ctx") // inner
    rows = tok.shape[0]
    half = rows // 2
    low = low_half((half, LANES))
    loads[0].wait()
    loads[1].wait()
    v = jnp.dot(tok[...], wv[...], preferred_element_type=jnp.float32)
    loads[2].wait()
    loads[3].wait()
    q = jnp.dot(tok[...], wq[...], preferred_element_type=jnp.float32) * HEAD_DIM ** (-0.5)
    k = jnp.dot(tok[...], wk[...], preferred_element_type=jnp.float32)
    for base, x in ((half, v), (rows, q)):
        for g in range(heads // 2):
            for i in range(rows // BLOCK):
                block = x[i * BLOCK : (i + 1) * BLOCK, g * LANES : (g + 1) * LANES]
                turned = jnp.transpose(block).astype(jnp.bfloat16)
                start = base + i * HEAD_DIM
                msg[2 * g, start : start + HEAD_DIM] = turned[:HEAD_DIM]
                msg[2 * g + 1, start : start + HEAD_DIM] = turned[HEAD_DIM:]
    for h in range(heads):
        cols = slice(LANES * (h // 2), LANES * (h // 2) + LANES)
        top, bottom = k[:half, cols], k[half:, cols]
        if h % 2 == 0:
            bottom = swap_halves(bottom)
        else:
            top = swap_halves(top)
        msg[h, :half] = jnp.where(low, top, bottom).astype(jnp.bfloat16)
    for j in range(heads):
        if j < near:
            outs[j][...] = msg[a ^ j]
        else:
            outs[j][...] = msg[a ^ j, :rows]
            outs[heads + j - near][...] = msg[a ^ j, rows:]


def list_kernel(inner, outer, per, cap, parts, mask, order, who, where, which, valid, first, steps, names, ends, load):
    c = lax.axis_index("ctx")
    a = c // inner
    b = (c % inner) // 2 * 2 + lax.axis_index("head") % 2
    blocks = inner * outer * per
    half = per // 2
    size = outer * per // parts
    span = blocks + SLOTS

    def name(dev, _):
        kb = ((lax.div(dev, inner) ^ a) * inner + (lax.rem(dev, inner) ^ b)) * per
        for i in range(per):
            names[dev * per + i] = order[kb + i // 2 + i % 2 * half]
        return 0

    lax.fori_loop(0, inner * outer, name, 0)

    def piece(k, _):
        qb = ((k ^ a) * inner + b) * per
        own = [order[qb + i] for i in range(per)]

        def col(n, to):
            to = list(to)
            for e in range(8):
                slot = n * 8 + e
                key = names[slot]
                for i in range(per):
                    which[to[i]] = slot
                    to[i] = to[i] + mask[own[i], key]
            return tuple(to)

        begin = [(k * per + i) * span for i in range(per)]
        end = lax.fori_loop(0, blocks // 8, col, tuple(begin))
        for i in range(per):
            keep = which[begin[i]]
            for extra in range(SLOTS):
                which[end[i] + extra] = keep
            ends[k * per + i] = end[i]
        return 0

    lax.fori_loop(0, outer, piece, 0)
    for part in range(parts):
        for s in range(STREAMS):
            load[s] = 0

        def row(qi, _):
            s, least = jnp.int32(0), load[0]
            for other in range(1, STREAMS):
                here = load[other]
                s = jnp.where(here < least, other, s)
                least = jnp.minimum(here, least)
            item = (part * STREAMS + s) * cap + least
            start = qi * span
            count = ends[qi] - start
            items = lax.div(count + (SLOTS - 1), SLOTS)

            def mark(t, left):
                who[item + t] = qi - part * size
                where[item + t] = start + t * SLOTS
                valid[item + t] = left
                first[item + t] = 0
                return left - SLOTS

            lax.fori_loop(0, items, mark, count)
            first[item] = 1
            load[s] = least + items
            return 0

        lax.fori_loop(part * size, (part + 1) * size, row, 0)
        most = load[0]
        for s in range(1, STREAMS):
            most = jnp.maximum(most, load[s])
        steps[part] = most
        for s in range(STREAMS):
            start = (part * STREAMS + s) * cap
            last = start + jnp.maximum(load[s] - 1, 0)
            idle = load[s] == 0
            qi = jnp.where(idle, size, who[last])
            key = jnp.where(idle, 0, where[last])

            def fill(t, _):
                who[start + t] = qi
                where[start + t] = key
                valid[start + t] = 0
                first[start + t] = 0
                return 0

            lax.fori_loop(load[s], most + 2, fill, 0)


def attend_kernel(part, per, cap, n_kv, spans, who, where, which, valid, first, steps, *rest):
    ins, rest = rest[:n_kv], rest[n_kv:]
    q_in, rest = rest[: len(spans)], rest[len(spans) :]
    outs, rest = rest[: len(spans)], rest[len(spans) :]
    if part == 0:
        (kq, vt), rest = rest[:2], rest[2:]
    else:
        kq, vt = ins
    qt, sc, m_s, al_s, l_s, acc_s, l_all, acc_all = rest
    half = per // 2
    nq = len(spans) * per
    zero = jnp.zeros((HEAD_DIM, BLOCK), jnp.bfloat16)
    for k, start in enumerate(spans):
        for i in range(per):
            turned = q_in[k][start + i * HEAD_DIM : start + (i + 1) * HEAD_DIM, :]
            qt[0, k * per + i] = jnp.concatenate([turned, zero], axis=0)
            qt[1, k * per + i] = jnp.concatenate([zero, turned], axis=0)
    qt[:, nq] = jnp.zeros((2, LANES, BLOCK), jnp.bfloat16)
    if part == 0:
        for n, msg in enumerate(ins):
            for r in range(half):
                kq[n * half + r] = msg[r * BLOCK : (r + 1) * BLOCK, :]
            for i in range(per):
                start = half * BLOCK + (i // 2 + i % 2 * half) * HEAD_DIM
                vt[n * per + i] = msg[start : start + HEAD_DIM, :]
    m_s[...] = jnp.full(m_s.shape, NEG, jnp.float32)
    l_s[...] = jnp.zeros(l_s.shape, jnp.float32)
    acc_s[...] = jnp.zeros(acc_s.shape, jnp.float32)

    def keys(s, t):
        start = where[(part * STREAMS + s) * cap + t]
        return [which[start + e] for e in range(SLOTS)]

    def score(t, buf):
        for s in range(STREAMS):
            qi = who[(part * STREAMS + s) * cap + t]
            tiles = []
            for e, slot in enumerate(keys(s, t)):
                tile = jnp.dot(
                    kq[slot >> 1], qt[slot & 1, qi], preferred_element_type=jnp.float32
                )
                sc[buf, s, e] = tile
                tiles.append(tile.reshape(BLOCK // 8, 8, BLOCK))
            top = jnp.max(functools.reduce(jnp.maximum, tiles), axis=0)
            top = jnp.max(top, axis=0, keepdims=True)
            m_old = jnp.where(first[(part * STREAMS + s) * cap + t] == 1, NEG, m_s[1 - buf, s])
            m_new = jnp.maximum(m_old, top)
            al_s[buf, s] = jnp.exp(m_old - m_new)
            m_s[buf, s] = m_new

    def weigh(t, buf):
        for s in range(STREAMS):
            qi = who[(part * STREAMS + s) * cap + t]
            n_valid = valid[(part * STREAMS + s) * cap + t]
            m, alpha = m_s[buf, s], al_s[buf, s]
            acc = acc_s[s] * alpha
            total = l_s[s] * alpha
            ids = keys(s, t)
            for e in range(0, SLOTS, 2):
                probs = []
                for f in (e, e + 1):
                    shut = m + jnp.where(f < n_valid, 0.0, -NEG)
                    p = jnp.exp(sc[buf, s, f] - shut)
                    total = total + jnp.sum(p.reshape(BLOCK // 8, 8, BLOCK), axis=0)
                    probs.append(p.astype(jnp.bfloat16))
                acc = acc + jnp.dot(
                    jnp.concatenate([vt[ids[e]], vt[ids[e + 1]]], axis=1),
                    jnp.concatenate(probs, axis=0),
                    preferred_element_type=jnp.float32,
                )
            acc_s[s] = acc
            l_s[s] = total
            acc_all[qi] = acc
            l_all[qi] = total

    score(0, 0)
    count = steps[part]

    def step(u, _):
        t = 2 * u
        score(t + 1, 1)
        weigh(t, 0)
        score(t + 2, 0)
        weigh(t + 1, 1)
        return 0

    lax.fori_loop(0, lax.div(count, 2), step, 0)

    @pl.when(lax.rem(count, 2) == 1)
    def _():
        weigh(count - 1, 0)

    for k in range(len(spans)):
        for r in range(half):
            done = []
            for i in (k * per + r, k * per + r + half):
                done.append(acc_all[i] * (1.0 / jnp.sum(l_all[i], axis=0, keepdims=True)))
            outs[k][r * BLOCK : (r + 1) * BLOCK, :] = jnp.transpose(
                jnp.concatenate(done, axis=0)
            ).astype(jnp.bfloat16)


def out_kernel(inner, heads, groups, other, *refs):
    pieces = [refs[g * heads : (g + 1) * heads] for g in range(groups)]
    ws = refs[groups * heads : groups * heads + groups]
    out = refs[-1]
    a = lax.axis_index("ctx") // inner
    side = (lax.axis_index("head") % 2) ^ other
    cols = pl.ds(pl.multiple_of(side * out.shape[1], LANES), out.shape[1])
    half = pieces[0][0].shape[0]
    low = low_half((half, LANES))
    tops, bottoms, rows = [], [], []
    for g in range(groups):
        for k in range(0, heads, 2):
            p0 = pieces[g][k][...].astype(jnp.float32)
            p1 = pieces[g][k + 1][...].astype(jnp.float32)
            tops.append(jnp.where(low, p0, swap_halves(p1)).astype(jnp.bfloat16))
            bottoms.append(jnp.where(low, swap_halves(p0), p1).astype(jnp.bfloat16))
            for e in (0, 1):
                start = pl.multiple_of(HEAD_DIM * (a ^ (k + e)), HEAD_DIM)
                rows.append(ws[g][pl.ds(start, HEAD_DIM), cols])
    w = jnp.concatenate(rows, axis=0)
    for n, parts in enumerate((tops, bottoms)):
        x = jnp.concatenate(parts, axis=1)
        total = jnp.dot(x, w, preferred_element_type=jnp.float32)
        if not other:
            total = total + refs[-2][n * half : (n + 1) * half, :].astype(jnp.float32)
        out[n * half : (n + 1) * half, :] = total.astype(out.dtype)


def solution(mesh):
    ctx, groups = mesh.shape["ctx"], mesh.shape["head"]

    def body(tokens, w_query, w_key, w_value, w_out, block_mask, block_order):
        rows = tokens.shape[0]
        heads = w_query.shape[1] // HEAD_DIM
        inner = ctx // heads
        per = rows // BLOCK
        nb = block_mask.shape[0]
        nq = heads * per
        cols = w_out.shape[1] // groups
        bf = jnp.bfloat16
        params = pltpu.CompilerParams(vmem_limit_bytes=GRANT)
        both = ("ctx", "head")
        places = [(c // inner, c % inner, h) for c in range(ctx) for h in range(groups)]

        def index(a, b, h):
            return (a * inner + b) * groups + h

        def turn(x, j):
            pairs = [
                (index(a, b, h), index(a ^ j, (b & ~1) | (h & 1), (h & ~1) | (b & 1)))
                for a, b, h in places
            ]
            return lax.ppermute(x, both, pairs)

        def spread(x, e):
            pairs = [
                (index(a, b, h), index(a, b ^ (e & ~1), h ^ (e & 1))) for a, b, h in places
            ]
            return lax.ppermute(x, both, pairs) if e else x

        def head_swap(x, j):
            return lax.ppermute(x, "head", [(h, h ^ j) for h in range(groups)]) if j else x

        half, size = rows // 2, rows + rows // 2
        near = heads // 2
        sizes = [size] * near + [rows] * (heads - near) + [half] * (heads - near)
        msgs = pl.pallas_call(
            functools.partial(proj_kernel, inner, heads, near),
            out_shape=[jax.ShapeDtypeStruct((n, LANES), bf) for n in sizes],
            in_specs=[HBM] * 4,
            out_specs=[VMEM] * len(sizes),
            scratch_shapes=[pltpu.VMEM(x.shape, bf) for x in (tokens, w_value, w_key, w_query)]
            + [
                pltpu.VMEM((heads, size, LANES), bf),
                pltpu.SemaphoreType.DMA((4,)),
            ],
            compiler_params=pltpu.CompilerParams(vmem_limit_bytes=WHOLE),
            name="proj",
        )(tokens, w_key, w_value, w_query)
        got, late = [None] * heads, [None] * heads
        for j in reversed(range(heads)):
            got[j] = turn(msgs[j], j)
        parts = heads // near
        longest = -(-nb // SLOTS)
        cap = -(-nq // parts * longest // STREAMS) + longest + 3
        tables = pl.pallas_call(
            functools.partial(list_kernel, inner, heads, per, cap, parts),
            out_shape=[
                jax.ShapeDtypeStruct((parts * STREAMS * cap,), jnp.int32),
                jax.ShapeDtypeStruct((parts * STREAMS * cap,), jnp.int32),
                jax.ShapeDtypeStruct((nq * (nb + SLOTS),), jnp.int32),
                jax.ShapeDtypeStruct((parts * STREAMS * cap,), jnp.int32),
                jax.ShapeDtypeStruct((parts * STREAMS * cap,), jnp.int32),
                jax.ShapeDtypeStruct((parts,), jnp.int32),
            ],
            in_specs=[SMEM] * 2,
            out_specs=[SMEM] * 6,
            scratch_shapes=[
                pltpu.SMEM((nb,), jnp.int32),
                pltpu.SMEM((nq,), jnp.int32),
                pltpu.SMEM((STREAMS,), jnp.int32),
            ],
            name="block_lists",
        )(block_mask, block_order)
        queries = list(msgs[heads:])
        queries, got[0], tables = lax.optimization_barrier((queries, got[0], tables))
        for j in range(near, heads):
            late[j] = turn(queries[j - near], j)
        kv = []
        for j in range(heads):
            for e in range(inner):
                kv.append(spread(got[j], e))
        o = []
        for part in range(parts):
            if part == 0:
                queries, spans = got[:near], (rows,) * near
                extra = [
                    jax.ShapeDtypeStruct((nb // 2, BLOCK, LANES), bf),
                    jax.ShapeDtypeStruct((nb, HEAD_DIM, BLOCK), bf),
                ]
            else:
                queries, spans, extra = late[part * near : (part + 1) * near], (0,) * near, []
            mini = near * per + 1
            made = pl.pallas_call(
                functools.partial(attend_kernel, part, per, cap, len(kv), spans),
                out_shape=[jax.ShapeDtypeStruct((half, LANES), bf)] * near + extra,
                in_specs=[SMEM] * 6 + [VMEM] * (len(kv) + near),
                out_specs=[VMEM] * (near + len(extra)),
                scratch_shapes=[
                    pltpu.VMEM((2, mini, LANES, BLOCK), bf),
                    pltpu.VMEM((2, STREAMS, SLOTS, BLOCK, BLOCK), jnp.float32),
                    pltpu.VMEM((2, STREAMS, 1, BLOCK), jnp.float32),
                    pltpu.VMEM((2, STREAMS, 1, BLOCK), jnp.float32),
                    pltpu.VMEM((STREAMS, 8, BLOCK), jnp.float32),
                    pltpu.VMEM((STREAMS, HEAD_DIM, BLOCK), jnp.float32),
                    pltpu.VMEM((mini, 8, BLOCK), jnp.float32),
                    pltpu.VMEM((mini, HEAD_DIM, BLOCK), jnp.float32),
                ],
                compiler_params=params,
            )(*tables, *kv, *queries)
            o += made[:near]
            if part == 0:
                h = lax.axis_index("head")
                w_out, kv = lax.optimization_barrier((w_out, made[near:]))
                w_cols = []
                for g in range(0, groups, 2):
                    start = (h // 2 ^ g // 2) * 2 * cols
                    share = lax.dynamic_slice_in_dim(w_out, start, 2 * cols, axis=1)
                    w_cols.append(head_swap(share, g))
        mine = [None] * heads
        for j in reversed(range(heads)):
            mine[j] = turn(o[j], j)
        pieces = []
        for g in range(0, groups, 2):
            for j in range(heads):
                pieces.append(head_swap(mine[j], g))

        def out(other, *more):
            return pl.pallas_call(
                functools.partial(out_kernel, inner, heads, groups // 2, other),
                out_shape=jax.ShapeDtypeStruct((rows, cols), bf),
                in_specs=[VMEM] * (len(pieces) + len(w_cols) + len(more)),
                out_specs=VMEM,
                compiler_params=params,
            )(*pieces, *w_cols, *more)

        return out(0, head_swap(out(1), 1))

    placed = (
        P("ctx", None),
        P(None, "head"),
        P(None, "head"),
        P(None, "head"),
        P("head", None),
        P(),
        P(),
    )
    return jax.shard_map(
        body, mesh=mesh, in_specs=placed, out_specs=P("ctx", "head"), check_vma=False
    )
```

```python
import functools

import jax
import jax.numpy as jnp
from jax import lax
from jax.experimental import pallas as pl
from jax.experimental.pallas import tpu as pltpu
from jax.sharding import PartitionSpec as P


HEAD_DIM = 64
BLOCK = 128
LANES = 128
SLOTS = 4
STREAMS = 4
NEG = -1e30


HBM = pl.BlockSpec(memory_space=pltpu.HBM)
VMEM = pl.BlockSpec(memory_space=pltpu.VMEM)
SMEM = pl.BlockSpec(memory_space=pltpu.SMEM)
GRANT = 16 * 1024 * 1024
WHOLE = 60 * 1024 * 1024


def low_half(shape):
    return lax.broadcasted_iota(jnp.int32, shape, len(shape) - 1) < HEAD_DIM


def swap_halves(x):
    return pltpu.roll(x, HEAD_DIM, 1)


def proj_kernel(inner, far, tok_in, wk_in, wv_in, wq_in, out0, out1, tok, w, msg, sems):
    a = lax.axis_index("ctx") // inner
    group = (a // 2) ^ far
    cols = pl.ds(pl.multiple_of(group * LANES, LANES), LANES)
    loads = [pltpu.make_async_copy(tok_in, tok, sems.at[0])] + [
        pltpu.make_async_copy(src.at[:, cols], w.at[:, pl.ds(n * LANES, LANES)], sems.at[n + 1])
        for n, src in enumerate((wv_in, wq_in, wk_in))
    ]
    for load in loads:
        load.start()
    rows = tok.shape[0]
    half = rows // 2
    low = low_half((half, LANES))
    for load in loads:
        load.wait()
    vqk = jnp.dot(tok[...], w[...], preferred_element_type=jnp.float32)
    v, q, k = (vqk[:, n * LANES : (n + 1) * LANES] for n in range(3))
    q = q * HEAD_DIM ** (-0.5)
    for base, x in ((half, v), (rows, q)):
        for i in range(rows // BLOCK):
            turned = jnp.transpose(x[i * BLOCK : (i + 1) * BLOCK]).astype(jnp.bfloat16)
            start = base + i * HEAD_DIM
            msg[0, start : start + HEAD_DIM] = turned[:HEAD_DIM]
            msg[1, start : start + HEAD_DIM] = turned[HEAD_DIM:]
    top, bottom = k[:half], k[half:]
    msg[0, :half] = jnp.where(low, top, swap_halves(bottom)).astype(jnp.bfloat16)
    msg[1, :half] = jnp.where(low, swap_halves(top), bottom).astype(jnp.bfloat16)
    odd = lax.rem(a, 2)
    out0[...] = msg[odd]
    out1[...] = msg[1 - odd]


def list_kernel(inner, outer, per, cap, mask, order, who, where, which, valid, first, steps, names, ends, load):
    c = lax.axis_index("ctx")
    a = c // inner
    b = (c % inner) // 2 * 2 + lax.axis_index("head") % 2
    blocks = inner * outer * per
    half = per // 2
    span = blocks + SLOTS

    def name(dev, _):
        kb = ((lax.div(dev, inner) ^ a) * inner + (lax.rem(dev, inner) ^ b)) * per
        for i in range(per):
            names[dev * per + i] = order[kb + i // 2 + i % 2 * half]
        return 0

    lax.fori_loop(0, inner * outer, name, 0)

    def piece(k, _):
        qb = ((k ^ a) * inner + b) * per
        own = [order[qb + i] for i in range(per)]

        def col(n, to):
            to = list(to)
            for e in range(8):
                slot = n * 8 + e
                key = names[slot]
                for i in range(per):
                    which[to[i]] = slot
                    to[i] = to[i] + mask[own[i], key]
            return tuple(to)

        begin = [(k * per + i) * span for i in range(per)]
        end = lax.fori_loop(0, blocks // 8, col, tuple(begin))
        for i in range(per):
            keep = which[begin[i]]
            for extra in range(SLOTS):
                which[end[i] + extra] = keep
            ends[k * per + i] = end[i]
        return 0

    lax.fori_loop(0, outer, piece, 0)
    for s in range(STREAMS):
        load[s] = 0

    def row(qi, _):
        s, least = jnp.int32(0), load[0]
        for other in range(1, STREAMS):
            here = load[other]
            s = jnp.where(here < least, other, s)
            least = jnp.minimum(here, least)
        item = s * cap + least
        start = qi * span
        count = ends[qi] - start
        items = lax.div(count + (SLOTS - 1), SLOTS)

        def mark(t, left):
            who[item + t] = qi
            where[item + t] = start + t * SLOTS
            valid[item + t] = left
            first[item + t] = 0
            return left - SLOTS

        lax.fori_loop(0, items, mark, count)
        first[item] = 1
        load[s] = least + items
        return 0

    lax.fori_loop(0, outer * per, row, 0)
    most = load[0]
    for s in range(1, STREAMS):
        most = jnp.maximum(most, load[s])
    steps[0] = most
    for s in range(STREAMS):
        start = s * cap
        last = start + jnp.maximum(load[s] - 1, 0)
        idle = load[s] == 0
        qi = jnp.where(idle, outer * per, who[last])
        key = jnp.where(idle, 0, where[last])

        def fill(t, _):
            who[start + t] = qi
            where[start + t] = key
            valid[start + t] = 0
            first[start + t] = 0
            return 0

        lax.fori_loop(load[s], most + 2, fill, 0)


def attend_kernel(per, cap, n_kv, start_q, n_q, who, where, which, valid, first, steps, *rest):
    ins, rest = rest[:n_kv], rest[n_kv:]
    q_in = ins[:: n_kv // n_q]
    outs, rest = rest[:n_q], rest[n_q:]
    kq, vt, qt, sc, m_s, al_s, l_s, acc_s, l_all, acc_all = rest
    half = per // 2
    nq = n_q * per
    zero = jnp.zeros((HEAD_DIM, BLOCK), jnp.bfloat16)
    for k, msg in enumerate(q_in):
        for i in range(per):
            turned = msg[start_q + i * HEAD_DIM : start_q + (i + 1) * HEAD_DIM, :]
            qt[0, k * per + i] = jnp.concatenate([turned, zero], axis=0)
            qt[1, k * per + i] = jnp.concatenate([zero, turned], axis=0)
    qt[:, nq] = jnp.zeros((2, LANES, BLOCK), jnp.bfloat16)
    for n, msg in enumerate(ins):
        for r in range(half):
            kq[n * half + r] = msg[r * BLOCK : (r + 1) * BLOCK, :]
        for i in range(per):
            start = half * BLOCK + (i // 2 + i % 2 * half) * HEAD_DIM
            vt[n * per + i] = msg[start : start + HEAD_DIM, :]
    m_s[...] = jnp.full(m_s.shape, NEG, jnp.float32)
    l_s[...] = jnp.zeros(l_s.shape, jnp.float32)
    acc_s[...] = jnp.zeros(acc_s.shape, jnp.float32)

    def keys(s, t):
        start = where[s * cap + t]
        return [which[start + e] for e in range(SLOTS)]

    def score(t, buf):
        for s in range(STREAMS):
            qi = who[s * cap + t]
            tiles = []
            for e, slot in enumerate(keys(s, t)):
                tile = jnp.dot(
                    kq[slot >> 1], qt[slot & 1, qi], preferred_element_type=jnp.float32
                )
                sc[buf, s, e] = tile
                tiles.append(tile.reshape(BLOCK // 8, 8, BLOCK))
            top = jnp.max(functools.reduce(jnp.maximum, tiles), axis=0)
            top = jnp.max(top, axis=0, keepdims=True)
            m_old = jnp.where(first[s * cap + t] == 1, NEG, m_s[1 - buf, s])
            m_new = jnp.maximum(m_old, top)
            al_s[buf, s] = jnp.exp(m_old - m_new)
            m_s[buf, s] = m_new

    def weigh(t, buf):
        for s in range(STREAMS):
            qi = who[s * cap + t]
            n_valid = valid[s * cap + t]
            m, alpha = m_s[buf, s], al_s[buf, s]
            acc = acc_s[s] * alpha
            total = l_s[s] * alpha
            ids = keys(s, t)
            for e in range(0, SLOTS, 2):
                probs = []
                for f in (e, e + 1):
                    shut = m + jnp.where(f < n_valid, 0.0, -NEG)
                    p = jnp.exp(sc[buf, s, f] - shut)
                    total = total + jnp.sum(p.reshape(BLOCK // 8, 8, BLOCK), axis=0)
                    probs.append(p.astype(jnp.bfloat16))
                acc = acc + jnp.dot(
                    jnp.concatenate([vt[ids[e]], vt[ids[e + 1]]], axis=1),
                    jnp.concatenate(probs, axis=0),
                    preferred_element_type=jnp.float32,
                )
            acc_s[s] = acc
            l_s[s] = total
            acc_all[qi] = acc
            l_all[qi] = total

    score(0, 0)
    count = steps[0]

    def step(u, _):
        t = 2 * u
        score(t + 1, 1)
        weigh(t, 0)
        score(t + 2, 0)
        weigh(t + 1, 1)
        return 0

    lax.fori_loop(0, lax.div(count, 2), step, 0)

    @pl.when(lax.rem(count, 2) == 1)
    def _():
        weigh(count - 1, 0)

    for k in range(n_q):
        for r in range(half):
            done = []
            for i in (k * per + r, k * per + r + half):
                done.append(acc_all[i] * (1.0 / jnp.sum(l_all[i], axis=0, keepdims=True)))
            outs[k][r * BLOCK : (r + 1) * BLOCK, :] = jnp.transpose(
                jnp.concatenate(done, axis=0)
            ).astype(jnp.bfloat16)


def out_kernel(inner, heads, groups, other, *refs):
    pieces = [refs[g * heads : (g + 1) * heads] for g in range(groups)]
    ws = refs[groups * heads : groups * heads + groups]
    out = refs[-1]
    a = lax.axis_index("ctx") // inner
    side = (lax.axis_index("head") % 2) ^ other
    cols = pl.ds(pl.multiple_of(side * out.shape[1], LANES), out.shape[1])
    half = pieces[0][0].shape[0]
    low = low_half((half, LANES))
    tops, bottoms, rows = [], [], []
    for g in range(groups):
        for k in range(0, heads, 2):
            p0 = pieces[g][k][...].astype(jnp.float32)
            p1 = pieces[g][k + 1][...].astype(jnp.float32)
            tops.append(jnp.where(low, p0, swap_halves(p1)).astype(jnp.bfloat16))
            bottoms.append(jnp.where(low, swap_halves(p0), p1).astype(jnp.bfloat16))
            for e in (0, 1):
                start = pl.multiple_of(HEAD_DIM * (a ^ (k + e)), HEAD_DIM)
                rows.append(ws[g][pl.ds(start, HEAD_DIM), cols])
    w = jnp.concatenate(rows, axis=0)
    for n, parts in enumerate((tops, bottoms)):
        x = jnp.concatenate(parts, axis=1)
        total = jnp.dot(x, w, preferred_element_type=jnp.float32)
        if not other:
            total = total + refs[-2][n * half : (n + 1) * half, :].astype(jnp.float32)
        out[n * half : (n + 1) * half, :] = total.astype(out.dtype)


def solution(mesh):
    ctx, groups = mesh.shape["ctx"], mesh.shape["head"]

    def body(tokens, w_query, w_key, w_value, w_out, block_mask, block_order):
        rows = tokens.shape[0]
        heads = w_query.shape[1] // HEAD_DIM
        inner = ctx // heads
        per = rows // BLOCK
        nb = block_mask.shape[0]
        nq = heads * per
        cols = w_out.shape[1] // groups
        bf = jnp.bfloat16
        params = pltpu.CompilerParams(vmem_limit_bytes=GRANT)
        both = ("ctx", "head")
        places = [(c // inner, c % inner, h) for c in range(ctx) for h in range(groups)]

        def index(a, b, h):
            return (a * inner + b) * groups + h

        def turn(x, j):
            pairs = [
                (index(a, b, h), index(a ^ j, (b & ~1) | (h & 1), (h & ~1) | (b & 1)))
                for a, b, h in places
            ]
            return lax.ppermute(x, both, pairs)

        def spread(x, e):
            pairs = [
                (index(a, b, h), index(a, b ^ (e & ~1), h ^ (e & 1))) for a, b, h in places
            ]
            return lax.ppermute(x, both, pairs) if e else x

        def head_swap(x, j):
            return lax.ppermute(x, "head", [(h, h ^ j) for h in range(groups)]) if j else x

        half, size = rows // 2, rows + rows // 2
        msgs = []
        for far in range(heads // 2):
            msgs += pl.pallas_call(
                functools.partial(proj_kernel, inner, far),
                out_shape=[jax.ShapeDtypeStruct((size, LANES), bf)] * 2,
                in_specs=[HBM] * 4,
                out_specs=[VMEM] * 2,
                scratch_shapes=[pltpu.VMEM(tokens.shape, bf)]
                + [
                    pltpu.VMEM((tokens.shape[1], 3 * LANES), bf),
                    pltpu.VMEM((2, size, LANES), bf),
                    pltpu.SemaphoreType.DMA((4,)),
                ],
                compiler_params=pltpu.CompilerParams(vmem_limit_bytes=WHOLE),
            )(tokens, w_key, w_value, w_query)
        got = [None] * heads
        for j in reversed(range(heads)):
            got[j] = turn(msgs[j], j)
        longest = -(-nb // SLOTS)
        cap = -(-nq * longest // STREAMS) + longest + 3
        table = jax.ShapeDtypeStruct((STREAMS * cap,), jnp.int32)
        tables = pl.pallas_call(
            functools.partial(list_kernel, inner, heads, per, cap),
            out_shape=[
                table,
                table,
                jax.ShapeDtypeStruct((nq * (nb + SLOTS),), jnp.int32),
                table,
                table,
                jax.ShapeDtypeStruct((1,), jnp.int32),
            ],
            in_specs=[SMEM] * 2,
            out_specs=[SMEM] * 6,
            scratch_shapes=[
                pltpu.SMEM((nb,), jnp.int32),
                pltpu.SMEM((nq,), jnp.int32),
                pltpu.SMEM((STREAMS,), jnp.int32),
            ],
            name="block_lists",
        )(block_mask, block_order)
        x = lax.axis_index("head") // 2
        w_out, msgs = lax.optimization_barrier((w_out, msgs))
        w_cols = []
        for g in range(0, groups, 2):
            share = lax.dynamic_slice_in_dim(w_out, (x ^ g // 2) * 2 * cols, 2 * cols, axis=1)
            w_cols.append(head_swap(share, g))
        got[0], tables, w_cols = lax.optimization_barrier((got[0], tables, w_cols))
        kv = []
        for j in range(heads):
            for e in range(inner):
                kv.append(spread(got[j], e))
        o = pl.pallas_call(
            functools.partial(attend_kernel, per, cap, len(kv), rows, heads),
            out_shape=[jax.ShapeDtypeStruct((half, LANES), bf)] * heads,
            in_specs=[SMEM] * 6 + [VMEM] * len(kv),
            out_specs=[VMEM] * heads,
            scratch_shapes=[
                pltpu.VMEM((nb // 2, BLOCK, LANES), bf),
                pltpu.VMEM((nb, HEAD_DIM, BLOCK), bf),
                pltpu.VMEM((2, nq + 1, LANES, BLOCK), bf),
                pltpu.VMEM((2, STREAMS, SLOTS, BLOCK, BLOCK), jnp.float32),
                pltpu.VMEM((2, STREAMS, 1, BLOCK), jnp.float32),
                pltpu.VMEM((2, STREAMS, 1, BLOCK), jnp.float32),
                pltpu.VMEM((STREAMS, 8, BLOCK), jnp.float32),
                pltpu.VMEM((STREAMS, HEAD_DIM, BLOCK), jnp.float32),
                pltpu.VMEM((nq + 1, 8, BLOCK), jnp.float32),
                pltpu.VMEM((nq + 1, HEAD_DIM, BLOCK), jnp.float32),
            ],
            compiler_params=params,
            name="attend",
        )(*tables, *kv)
        mine = [None] * heads
        for j in reversed(range(heads)):
            mine[j] = turn(o[j], j)
        pieces = []
        for g in range(0, groups, 2):
            for j in range(heads):
                pieces.append(head_swap(mine[j], g))

        def out(other, *more):
            return pl.pallas_call(
                functools.partial(out_kernel, inner, heads, groups // 2, other),
                out_shape=jax.ShapeDtypeStruct((rows, cols), bf),
                in_specs=[VMEM] * (len(pieces) + len(w_cols) + len(more)),
                out_specs=VMEM,
                compiler_params=params,
            )(*pieces, *w_cols, *more)

        return out(0, head_swap(out(1), 1))

    placed = (
        P("ctx", None),
        P(None, "head"),
        P(None, "head"),
        P(None, "head"),
        P("head", None),
        P(),
        P(),
    )
    return jax.shard_map(
        body, mesh=mesh, in_specs=placed, out_specs=P("ctx", "head"), check_vma=False
    )
```

```python
import functools

import jax
import jax.numpy as jnp
from jax import lax
from jax.experimental import pallas as pl
from jax.experimental.pallas import tpu as pltpu
from jax.sharding import PartitionSpec as P


HEAD_DIM = 64
BLOCK = 128
LANES = 128
SLOTS = 4
STREAMS = 4
TALL = HEAD_DIM + 16
NEG = -1e30


HBM = pl.BlockSpec(memory_space=pltpu.HBM)
VMEM = pl.BlockSpec(memory_space=pltpu.VMEM)
SMEM = pl.BlockSpec(memory_space=pltpu.SMEM)
GRANT = 16 * 1024 * 1024
WHOLE = 60 * 1024 * 1024


def low_half(shape):
    return lax.broadcasted_iota(jnp.int32, shape, len(shape) - 1) < HEAD_DIM


def swap_halves(x):
    return pltpu.roll(x, HEAD_DIM, 1)


def proj_kernel(inner, far, tok_in, wk_in, wv_in, wq_in, out0, out1, tok, w, msg, sems):
    a = lax.axis_index("ctx") // inner
    group = (a // 2) ^ far
    cols = pl.ds(pl.multiple_of(group * LANES, LANES), LANES)
    loads = [pltpu.make_async_copy(tok_in, tok, sems.at[0])] + [
        pltpu.make_async_copy(src.at[:, cols], w.at[:, pl.ds(n * LANES, LANES)], sems.at[n + 1])
        for n, src in enumerate((wv_in, wq_in, wk_in))
    ]
    for load in loads:
        load.start()
    rows = tok.shape[0]
    half = rows // 2
    low = low_half((half, LANES))
    for load in loads:
        load.wait()
    vqk = jnp.dot(tok[...], w[...], preferred_element_type=jnp.float32)
    v, q, k = (vqk[:, n * LANES : (n + 1) * LANES] for n in range(3))
    q = q * HEAD_DIM ** (-0.5)
    for base, x in ((half, v), (rows, q)):
        for i in range(rows // BLOCK):
            turned = jnp.transpose(x[i * BLOCK : (i + 1) * BLOCK]).astype(jnp.bfloat16)
            start = base + i * HEAD_DIM
            msg[0, start : start + HEAD_DIM] = turned[:HEAD_DIM]
            msg[1, start : start + HEAD_DIM] = turned[HEAD_DIM:]
    top, bottom = k[:half], k[half:]
    msg[0, :half] = jnp.where(low, top, swap_halves(bottom)).astype(jnp.bfloat16)
    msg[1, :half] = jnp.where(low, swap_halves(top), bottom).astype(jnp.bfloat16)
    odd = lax.rem(a, 2)
    out0[...] = msg[odd]
    out1[...] = msg[1 - odd]


def list_kernel(inner, outer, per, cap, mask, order, who, where, which, valid, first, steps, names, ends, load):
    c = lax.axis_index("ctx")
    a = c // inner
    b = (c % inner) // 2 * 2 + lax.axis_index("head") % 2
    blocks = inner * outer * per
    half = per // 2
    span = blocks + SLOTS

    def name(dev, _):
        kb = ((lax.div(dev, inner) ^ a) * inner + (lax.rem(dev, inner) ^ b)) * per
        for i in range(per):
            names[dev * per + i] = order[kb + i // 2 + i % 2 * half]
        return 0

    lax.fori_loop(0, inner * outer, name, 0)

    def piece(k, _):
        qb = ((k ^ a) * inner + b) * per
        own = [order[qb + i] for i in range(per)]

        def col(n, to):
            to = list(to)
            for e in range(8):
                slot = n * 8 + e
                key = names[slot]
                for i in range(per):
                    which[to[i]] = slot
                    to[i] = to[i] + mask[own[i], key]
            return tuple(to)

        begin = [(k * per + i) * span for i in range(per)]
        end = lax.fori_loop(0, blocks // 8, col, tuple(begin))
        for i in range(per):
            keep = which[begin[i]]
            for extra in range(SLOTS):
                which[end[i] + extra] = keep
            ends[k * per + i] = end[i]
        return 0

    lax.fori_loop(0, outer, piece, 0)
    for s in range(STREAMS):
        load[s] = 0

    def row(qi, _):
        s, least = jnp.int32(0), load[0]
        for other in range(1, STREAMS):
            here = load[other]
            s = jnp.where(here < least, other, s)
            least = jnp.minimum(here, least)
        item = s * cap + least
        start = qi * span
        count = ends[qi] - start
        items = lax.div(count + (SLOTS - 1), SLOTS)

        def mark(t, left):
            who[item + t] = qi
            where[item + t] = start + t * SLOTS
            valid[item + t] = left
            first[item + t] = 0
            return left - SLOTS

        lax.fori_loop(0, items, mark, count)
        first[item] = 1
        load[s] = least + items
        return 0

    lax.fori_loop(0, outer * per, row, 0)
    most = load[0]
    for s in range(1, STREAMS):
        most = jnp.maximum(most, load[s])
    steps[0] = most
    for s in range(STREAMS):
        start = s * cap
        last = start + jnp.maximum(load[s] - 1, 0)
        idle = load[s] == 0
        qi = jnp.where(idle, outer * per, who[last])
        key = jnp.where(idle, 0, where[last])

        def fill(t, _):
            who[start + t] = qi
            where[start + t] = key
            valid[start + t] = 0
            first[start + t] = 0
            return 0

        lax.fori_loop(load[s], most + 2, fill, 0)


def attend_kernel(per, cap, n_kv, start_q, n_q, who, where, which, valid, first, steps, *rest):
    ins, rest = rest[:n_kv], rest[n_kv:]
    q_in = ins[:: n_kv // n_q]
    outs, rest = rest[:n_q], rest[n_q:]
    kq, vt, qt, sc, m_s, al_s, acc_s, acc_all = rest
    half = per // 2
    nq = n_q * per
    zero = jnp.zeros((HEAD_DIM, BLOCK), jnp.bfloat16)
    ones = jnp.ones((TALL - HEAD_DIM, BLOCK), jnp.bfloat16)
    for k, msg in enumerate(q_in):
        for i in range(per):
            turned = msg[start_q + i * HEAD_DIM : start_q + (i + 1) * HEAD_DIM, :]
            qt[0, k * per + i] = jnp.concatenate([turned, zero], axis=0)
            qt[1, k * per + i] = jnp.concatenate([zero, turned], axis=0)
    qt[:, nq] = jnp.zeros((2, LANES, BLOCK), jnp.bfloat16)
    for n, msg in enumerate(ins):
        for r in range(half):
            kq[n * half + r] = msg[r * BLOCK : (r + 1) * BLOCK, :]
        for i in range(per):
            start = half * BLOCK + (i // 2 + i % 2 * half) * HEAD_DIM
            vt[n * per + i, :HEAD_DIM] = msg[start : start + HEAD_DIM, :]
            vt[n * per + i, HEAD_DIM:] = ones
    m_s[...] = jnp.full(m_s.shape, NEG, jnp.float32)
    acc_s[...] = jnp.zeros(acc_s.shape, jnp.float32)

    def keys(s, t):
        start = where[s * cap + t]
        return [which[start + e] for e in range(SLOTS)]

    def score(t, buf, s):
        qi = who[s * cap + t]
        tiles = []
        for e, slot in enumerate(keys(s, t)):
            tile = jnp.dot(kq[slot >> 1], qt[slot & 1, qi], preferred_element_type=jnp.float32)
            sc[buf, s, e] = tile
            tiles.append(tile.reshape(BLOCK // 8, 8, BLOCK))
        top = jnp.max(functools.reduce(jnp.maximum, tiles), axis=0)
        top = jnp.max(top, axis=0, keepdims=True)
        m_old = jnp.where(first[s * cap + t] == 1, NEG, m_s[1 - buf, s])
        m_new = jnp.maximum(m_old, top)
        al_s[buf, s] = jnp.exp(m_old - m_new)
        m_s[buf, s] = m_new

    def weigh(t, buf, s):
        qi = who[s * cap + t]
        n_valid = valid[s * cap + t]
        m, alpha = m_s[buf, s], al_s[buf, s]
        acc = acc_s[s] * alpha
        ids = keys(s, t)
        for e in range(0, SLOTS, 2):
            probs = []
            for f in (e, e + 1):
                shut = m + jnp.where(f < n_valid, 0.0, -NEG)
                probs.append(jnp.exp(sc[buf, s, f] - shut).astype(jnp.bfloat16))
            acc = acc + jnp.dot(
                jnp.concatenate([vt[ids[e]], vt[ids[e + 1]]], axis=1),
                jnp.concatenate(probs, axis=0),
                preferred_element_type=jnp.float32,
            )
        acc_s[s] = acc
        acc_all[qi] = acc

    for s in range(STREAMS):
        score(0, 0, s)
    count = steps[0]

    def step(u, _):
        for buf in (0, 1):
            for s in range(STREAMS):
                score(2 * u + 1 + buf, 1 - buf, s)
                weigh(2 * u + buf, buf, s)
        return 0

    lax.fori_loop(0, lax.div(count, 2), step, 0)

    @pl.when(lax.rem(count, 2) == 1)
    def _():
        for s in range(STREAMS):
            weigh(count - 1, 0, s)

    for k in range(n_q):
        for r in range(half):
            done = []
            for i in (k * per + r, k * per + r + half):
                total = acc_all[i]
                done.append(total[:HEAD_DIM] * (1.0 / total[HEAD_DIM : HEAD_DIM + 1]))
            outs[k][r * BLOCK : (r + 1) * BLOCK, :] = jnp.transpose(
                jnp.concatenate(done, axis=0)
            ).astype(jnp.bfloat16)


def out_kernel(inner, heads, groups, *refs):
    pieces = [refs[g * heads : (g + 1) * heads] for g in range(groups)]
    ws = refs[groups * heads : groups * heads + groups]
    out = refs[-1]
    a = lax.axis_index("ctx") // inner
    half = pieces[0][0].shape[0]
    low = low_half((half, LANES))
    tops, bottoms, rows = [], [], []
    for g in range(groups):
        for k in range(0, heads, 2):
            p0 = pieces[g][k][...].astype(jnp.float32)
            p1 = pieces[g][k + 1][...].astype(jnp.float32)
            tops.append(jnp.where(low, p0, swap_halves(p1)).astype(jnp.bfloat16))
            bottoms.append(jnp.where(low, swap_halves(p0), p1).astype(jnp.bfloat16))
            for e in (0, 1):
                start = pl.multiple_of(HEAD_DIM * (a ^ (k + e)), HEAD_DIM)
                rows.append(ws[g][pl.ds(start, HEAD_DIM), :])
    w = jnp.concatenate(rows, axis=0)
    for n, parts in enumerate((tops, bottoms)):
        x = jnp.concatenate(parts, axis=1)
        out[n * half : (n + 1) * half, :] = jnp.dot(
            x, w, preferred_element_type=jnp.float32
        ).astype(out.dtype)


def solution(mesh):
    ctx, groups = mesh.shape["ctx"], mesh.shape["head"]

    def body(tokens, w_query, w_key, w_value, w_out, block_mask, block_order):
        rows = tokens.shape[0]
        heads = w_query.shape[1] // HEAD_DIM
        inner = ctx // heads
        per = rows // BLOCK
        nb = block_mask.shape[0]
        nq = heads * per
        cols = w_out.shape[1] // groups
        bf = jnp.bfloat16
        params = pltpu.CompilerParams(vmem_limit_bytes=GRANT)
        both = ("ctx", "head")
        places = [(c // inner, c % inner, h) for c in range(ctx) for h in range(groups)]

        def index(a, b, h):
            return (a * inner + b) * groups + h

        def turn(x, j):
            pairs = [
                (index(a, b, h), index(a ^ j, (b & ~1) | (h & 1), (h & ~1) | (b & 1)))
                for a, b, h in places
            ]
            return lax.ppermute(x, both, pairs)

        def spread(x, e):
            pairs = [
                (index(a, b, h), index(a, b ^ (e & ~1), h ^ (e & 1))) for a, b, h in places
            ]
            return lax.ppermute(x, both, pairs) if e else x

        def head_swap(x, j):
            return lax.ppermute(x, "head", [(h, h ^ j) for h in range(groups)]) if j else x

        half, size = rows // 2, rows + rows // 2
        msgs = []
        for far in range(heads // 2):
            msgs += pl.pallas_call(
                functools.partial(proj_kernel, inner, far),
                out_shape=[jax.ShapeDtypeStruct((size, LANES), bf)] * 2,
                in_specs=[HBM] * 4,
                out_specs=[VMEM] * 2,
                scratch_shapes=[pltpu.VMEM(tokens.shape, bf)]
                + [
                    pltpu.VMEM((tokens.shape[1], 3 * LANES), bf),
                    pltpu.VMEM((2, size, LANES), bf),
                    pltpu.SemaphoreType.DMA((4,)),
                ],
                compiler_params=pltpu.CompilerParams(vmem_limit_bytes=WHOLE),
            )(tokens, w_key, w_value, w_query)
        got = [None] * heads
        for j in reversed(range(heads)):
            got[j] = turn(msgs[j], j)
        longest = -(-nb // SLOTS)
        cap = -(-nq * longest // STREAMS) + longest + 3
        table = jax.ShapeDtypeStruct((STREAMS * cap,), jnp.int32)
        tables = pl.pallas_call(
            functools.partial(list_kernel, inner, heads, per, cap),
            out_shape=[
                table,
                table,
                jax.ShapeDtypeStruct((nq * (nb + SLOTS),), jnp.int32),
                table,
                table,
                jax.ShapeDtypeStruct((1,), jnp.int32),
            ],
            in_specs=[SMEM] * 2,
            out_specs=[SMEM] * 6,
            scratch_shapes=[
                pltpu.SMEM((nb,), jnp.int32),
                pltpu.SMEM((nq,), jnp.int32),
                pltpu.SMEM((STREAMS,), jnp.int32),
            ],
            name="block_lists",
        )(block_mask, block_order)
        h = lax.axis_index("head")
        w_out, msgs = lax.optimization_barrier((w_out, msgs))
        w_cols = []
        for g in range(groups):
            share = lax.dynamic_slice_in_dim(w_out, (h ^ g) * cols, cols, axis=1)
            w_cols.append(head_swap(share, g))
        got[0], tables = lax.optimization_barrier((got[0], tables))
        kv = []
        for j in range(heads):
            for e in range(inner):
                kv.append(spread(got[j], e))
        o = pl.pallas_call(
            functools.partial(attend_kernel, per, cap, len(kv), rows, heads),
            out_shape=[jax.ShapeDtypeStruct((half, LANES), bf)] * heads,
            in_specs=[SMEM] * 6 + [VMEM] * len(kv),
            out_specs=[VMEM] * heads,
            scratch_shapes=[
                pltpu.VMEM((nb // 2, BLOCK, LANES), bf),
                pltpu.VMEM((nb, TALL, BLOCK), bf),
                pltpu.VMEM((2, nq + 1, LANES, BLOCK), bf),
                pltpu.VMEM((2, STREAMS, SLOTS, BLOCK, BLOCK), jnp.float32),
                pltpu.VMEM((2, STREAMS, 1, BLOCK), jnp.float32),
                pltpu.VMEM((2, STREAMS, 1, BLOCK), jnp.float32),
                pltpu.VMEM((STREAMS, TALL, BLOCK), jnp.float32),
                pltpu.VMEM((nq + 1, TALL, BLOCK), jnp.float32),
            ],
            compiler_params=params,
            name="attend",
        )(*tables, *kv)
        mine = [None] * heads
        for j in reversed(range(heads)):
            mine[j] = turn(o[j], j)
        parts = [mine]
        for g in range(1, groups):
            part = []
            for j in range(heads):
                part.append(head_swap(parts[g - 1][j], 1) if g % 2 else head_swap(mine[j], g))
            parts.append(part)
        return pl.pallas_call(
            functools.partial(out_kernel, inner, heads, groups),
            out_shape=jax.ShapeDtypeStruct((rows, cols), bf),
            in_specs=[VMEM] * (groups * heads + groups),
            out_specs=VMEM,
            compiler_params=params,
            name="out_proj",
        )(*[x for part in parts for x in part], *w_cols)

    placed = (
        P("ctx", None),
        P(None, "head"),
        P(None, "head"),
        P(None, "head"),
        P("head", None),
        P(),
        P(),
    )
    return jax.shard_map(
        body, mesh=mesh, in_specs=placed, out_specs=P("ctx", "head"), check_vma=False
    )
```

```python
import functools

import jax
import jax.numpy as jnp
from jax import lax
from jax.experimental import pallas as pl
from jax.experimental.pallas import tpu as pltpu
from jax.sharding import PartitionSpec as P


HEAD_DIM = 64
BLOCK = 128
LANES = 128
PAIR = 2
SLOTS = 4
LINES = 2
TALL = HEAD_DIM + 16
NEG = -1e30


HBM = pl.BlockSpec(memory_space=pltpu.HBM)
VMEM = pl.BlockSpec(memory_space=pltpu.VMEM)
SMEM = pl.BlockSpec(memory_space=pltpu.SMEM)
GRANT = 16 * 1024 * 1024
WHOLE = 60 * 1024 * 1024


def proj_kernel(inner, tok_in, wk_in, wv_in, wq_in, *rest):
    outs, (tok, wk, wv, wq, msg, sems) = rest[:4], rest[4:]
    loads = [
        pltpu.make_async_copy(src, dst, sems.at[n])
        for n, (src, dst) in enumerate(((tok_in, tok), (wv_in, wv), (wk_in, wk), (wq_in, wq)))
    ]
    for load in loads:
        load.start()
    low = (lax.axis_index("ctx") // inner) % PAIR
    rows = tok.shape[0]
    loads[0].wait()
    loads[1].wait()
    v = jnp.dot(tok[...], wv[...], preferred_element_type=jnp.float32)
    loads[2].wait()
    loads[3].wait()
    q = jnp.dot(tok[...], wq[...], preferred_element_type=jnp.float32) * HEAD_DIM ** (-0.5)
    k = jnp.dot(tok[...], wk[...], preferred_element_type=jnp.float32)
    for g in range(PAIR):
        cols = slice(g * LANES, (g + 1) * LANES)
        msg[g, :rows] = k[:, cols].astype(jnp.bfloat16)
        for base, x in ((rows, v), (2 * rows, q)):
            for i in range(rows // BLOCK):
                block = x[i * BLOCK : (i + 1) * BLOCK, cols]
                start = base + i * BLOCK
                msg[g, start : start + BLOCK] = jnp.transpose(block).astype(jnp.bfloat16)
    for j, out in enumerate(outs):
        out[...] = msg[low ^ (j % PAIR), : out.shape[0]]


def list_kernel(inner, outer, per, cap, mask, order, who, where, which, valid, first, steps, names, ends, load):
    c = lax.axis_index("ctx")
    a = c // inner
    b = (c % inner) // 2 * 2 + lax.axis_index("head") % 2
    part_blocks = inner * PAIR * per
    parts = outer // PAIR
    size = PAIR * per
    span = part_blocks + SLOTS

    def name(dev, _):
        kb = ((lax.div(dev, inner) ^ a) * inner + (lax.rem(dev, inner) ^ b)) * per
        for i in range(per):
            names[dev * per + i] = order[kb + i]
        return 0

    lax.fori_loop(0, inner * outer, name, 0)

    def piece(n, _):
        part, k = lax.div(n, PAIR), lax.rem(n, PAIR)
        qb = ((k ^ a) * inner + b) * per
        own = [order[qb + i] for i in range(per)]

        def col(m, to):
            to = list(to)
            for e in range(8):
                slot = m * 8 + e
                key = names[part * part_blocks + slot]
                for i in range(per):
                    which[to[i]] = slot
                    to[i] = to[i] + mask[own[i], key]
            return tuple(to)

        begin = [(n * per + i) * span for i in range(per)]
        end = lax.fori_loop(0, part_blocks // 8, col, tuple(begin))
        for i in range(per):
            some = end[i] > begin[i]
            keep = jnp.where(some, which[begin[i]], 0)
            for extra in range(SLOTS):
                which[end[i] + extra] = keep
            ends[n * per + i] = end[i]
        return 0

    lax.fori_loop(0, parts * PAIR, piece, 0)
    for part in range(parts):
        for s in range(LINES):
            load[s] = 0

        def row(qi, _):
            s, least = jnp.int32(0), load[0]
            for other in range(1, LINES):
                here = load[other]
                s = jnp.where(here < least, other, s)
                least = jnp.minimum(here, least)
            item = (part * LINES + s) * cap + least
            start = (part * size + qi) * span
            count = ends[part * size + qi] - start
            items = lax.div(count + (SLOTS - 1), SLOTS)
            first[item] = 1

            def mark(t, left):
                who[item + t] = qi
                where[item + t] = start + t * SLOTS
                valid[item + t] = left
                first[item + t + 1] = 0
                return left - SLOTS

            lax.fori_loop(0, items, mark, count)
            load[s] = least + items
            return 0

        lax.fori_loop(0, size, row, 0)
        most = load[0]
        for s in range(1, LINES):
            most = jnp.maximum(most, load[s])
        steps[part] = most
        for s in range(LINES):
            start = (part * LINES + s) * cap
            last = start + jnp.maximum(load[s] - 1, 0)
            idle = load[s] == 0
            qi = jnp.where(idle, size, who[last])
            key = jnp.where(idle, part * size * span, where[last])

            def fill(t, _):
                who[start + t] = qi
                where[start + t] = key
                valid[start + t] = 0
                first[start + t] = 0
                return 0

            lax.fori_loop(load[s], most + 2, fill, 0)


def attend_kernel(part, per, cap, n_kv, n_q, who, where, which, valid, first, steps, *rest):
    ins, rest = rest[:n_kv], rest[n_kv:]
    q_in, rest = rest[:n_q], rest[n_q:]
    if part:
        (acc_old, m_old_all), rest = rest[:2], rest[2:]
        outs, (kq, vt, qt, sc, m_s, al_s, acc_s, acc_all, m_all) = rest[:n_q], rest[n_q:]
    else:
        (acc_all, m_all), (kq, vt, qt, sc, m_s, al_s, acc_s) = rest[:2], rest[2:]
    nq = n_q * per
    rows = per * BLOCK
    zero = jnp.zeros((HEAD_DIM, BLOCK), jnp.bfloat16)
    ones = jnp.ones((TALL - HEAD_DIM, BLOCK), jnp.bfloat16)
    for k, msg in enumerate(q_in):
        for i in range(per):
            start = 2 * rows + i * BLOCK
            turned = msg[start : start + BLOCK, :]
            qt[k * per + i] = jnp.concatenate([turned[:HEAD_DIM], zero], axis=0)
            qt[nq + 1 + k * per + i] = jnp.concatenate([zero, turned[HEAD_DIM:]], axis=0)
    for e in range(PAIR):
        qt[e * (nq + 1) + nq] = jnp.zeros((LANES, BLOCK), jnp.bfloat16)
    for n, msg in enumerate(ins):
        for i in range(per):
            kq[n * per + i] = msg[i * BLOCK : (i + 1) * BLOCK, :]
            start = rows + i * BLOCK
            for e in range(PAIR):
                at = 2 * (n * per + i) + e
                vt[at, :HEAD_DIM] = msg[start + e * HEAD_DIM : start + (e + 1) * HEAD_DIM, :]
                vt[at, HEAD_DIM:] = ones
    m_s[...] = jnp.full(m_s.shape, NEG, jnp.float32)
    acc_s[...] = jnp.zeros(acc_s.shape, jnp.float32)
    if part:
        acc_all[...] = acc_old[...]

    def score(t, buf, s):
        line, e = s // PAIR, s % PAIR
        at = (part * LINES + line) * cap + t
        row = e * (nq + 1) + who[at]
        start = where[at]
        q = qt[row]
        tiles = []
        for f in range(SLOTS):
            tile = jnp.dot(kq[which[start + f]], q, preferred_element_type=jnp.float32)
            sc[buf, s, f] = tile
            tiles.append(tile.reshape(BLOCK // 8, 8, BLOCK))
        top = jnp.max(functools.reduce(jnp.maximum, tiles), axis=0)
        top = jnp.max(top, axis=0, keepdims=True)
        before = m_old_all[row] if part else NEG
        m_old = jnp.where(first[at] == 1, before, m_s[1 - buf, s])
        m_new = jnp.where(valid[at] > 0, jnp.maximum(m_old, top), m_old)
        al_s[buf, s] = jnp.exp(m_old - m_new)
        m_s[buf, s] = m_new

    def weigh(t, buf, s):
        line, e = s // PAIR, s % PAIR
        at = (part * LINES + line) * cap + t
        row = e * (nq + 1) + who[at]
        start = where[at]
        n_valid = valid[at]
        m, alpha = m_s[buf, s], al_s[buf, s]
        acc = acc_s[s]
        if part:
            acc = jnp.where(first[at] == 1, acc_old[row], acc)
        acc = acc * alpha
        for f in range(0, SLOTS, 2):
            probs, values = [], []
            for n in (f, f + 1):
                shut = m + jnp.where(n < n_valid, 0.0, -NEG)
                probs.append(jnp.exp(sc[buf, s, n] - shut).astype(jnp.bfloat16))
                values.append(vt[which[start + n] * 2 + e])
            acc = acc + jnp.dot(
                jnp.concatenate(values, axis=1),
                jnp.concatenate(probs, axis=0),
                preferred_element_type=jnp.float32,
            )
        acc_s[s] = acc
        acc_all[row] = acc
        if not part:
            m_all[row] = m

    streams = range(LINES * PAIR)
    for s in streams:
        score(0, 0, s)
    count = steps[part]

    def step(u, _):
        for buf in (0, 1):
            for s in streams:
                score(2 * u + 1 + buf, 1 - buf, s)
                weigh(2 * u + buf, buf, s)
        return 0

    lax.fori_loop(0, lax.div(count, 2), step, 0)

    @pl.when(lax.rem(count, 2) == 1)
    def _():
        for s in streams:
            weigh(count - 1, 0, s)

    if part:
        for k in range(n_q):
            for i in range(per):
                done = []
                for e in range(PAIR):
                    total = acc_all[e * (nq + 1) + k * per + i]
                    done.append(total[:HEAD_DIM] * (1.0 / total[HEAD_DIM : HEAD_DIM + 1]))
                outs[k][i * BLOCK : (i + 1) * BLOCK, :] = jnp.transpose(
                    jnp.concatenate(done, axis=0)
                ).astype(jnp.bfloat16)


def out_kernel(inner, groups, *refs):
    pieces, ws, out = refs[: groups * PAIR], refs[groups * PAIR : -1], refs[-1]
    low = (lax.axis_index("ctx") // inner) % PAIR
    rows = []
    for g in range(groups):
        for k in range(PAIR):
            start = pl.multiple_of(LANES * (low ^ k), LANES)
            rows.append(ws[g][pl.ds(start, LANES), :])
    x = jnp.concatenate([piece[...] for piece in pieces], axis=1)
    w = jnp.concatenate(rows, axis=0)
    out[...] = jnp.dot(x, w, preferred_element_type=jnp.float32).astype(out.dtype)


def solution(mesh):
    ctx, groups = mesh.shape["ctx"], mesh.shape["head"]

    def body(tokens, w_query, w_key, w_value, w_out, block_mask, block_order):
        rows = tokens.shape[0]
        outer = w_query.shape[1] // HEAD_DIM
        inner = ctx // outer
        per = rows // BLOCK
        nb = block_mask.shape[0]
        nq = PAIR * per
        cols = w_out.shape[1] // groups
        bf, f32 = jnp.bfloat16, jnp.float32
        params = pltpu.CompilerParams(vmem_limit_bytes=GRANT)
        both = ("ctx", "head")
        places = [(c // inner, c % inner, h) for c in range(ctx) for h in range(groups)]

        def index(a, b, h):
            return (a * inner + b) * groups + h

        def turn(x, j, g=0):
            pairs = [
                (index(a, b, h), index(a ^ j, (b & ~1) | (h & 1), ((h & ~1) | (b & 1)) ^ g))
                for a, b, h in places
            ]
            return lax.ppermute(x, both, pairs)

        def spread(x, e):
            pairs = [
                (index(a, b, h), index(a, b ^ (e & ~1), h ^ (e & 1))) for a, b, h in places
            ]
            return lax.ppermute(x, both, pairs) if e else x

        def head_swap(x, j):
            return lax.ppermute(x, "head", [(h, h ^ j) for h in range(groups)]) if j else x

        sizes = [3 * rows] * PAIR + [2 * rows] * (outer - PAIR)
        msgs = pl.pallas_call(
            functools.partial(proj_kernel, inner),
            out_shape=[jax.ShapeDtypeStruct((n, LANES), bf) for n in sizes],
            in_specs=[HBM] * 4,
            out_specs=[VMEM] * len(sizes),
            scratch_shapes=[pltpu.VMEM(x.shape, bf) for x in (tokens, w_value, w_key, w_query)]
            + [
                pltpu.VMEM((PAIR, 3 * rows, LANES), bf),
                pltpu.SemaphoreType.DMA((4,)),
            ],
            compiler_params=pltpu.CompilerParams(vmem_limit_bytes=WHOLE),
            name="proj",
        )(tokens, w_key, w_value, w_query)
        got = [turn(msgs[j], j) for j in range(outer)]
        parts = outer // PAIR
        part_nb = nb // parts
        longest = -(-part_nb // SLOTS)
        cap = -(-nq * longest // LINES) + longest + 3
        table = jax.ShapeDtypeStruct((parts * LINES * cap,), jnp.int32)
        tables = pl.pallas_call(
            functools.partial(list_kernel, inner, outer, per, cap),
            out_shape=[
                table,
                table,
                jax.ShapeDtypeStruct((parts * nq * (part_nb + SLOTS),), jnp.int32),
                table,
                table,
                jax.ShapeDtypeStruct((parts,), jnp.int32),
            ],
            in_specs=[SMEM] * 2,
            out_specs=[SMEM] * 6,
            scratch_shapes=[
                pltpu.SMEM((nb,), jnp.int32),
                pltpu.SMEM((parts * nq,), jnp.int32),
                pltpu.SMEM((LINES,), jnp.int32),
            ],
            name="block_lists",
        )(block_mask, block_order)
        h = lax.axis_index("head")
        w_out, msgs = lax.optimization_barrier((w_out, msgs))
        w_cols = []
        for g in range(groups):
            share = lax.dynamic_slice_in_dim(w_out, (h ^ g) * cols, cols, axis=1)
            w_cols.append(head_swap(share, g))
        got[0], tables = lax.optimization_barrier((got[0], tables))
        wide = PAIR * (nq + 1)
        state = [
            jax.ShapeDtypeStruct((wide, TALL, BLOCK), f32),
            jax.ShapeDtypeStruct((wide, 1, BLOCK), f32),
        ]
        made = []
        for part in range(parts):
            last = part > 0
            pieces = range(part * PAIR, (part + 1) * PAIR)
            if last:
                got[pieces[0]], made = lax.optimization_barrier((got[pieces[0]], made))
            kv = [spread(got[j], e) for j in pieces for e in range(inner)]
            made = pl.pallas_call(
                functools.partial(attend_kernel, part, per, cap, len(kv), PAIR),
                out_shape=[jax.ShapeDtypeStruct((rows, LANES), bf)] * PAIR if last else state,
                in_specs=[SMEM] * 6 + [VMEM] * (len(kv) + PAIR + len(made)),
                out_specs=[VMEM] * 2,
                scratch_shapes=[
                    pltpu.VMEM((part_nb, BLOCK, LANES), bf),
                    pltpu.VMEM((2 * part_nb, TALL, BLOCK), bf),
                    pltpu.VMEM((wide, LANES, BLOCK), bf),
                    pltpu.VMEM((2, LINES * PAIR, SLOTS, BLOCK, BLOCK), f32),
                    pltpu.VMEM((2, LINES * PAIR, 1, BLOCK), f32),
                    pltpu.VMEM((2, LINES * PAIR, 1, BLOCK), f32),
                    pltpu.VMEM((LINES * PAIR, TALL, BLOCK), f32),
                ]
                + ([pltpu.VMEM(x.shape, f32) for x in state] if last else []),
                compiler_params=params,
            )(*tables, *kv, *got[:PAIR], *made)
        pieces = []
        for g in range(0, groups, 2):
            for k in range(PAIR):
                pieces.append(turn(made[k], k, g))
        gathered = []
        for g in range(0, groups, 2):
            own = pieces[g : g + PAIR]
            gathered += own
            gathered += [head_swap(own[k], 1) for k in range(PAIR)]
        return pl.pallas_call(
            functools.partial(out_kernel, inner, groups),
            out_shape=jax.ShapeDtypeStruct((rows, cols), bf),
            in_specs=[VMEM] * (len(gathered) + groups),
            out_specs=VMEM,
            compiler_params=params,
            name="out_proj",
        )(*gathered, *w_cols)

    placed = (
        P("ctx", None),
        P(None, "head"),
        P(None, "head"),
        P(None, "head"),
        P("head", None),
        P(),
        P(),
    )
    return jax.shard_map(
        body, mesh=mesh, in_specs=placed, out_specs=P("ctx", "head"), check_vma=False
    )
```

```python
import functools

import jax
import jax.numpy as jnp
from jax import lax
from jax.experimental import pallas as pl
from jax.experimental.pallas import tpu as pltpu
from jax.sharding import PartitionSpec as P


HEAD_DIM = 64
BLOCK = 128
LANES = 128
SLOTS = 4
STREAMS = 4
TALL = HEAD_DIM + 16
NEG = -1e30


HBM = pl.BlockSpec(memory_space=pltpu.HBM)
VMEM = pl.BlockSpec(memory_space=pltpu.VMEM)
SMEM = pl.BlockSpec(memory_space=pltpu.SMEM)
GRANT = 16 * 1024 * 1024
WHOLE = 60 * 1024 * 1024


def low_half(shape):
    return lax.broadcasted_iota(jnp.int32, shape, len(shape) - 1) < HEAD_DIM


def swap_halves(x):
    return pltpu.roll(x, HEAD_DIM, 1)


def proj_kernel(inner, heads, near, tok_in, wk_in, wv_in, wq_in, *rest):
    n_out = 2 * heads - near
    outs, (tok, wk, wv, wq, msg, sems) = rest[:n_out], rest[n_out:]
    loads = [
        pltpu.make_async_copy(src, dst, sems.at[n])
        for n, (src, dst) in enumerate(((tok_in, tok), (wv_in, wv), (wk_in, wk), (wq_in, wq)))
    ]
    for load in loads:
        load.start()
    a = lax.axis_index("ctx") // inner
    rows = tok.shape[0]
    half = rows // 2
    low = low_half((half, LANES))
    loads[0].wait()
    loads[1].wait()
    v = jnp.dot(tok[...], wv[...], preferred_element_type=jnp.float32)
    loads[2].wait()
    loads[3].wait()
    q = jnp.dot(tok[...], wq[...], preferred_element_type=jnp.float32) * HEAD_DIM ** (-0.5)
    k = jnp.dot(tok[...], wk[...], preferred_element_type=jnp.float32)
    for base, x in ((half, v), (rows, q)):
        for g in range(heads // 2):
            for i in range(rows // BLOCK):
                block = x[i * BLOCK : (i + 1) * BLOCK, g * LANES : (g + 1) * LANES]
                turned = jnp.transpose(block).astype(jnp.bfloat16)
                start = base + i * HEAD_DIM
                msg[2 * g, start : start + HEAD_DIM] = turned[:HEAD_DIM]
                msg[2 * g + 1, start : start + HEAD_DIM] = turned[HEAD_DIM:]
    for h in range(heads):
        cols = slice(LANES * (h // 2), LANES * (h // 2) + LANES)
        top, bottom = k[:half, cols], k[half:, cols]
        if h % 2 == 0:
            bottom = swap_halves(bottom)
        else:
            top = swap_halves(top)
        msg[h, :half] = jnp.where(low, top, bottom).astype(jnp.bfloat16)
    for j in range(heads):
        if j < near:
            outs[j][...] = msg[a ^ j]
        else:
            outs[j][...] = msg[a ^ j, :rows]
            outs[heads + j - near][...] = msg[a ^ j, rows:]


def list_kernel(inner, outer, per, cap, parts, mask, order, who, where, which, valid, first, steps, names, ends, load):
    c = lax.axis_index("ctx")
    a = c // inner
    b = (c % inner) // 2 * 2 + lax.axis_index("head") % 2
    blocks = inner * outer * per
    half = per // 2
    size = outer * per // parts
    span = blocks + SLOTS

    def name(dev, _):
        kb = ((lax.div(dev, inner) ^ a) * inner + (lax.rem(dev, inner) ^ b)) * per
        for i in range(per):
            names[dev * per + i] = order[kb + i // 2 + i % 2 * half]
        return 0

    lax.fori_loop(0, inner * outer, name, 0)

    def piece(k, _):
        qb = ((k ^ a) * inner + b) * per
        own = [order[qb + i] for i in range(per)]

        def col(n, to):
            to = list(to)
            for e in range(8):
                slot = n * 8 + e
                key = names[slot]
                for i in range(per):
                    which[to[i]] = slot
                    to[i] = to[i] + mask[own[i], key]
            return tuple(to)

        begin = [(k * per + i) * span for i in range(per)]
        end = lax.fori_loop(0, blocks // 8, col, tuple(begin))
        for i in range(per):
            keep = which[begin[i]]
            for extra in range(SLOTS):
                which[end[i] + extra] = keep
            ends[k * per + i] = end[i]
        return 0

    lax.fori_loop(0, outer, piece, 0)
    for part in range(parts):
        for s in range(STREAMS):
            load[s] = 0

        def row(qi, _):
            s, least = jnp.int32(0), load[0]
            for other in range(1, STREAMS):
                here = load[other]
                s = jnp.where(here < least, other, s)
                least = jnp.minimum(here, least)
            item = (part * STREAMS + s) * cap + least
            start = qi * span
            count = ends[qi] - start
            items = lax.div(count + (SLOTS - 1), SLOTS)

            def mark(t, left):
                who[item + t] = qi - part * size
                where[item + t] = start + t * SLOTS
                valid[item + t] = left
                first[item + t] = 0
                return left - SLOTS

            lax.fori_loop(0, items, mark, count)
            first[item] = 1
            load[s] = least + items
            return 0

        lax.fori_loop(part * size, (part + 1) * size, row, 0)
        most = load[0]
        for s in range(1, STREAMS):
            most = jnp.maximum(most, load[s])
        steps[part] = most
        for s in range(STREAMS):
            start = (part * STREAMS + s) * cap
            last = start + jnp.maximum(load[s] - 1, 0)
            idle = load[s] == 0
            qi = jnp.where(idle, size, who[last])
            key = jnp.where(idle, 0, where[last])

            def fill(t, _):
                who[start + t] = qi
                where[start + t] = key
                valid[start + t] = 0
                first[start + t] = 0
                return 0

            lax.fori_loop(load[s], most + 2, fill, 0)


def attend_kernel(part, per, cap, n_kv, spans, who, where, which, valid, first, steps, *rest):
    ins, rest = rest[:n_kv], rest[n_kv:]
    q_in, rest = rest[: len(spans)], rest[len(spans) :]
    outs, rest = rest[: len(spans)], rest[len(spans) :]
    if part == 0:
        (kq, vt), rest = rest[:2], rest[2:]
    else:
        kq, vt = ins
    qt, sc, m_s, al_s, acc_s, acc_all = rest
    half = per // 2
    nq = len(spans) * per
    zero = jnp.zeros((HEAD_DIM, BLOCK), jnp.bfloat16)
    ones = jnp.ones((TALL - HEAD_DIM, BLOCK), jnp.bfloat16)
    for k, start in enumerate(spans):
        for i in range(per):
            turned = q_in[k][start + i * HEAD_DIM : start + (i + 1) * HEAD_DIM, :]
            qt[0, k * per + i] = jnp.concatenate([turned, zero], axis=0)
            qt[1, k * per + i] = jnp.concatenate([zero, turned], axis=0)
    qt[:, nq] = jnp.zeros((2, LANES, BLOCK), jnp.bfloat16)
    if part == 0:
        for n, msg in enumerate(ins):
            for r in range(half):
                kq[n * half + r] = msg[r * BLOCK : (r + 1) * BLOCK, :]
            for i in range(per):
                start = half * BLOCK + (i // 2 + i % 2 * half) * HEAD_DIM
                vt[n * per + i, :HEAD_DIM] = msg[start : start + HEAD_DIM, :]
                vt[n * per + i, HEAD_DIM:] = ones
    m_s[...] = jnp.full(m_s.shape, NEG, jnp.float32)
    acc_s[...] = jnp.zeros(acc_s.shape, jnp.float32)

    def keys(s, t):
        start = where[(part * STREAMS + s) * cap + t]
        return [which[start + e] for e in range(SLOTS)]

    def score(t, buf, s):
        qi = who[(part * STREAMS + s) * cap + t]
        tiles = []
        for e, slot in enumerate(keys(s, t)):
            tile = jnp.dot(kq[slot >> 1], qt[slot & 1, qi], preferred_element_type=jnp.float32)
            sc[buf, s, e] = tile
            tiles.append(tile.reshape(BLOCK // 8, 8, BLOCK))
        top = jnp.max(functools.reduce(jnp.maximum, tiles), axis=0)
        top = jnp.max(top, axis=0, keepdims=True)
        m_old = jnp.where(first[(part * STREAMS + s) * cap + t] == 1, NEG, m_s[1 - buf, s])
        m_new = jnp.maximum(m_old, top)
        al_s[buf, s] = jnp.exp(m_old - m_new)
        m_s[buf, s] = m_new

    def weigh(t, buf, s):
        qi = who[(part * STREAMS + s) * cap + t]
        n_valid = valid[(part * STREAMS + s) * cap + t]
        m, alpha = m_s[buf, s], al_s[buf, s]
        acc = acc_s[s] * alpha
        ids = keys(s, t)
        for e in range(0, SLOTS, 2):
            probs = []
            for f in (e, e + 1):
                shut = m + jnp.where(f < n_valid, 0.0, -NEG)
                probs.append(jnp.exp(sc[buf, s, f] - shut).astype(jnp.bfloat16))
            acc = acc + jnp.dot(
                jnp.concatenate([vt[ids[e]], vt[ids[e + 1]]], axis=1),
                jnp.concatenate(probs, axis=0),
                preferred_element_type=jnp.float32,
            )
        acc_s[s] = acc
        acc_all[qi] = acc

    for s in range(STREAMS):
        score(0, 0, s)
    count = steps[part]

    def step(u, _):
        for buf in (0, 1):
            for s in range(STREAMS):
                score(2 * u + 1 + buf, 1 - buf, s)
                weigh(2 * u + buf, buf, s)
        return 0

    lax.fori_loop(0, lax.div(count, 2), step, 0)

    @pl.when(lax.rem(count, 2) == 1)
    def _():
        for s in range(STREAMS):
            weigh(count - 1, 0, s)

    for k in range(len(spans)):
        for r in range(half):
            done = []
            for i in (k * per + r, k * per + r + half):
                total = acc_all[i]
                done.append(total[:HEAD_DIM] * (1.0 / total[HEAD_DIM : HEAD_DIM + 1]))
            outs[k][r * BLOCK : (r + 1) * BLOCK, :] = jnp.transpose(
                jnp.concatenate(done, axis=0)
            ).astype(jnp.bfloat16)


def out_kernel(inner, heads, groups, other, *refs):
    pieces = [refs[g * heads : (g + 1) * heads] for g in range(groups)]
    ws = refs[groups * heads : groups * heads + groups]
    out = refs[-1]
    a = lax.axis_index("ctx") // inner
    side = (lax.axis_index("head") % 2) ^ other
    cols = pl.ds(pl.multiple_of(side * out.shape[1], LANES), out.shape[1])
    half = pieces[0][0].shape[0]
    low = low_half((half, LANES))
    tops, bottoms, rows = [], [], []
    for g in range(groups):
        for k in range(0, heads, 2):
            p0 = pieces[g][k][...].astype(jnp.float32)
            p1 = pieces[g][k + 1][...].astype(jnp.float32)
            tops.append(jnp.where(low, p0, swap_halves(p1)).astype(jnp.bfloat16))
            bottoms.append(jnp.where(low, swap_halves(p0), p1).astype(jnp.bfloat16))
            for e in (0, 1):
                start = pl.multiple_of(HEAD_DIM * (a ^ (k + e)), HEAD_DIM)
                rows.append(ws[g][pl.ds(start, HEAD_DIM), cols])
    w = jnp.concatenate(rows, axis=0)
    for n, parts in enumerate((tops, bottoms)):
        x = jnp.concatenate(parts, axis=1)
        total = jnp.dot(x, w, preferred_element_type=jnp.float32)
        if not other:
            total = total + refs[-2][n * half : (n + 1) * half, :].astype(jnp.float32)
        out[n * half : (n + 1) * half, :] = total.astype(out.dtype)


def solution(mesh):
    ctx, groups = mesh.shape["ctx"], mesh.shape["head"]

    def body(tokens, w_query, w_key, w_value, w_out, block_mask, block_order):
        rows = tokens.shape[0]
        heads = w_query.shape[1] // HEAD_DIM
        inner = ctx // heads
        per = rows // BLOCK
        nb = block_mask.shape[0]
        nq = heads * per
        cols = w_out.shape[1] // groups
        bf = jnp.bfloat16
        params = pltpu.CompilerParams(vmem_limit_bytes=GRANT)
        both = ("ctx", "head")
        places = [(c // inner, c % inner, h) for c in range(ctx) for h in range(groups)]

        def index(a, b, h):
            return (a * inner + b) * groups + h

        def turn(x, j):
            pairs = [
                (index(a, b, h), index(a ^ j, (b & ~1) | (h & 1), (h & ~1) | (b & 1)))
                for a, b, h in places
            ]
            return lax.ppermute(x, both, pairs)

        def spread(x, e):
            pairs = [
                (index(a, b, h), index(a, b ^ (e & ~1), h ^ (e & 1))) for a, b, h in places
            ]
            return lax.ppermute(x, both, pairs) if e else x

        def head_swap(x, j):
            return lax.ppermute(x, "head", [(h, h ^ j) for h in range(groups)]) if j else x

        half, size = rows // 2, rows + rows // 2
        near = heads // 2
        sizes = [size] * near + [rows] * (heads - near) + [half] * (heads - near)
        msgs = pl.pallas_call(
            functools.partial(proj_kernel, inner, heads, near),
            out_shape=[jax.ShapeDtypeStruct((n, LANES), bf) for n in sizes],
            in_specs=[HBM] * 4,
            out_specs=[VMEM] * len(sizes),
            scratch_shapes=[pltpu.VMEM(x.shape, bf) for x in (tokens, w_value, w_key, w_query)]
            + [
                pltpu.VMEM((heads, size, LANES), bf),
                pltpu.SemaphoreType.DMA((4,)),
            ],
            compiler_params=pltpu.CompilerParams(vmem_limit_bytes=WHOLE),
            name="proj",
        )(tokens, w_key, w_value, w_query)
        got, late = [None] * heads, [None] * heads
        for j in reversed(range(heads)):
            got[j] = turn(msgs[j], j)
        parts = heads // near
        longest = -(-nb // SLOTS)
        cap = -(-nq // parts * longest // STREAMS) + longest + 3
        tables = pl.pallas_call(
            functools.partial(list_kernel, inner, heads, per, cap, parts),
            out_shape=[
                jax.ShapeDtypeStruct((parts * STREAMS * cap,), jnp.int32),
                jax.ShapeDtypeStruct((parts * STREAMS * cap,), jnp.int32),
                jax.ShapeDtypeStruct((nq * (nb + SLOTS),), jnp.int32),
                jax.ShapeDtypeStruct((parts * STREAMS * cap,), jnp.int32),
                jax.ShapeDtypeStruct((parts * STREAMS * cap,), jnp.int32),
                jax.ShapeDtypeStruct((parts,), jnp.int32),
            ],
            in_specs=[SMEM] * 2,
            out_specs=[SMEM] * 6,
            scratch_shapes=[
                pltpu.SMEM((nb,), jnp.int32),
                pltpu.SMEM((nq,), jnp.int32),
                pltpu.SMEM((STREAMS,), jnp.int32),
            ],
            name="block_lists",
        )(block_mask, block_order)
        queries = msgs[heads:]
        got[0], tables = lax.optimization_barrier((got[0], tables))
        for j in range(near, heads):
            late[j] = turn(queries[j - near], j)
        kv = []
        for j in range(heads):
            for e in range(inner):
                kv.append(spread(got[j], e))
        o = []
        for part in range(parts):
            if part == 0:
                queries, spans = got[:near], (rows,) * near
                extra = [
                    jax.ShapeDtypeStruct((nb // 2, BLOCK, LANES), bf),
                    jax.ShapeDtypeStruct((nb, TALL, BLOCK), bf),
                ]
            else:
                queries, spans, extra = late[part * near : (part + 1) * near], (0,) * near, []
            mini = near * per + 1
            made = pl.pallas_call(
                functools.partial(attend_kernel, part, per, cap, len(kv), spans),
                out_shape=[jax.ShapeDtypeStruct((half, LANES), bf)] * near + extra,
                in_specs=[SMEM] * 6 + [VMEM] * (len(kv) + near),
                out_specs=[VMEM] * (near + len(extra)),
                scratch_shapes=[
                    pltpu.VMEM((2, mini, LANES, BLOCK), bf),
                    pltpu.VMEM((2, STREAMS, SLOTS, BLOCK, BLOCK), jnp.float32),
                    pltpu.VMEM((2, STREAMS, 1, BLOCK), jnp.float32),
                    pltpu.VMEM((2, STREAMS, 1, BLOCK), jnp.float32),
                    pltpu.VMEM((STREAMS, TALL, BLOCK), jnp.float32),
                    pltpu.VMEM((mini, TALL, BLOCK), jnp.float32),
                ],
                compiler_params=params,
            )(*tables, *kv, *queries)
            o += made[:near]
            if part == 0:
                h = lax.axis_index("head")
                w_out, kv = lax.optimization_barrier((w_out, made[near:]))
                w_cols = []
                for g in range(0, groups, 2):
                    start = (h // 2 ^ g // 2) * 2 * cols
                    share = lax.dynamic_slice_in_dim(w_out, start, 2 * cols, axis=1)
                    w_cols.append(head_swap(share, g))
        mine = [None] * heads
        for j in reversed(range(heads)):
            mine[j] = turn(o[j], j)
        pieces = []
        for g in range(0, groups, 2):
            for j in range(heads):
                pieces.append(head_swap(mine[j], g))

        def out(other, *more):
            return pl.pallas_call(
                functools.partial(out_kernel, inner, heads, groups // 2, other),
                out_shape=jax.ShapeDtypeStruct((rows, cols), bf),
                in_specs=[VMEM] * (len(pieces) + len(w_cols) + len(more)),
                out_specs=VMEM,
                compiler_params=params,
            )(*pieces, *w_cols, *more)

        return out(0, head_swap(out(1), 1))

    placed = (
        P("ctx", None),
        P(None, "head"),
        P(None, "head"),
        P(None, "head"),
        P("head", None),
        P(),
        P(),
    )
    return jax.shard_map(
        body, mesh=mesh, in_specs=placed, out_specs=P("ctx", "head"), check_vma=False
    )
```

```python
import functools

import jax
import jax.numpy as jnp
from jax import lax
from jax.experimental import pallas as pl
from jax.experimental.pallas import tpu as pltpu
from jax.sharding import PartitionSpec as P


HEAD_DIM = 64
BLOCK = 128
LANES = 128
SLOTS = 4
STREAMS = 4
TALL = HEAD_DIM + 16
NEG = -1e30


HBM = pl.BlockSpec(memory_space=pltpu.HBM)
VMEM = pl.BlockSpec(memory_space=pltpu.VMEM)
SMEM = pl.BlockSpec(memory_space=pltpu.SMEM)
GRANT = 16 * 1024 * 1024
WHOLE = 60 * 1024 * 1024


def low_half(shape):
    return lax.broadcasted_iota(jnp.int32, shape, len(shape) - 1) < HEAD_DIM


def swap_halves(x):
    return pltpu.roll(x, HEAD_DIM, 1)


def proj_kernel(inner, heads, near, tok_in, wk_in, wv_in, wq_in, *rest):
    n_out = 2 * heads - near
    outs, (tok, wk, wv, wq, msg, sems) = rest[:n_out], rest[n_out:]
    loads = [
        pltpu.make_async_copy(src, dst, sems.at[n])
        for n, (src, dst) in enumerate(((tok_in, tok), (wv_in, wv), (wk_in, wk), (wq_in, wq)))
    ]
    for load in loads:
        load.start()
    a = lax.axis_index("ctx") // inner
    rows = tok.shape[0]
    half = rows // 2
    low = low_half((half, LANES))
    loads[0].wait()
    loads[1].wait()
    v = jnp.dot(tok[...], wv[...], preferred_element_type=jnp.float32)
    loads[2].wait()
    loads[3].wait()
    q = jnp.dot(tok[...], wq[...], preferred_element_type=jnp.float32) * HEAD_DIM ** (-0.5)
    k = jnp.dot(tok[...], wk[...], preferred_element_type=jnp.float32)
    for base, x in ((half, v), (rows, q)):
        for g in range(heads // 2):
            for i in range(rows // BLOCK):
                block = x[i * BLOCK : (i + 1) * BLOCK, g * LANES : (g + 1) * LANES]
                turned = jnp.transpose(block).astype(jnp.bfloat16)
                start = base + i * HEAD_DIM
                msg[2 * g, start : start + HEAD_DIM] = turned[:HEAD_DIM]
                msg[2 * g + 1, start : start + HEAD_DIM] = turned[HEAD_DIM:]
    for h in range(heads):
        cols = slice(LANES * (h // 2), LANES * (h // 2) + LANES)
        top, bottom = k[:half, cols], k[half:, cols]
        if h % 2 == 0:
            bottom = swap_halves(bottom)
        else:
            top = swap_halves(top)
        msg[h, :half] = jnp.where(low, top, bottom).astype(jnp.bfloat16)
    for j in range(heads):
        if j < near:
            outs[j][...] = msg[a ^ j]
        else:
            outs[j][...] = msg[a ^ j, :rows]
            outs[heads + j - near][...] = msg[a ^ j, rows:]


def list_kernel(inner, outer, per, cap, parts, mask, order, who, where, which, valid, first, steps, names, ends, load):
    c = lax.axis_index("ctx")
    a = c // inner
    b = (c % inner) // 2 * 2 + lax.axis_index("head") % 2
    blocks = inner * outer * per
    half = per // 2
    size = outer * per // parts
    span = blocks + SLOTS

    def name(dev, _):
        kb = ((lax.div(dev, inner) ^ a) * inner + (lax.rem(dev, inner) ^ b)) * per
        for i in range(per):
            names[dev * per + i] = order[kb + i // 2 + i % 2 * half]
        return 0

    lax.fori_loop(0, inner * outer, name, 0)

    def piece(k, _):
        qb = ((k ^ a) * inner + b) * per
        own = [order[qb + i] for i in range(per)]

        def col(n, to):
            to = list(to)
            for e in range(8):
                slot = n * 8 + e
                key = names[slot]
                for i in range(per):
                    which[to[i]] = slot
                    to[i] = to[i] + mask[own[i], key]
            return tuple(to)

        begin = [(k * per + i) * span for i in range(per)]
        end = lax.fori_loop(0, blocks // 8, col, tuple(begin))
        for i in range(per):
            keep = which[begin[i]]
            for extra in range(SLOTS):
                which[end[i] + extra] = keep
            ends[k * per + i] = end[i]
        return 0

    lax.fori_loop(0, outer, piece, 0)
    for part in range(parts):
        for s in range(STREAMS):
            load[s] = 0

        def row(qi, _):
            s, least = jnp.int32(0), load[0]
            for other in range(1, STREAMS):
                here = load[other]
                s = jnp.where(here < least, other, s)
                least = jnp.minimum(here, least)
            item = (part * STREAMS + s) * cap + least
            start = qi * span
            count = ends[qi] - start
            items = lax.div(count + (SLOTS - 1), SLOTS)

            def mark(t, left):
                who[item + t] = qi - part * size
                where[item + t] = start + t * SLOTS
                valid[item + t] = left
                first[item + t] = 0
                return left - SLOTS

            lax.fori_loop(0, items, mark, count)
            first[item] = 1
            load[s] = least + items
            return 0

        lax.fori_loop(part * size, (part + 1) * size, row, 0)
        most = load[0]
        for s in range(1, STREAMS):
            most = jnp.maximum(most, load[s])
        steps[part] = most
        for s in range(STREAMS):
            start = (part * STREAMS + s) * cap
            last = start + jnp.maximum(load[s] - 1, 0)
            idle = load[s] == 0
            qi = jnp.where(idle, size, who[last])
            key = jnp.where(idle, 0, where[last])

            def fill(t, _):
                who[start + t] = qi
                where[start + t] = key
                valid[start + t] = 0
                first[start + t] = 0
                return 0

            lax.fori_loop(load[s], most + 2, fill, 0)


def attend_kernel(part, per, cap, n_kv, spans, who, where, which, valid, first, steps, *rest):
    ins, rest = rest[:n_kv], rest[n_kv:]
    q_in, rest = rest[: len(spans)], rest[len(spans) :]
    outs, rest = rest[: len(spans)], rest[len(spans) :]
    if part == 0:
        (kq, vt), rest = rest[:2], rest[2:]
    else:
        kq, vt = ins
    qt, sc, m_s, al_s, acc_s, acc_all = rest
    half = per // 2
    nq = len(spans) * per
    zero = jnp.zeros((HEAD_DIM, BLOCK), jnp.bfloat16)
    ones = jnp.ones((TALL - HEAD_DIM, BLOCK), jnp.bfloat16)
    for k, start in enumerate(spans):
        for i in range(per):
            turned = q_in[k][start + i * HEAD_DIM : start + (i + 1) * HEAD_DIM, :]
            qt[0, k * per + i] = jnp.concatenate([turned, zero], axis=0)
            qt[1, k * per + i] = jnp.concatenate([zero, turned], axis=0)
    qt[:, nq] = jnp.zeros((2, LANES, BLOCK), jnp.bfloat16)
    if part == 0:
        for n, msg in enumerate(ins):
            for r in range(half):
                kq[n * half + r] = msg[r * BLOCK : (r + 1) * BLOCK, :]
            for i in range(per):
                start = half * BLOCK + (i // 2 + i % 2 * half) * HEAD_DIM
                vt[n * per + i, :HEAD_DIM] = msg[start : start + HEAD_DIM, :]
                vt[n * per + i, HEAD_DIM:] = ones
    m_s[...] = jnp.full(m_s.shape, NEG, jnp.float32)
    acc_s[...] = jnp.zeros(acc_s.shape, jnp.float32)

    def keys(s, t):
        start = where[(part * STREAMS + s) * cap + t]
        return [which[start + e] for e in range(SLOTS)]

    def score(t, buf, s):
        qi = who[(part * STREAMS + s) * cap + t]
        tiles = []
        for e, slot in enumerate(keys(s, t)):
            tile = jnp.dot(kq[slot >> 1], qt[slot & 1, qi], preferred_element_type=jnp.float32)
            sc[buf, s, e] = tile
            tiles.append(tile.reshape(BLOCK // 8, 8, BLOCK))
        top = jnp.max(functools.reduce(jnp.maximum, tiles), axis=0)
        top = jnp.max(top, axis=0, keepdims=True)
        m_old = jnp.where(first[(part * STREAMS + s) * cap + t] == 1, NEG, m_s[1 - buf, s])
        m_new = jnp.maximum(m_old, top)
        al_s[buf, s] = jnp.exp(m_old - m_new)
        m_s[buf, s] = m_new

    def weigh(t, buf, s):
        qi = who[(part * STREAMS + s) * cap + t]
        n_valid = valid[(part * STREAMS + s) * cap + t]
        m, alpha = m_s[buf, s], al_s[buf, s]
        acc = acc_s[s] * alpha
        ids = keys(s, t)
        for e in range(0, SLOTS, 2):
            probs = []
            for f in (e, e + 1):
                shut = m + jnp.where(f < n_valid, 0.0, -NEG)
                probs.append(jnp.exp(sc[buf, s, f] - shut).astype(jnp.bfloat16))
            acc = acc + jnp.dot(
                jnp.concatenate([vt[ids[e]], vt[ids[e + 1]]], axis=1),
                jnp.concatenate(probs, axis=0),
                preferred_element_type=jnp.float32,
            )
        acc_s[s] = acc
        acc_all[qi] = acc

    for s in range(STREAMS):
        score(0, 0, s)
    count = steps[part]

    def step(u, _):
        for buf in (0, 1):
            for s in range(STREAMS):
                score(2 * u + 1 + buf, 1 - buf, s)
                weigh(2 * u + buf, buf, s)
        return 0

    lax.fori_loop(0, lax.div(count, 2), step, 0)

    @pl.when(lax.rem(count, 2) == 1)
    def _():
        for s in range(STREAMS):
            weigh(count - 1, 0, s)

    for k in range(len(spans)):
        for r in range(half):
            done = []
            for i in (k * per + r, k * per + r + half):
                total = acc_all[i]
                done.append(total[:HEAD_DIM] * (1.0 / total[HEAD_DIM : HEAD_DIM + 1]))
            outs[k][r * BLOCK : (r + 1) * BLOCK, :] = jnp.transpose(
                jnp.concatenate(done, axis=0)
            ).astype(jnp.bfloat16)


def out_kernel(inner, heads, groups, other, *refs):
    pieces = [refs[g * heads : (g + 1) * heads] for g in range(groups)]
    ws = refs[groups * heads : groups * heads + groups]
    out = refs[-1]
    a = lax.axis_index("ctx") // inner
    side = (lax.axis_index("head") % 2) ^ other
    cols = pl.ds(pl.multiple_of(side * out.shape[1], LANES), out.shape[1])
    half = pieces[0][0].shape[0]
    low = low_half((half, LANES))
    tops, bottoms, rows = [], [], []
    for g in range(groups):
        for k in range(0, heads, 2):
            p0 = pieces[g][k][...].astype(jnp.float32)
            p1 = pieces[g][k + 1][...].astype(jnp.float32)
            tops.append(jnp.where(low, p0, swap_halves(p1)).astype(jnp.bfloat16))
            bottoms.append(jnp.where(low, swap_halves(p0), p1).astype(jnp.bfloat16))
            for e in (0, 1):
                start = pl.multiple_of(HEAD_DIM * (a ^ (k + e)), HEAD_DIM)
                rows.append(ws[g][pl.ds(start, HEAD_DIM), cols])
    w = jnp.concatenate(rows, axis=0)
    for n, parts in enumerate((tops, bottoms)):
        x = jnp.concatenate(parts, axis=1)
        total = jnp.dot(x, w, preferred_element_type=jnp.float32)
        if not other:
            total = total + refs[-2][n * half : (n + 1) * half, :].astype(jnp.float32)
        out[n * half : (n + 1) * half, :] = total.astype(out.dtype)


def solution(mesh):
    ctx, groups = mesh.shape["ctx"], mesh.shape["head"]

    def body(tokens, w_query, w_key, w_value, w_out, block_mask, block_order):
        rows = tokens.shape[0]
        heads = w_query.shape[1] // HEAD_DIM
        inner = ctx // heads
        per = rows // BLOCK
        nb = block_mask.shape[0]
        nq = heads * per
        cols = w_out.shape[1] // groups
        bf = jnp.bfloat16
        params = pltpu.CompilerParams(vmem_limit_bytes=GRANT)
        both = ("ctx", "head")
        places = [(c // inner, c % inner, h) for c in range(ctx) for h in range(groups)]

        def index(a, b, h):
            return (a * inner + b) * groups + h

        def turn(x, j, g=0):
            pairs = [
                (index(a, b, h), index(a ^ j, (b & ~1) | (h & 1), ((h & ~1) | (b & 1)) ^ g))
                for a, b, h in places
            ]
            return lax.ppermute(x, both, pairs)

        def spread(x, e):
            pairs = [
                (index(a, b, h), index(a, b ^ (e & ~1), h ^ (e & 1))) for a, b, h in places
            ]
            return lax.ppermute(x, both, pairs) if e else x

        def head_swap(x, j):
            return lax.ppermute(x, "head", [(h, h ^ j) for h in range(groups)]) if j else x

        half, size = rows // 2, rows + rows // 2
        near = heads // 2
        sizes = [size] * near + [rows] * (heads - near) + [half] * (heads - near)
        msgs = pl.pallas_call(
            functools.partial(proj_kernel, inner, heads, near),
            out_shape=[jax.ShapeDtypeStruct((n, LANES), bf) for n in sizes],
            in_specs=[HBM] * 4,
            out_specs=[VMEM] * len(sizes),
            scratch_shapes=[pltpu.VMEM(x.shape, bf) for x in (tokens, w_value, w_key, w_query)]
            + [
                pltpu.VMEM((heads, size, LANES), bf),
                pltpu.SemaphoreType.DMA((4,)),
            ],
            compiler_params=pltpu.CompilerParams(vmem_limit_bytes=WHOLE),
            name="proj",
        )(tokens, w_key, w_value, w_query)
        got, late = [None] * heads, [None] * heads
        for j in reversed(range(heads)):
            got[j] = turn(msgs[j], j)
        parts = heads // near
        longest = -(-nb // SLOTS)
        cap = -(-nq // parts * longest // STREAMS) + longest + 3
        tables = pl.pallas_call(
            functools.partial(list_kernel, inner, heads, per, cap, parts),
            out_shape=[
                jax.ShapeDtypeStruct((parts * STREAMS * cap,), jnp.int32),
                jax.ShapeDtypeStruct((parts * STREAMS * cap,), jnp.int32),
                jax.ShapeDtypeStruct((nq * (nb + SLOTS),), jnp.int32),
                jax.ShapeDtypeStruct((parts * STREAMS * cap,), jnp.int32),
                jax.ShapeDtypeStruct((parts * STREAMS * cap,), jnp.int32),
                jax.ShapeDtypeStruct((parts,), jnp.int32),
            ],
            in_specs=[SMEM] * 2,
            out_specs=[SMEM] * 6,
            scratch_shapes=[
                pltpu.SMEM((nb,), jnp.int32),
                pltpu.SMEM((nq,), jnp.int32),
                pltpu.SMEM((STREAMS,), jnp.int32),
            ],
            name="block_lists",
        )(block_mask, block_order)
        queries = msgs[heads:]
        h = lax.axis_index("head")
        w_out, msgs = lax.optimization_barrier((w_out, msgs))
        w_cols = []
        for g in range(0, groups, 2):
            share = lax.dynamic_slice_in_dim(w_out, (h // 2 ^ g // 2) * 2 * cols, 2 * cols, axis=1)
            w_cols.append(head_swap(share, g))
        got[0], tables = lax.optimization_barrier((got[0], tables))
        for j in range(near, heads):
            late[j] = turn(queries[j - near], j)
        kv = []
        for j in range(heads):
            for e in range(inner):
                kv.append(spread(got[j], e))
        o = []
        for part in range(parts):
            if part == 0:
                queries, spans = got[:near], (rows,) * near
                extra = [
                    jax.ShapeDtypeStruct((nb // 2, BLOCK, LANES), bf),
                    jax.ShapeDtypeStruct((nb, TALL, BLOCK), bf),
                ]
            else:
                queries, spans, extra = late[part * near : (part + 1) * near], (0,) * near, []
            mini = near * per + 1
            made = pl.pallas_call(
                functools.partial(attend_kernel, part, per, cap, len(kv), spans),
                out_shape=[jax.ShapeDtypeStruct((half, LANES), bf)] * near + extra,
                in_specs=[SMEM] * 6 + [VMEM] * (len(kv) + near),
                out_specs=[VMEM] * (near + len(extra)),
                scratch_shapes=[
                    pltpu.VMEM((2, mini, LANES, BLOCK), bf),
                    pltpu.VMEM((2, STREAMS, SLOTS, BLOCK, BLOCK), jnp.float32),
                    pltpu.VMEM((2, STREAMS, 1, BLOCK), jnp.float32),
                    pltpu.VMEM((2, STREAMS, 1, BLOCK), jnp.float32),
                    pltpu.VMEM((STREAMS, TALL, BLOCK), jnp.float32),
                    pltpu.VMEM((mini, TALL, BLOCK), jnp.float32),
                ],
                compiler_params=params,
            )(*tables, *kv, *queries)
            o += made[:near]
            if part == 0:
                kv = made[near:]
        mine = [None] * heads
        for j in reversed(range(heads)):
            mine[j] = turn(o[j], j)
        pieces = []
        for g in range(0, groups, 2):
            for j in range(heads):
                pieces.append(head_swap(mine[j], g) if j >= near or not g else turn(o[j], j, g))

        def out(other, *more):
            return pl.pallas_call(
                functools.partial(out_kernel, inner, heads, groups // 2, other),
                out_shape=jax.ShapeDtypeStruct((rows, cols), bf),
                in_specs=[VMEM] * (len(pieces) + len(w_cols) + len(more)),
                out_specs=VMEM,
                compiler_params=params,
            )(*pieces, *w_cols, *more)

        return out(0, head_swap(out(1), 1))

    placed = (
        P("ctx", None),
        P(None, "head"),
        P(None, "head"),
        P(None, "head"),
        P("head", None),
        P(),
        P(),
    )
    return jax.shard_map(
        body, mesh=mesh, in_specs=placed, out_specs=P("ctx", "head"), check_vma=False
    )
```
